32 devices in a mesh: section: 4 (over z), space: 8 (over y, x, core).
Axes of the slice: x: 2, y: 2, z: 4, core: 2. Of those that a mesh axis runs over, the one named last changes fastest.
Arguments:
- features: bfloat16 [1, 32, 128, 320], P(None, 'space'), may hold values from -30 to 30
- section_packs: bfloat16 [4, 11520, 640], P('section', None, 'space'), may hold values from -6 to 6
Outputs:
- output: bfloat16 [1, 32, 128, 320], P(None, 'space', 'section')
The draws below stay inside these ranges and needn't reach their ends.
All inputs are finite; a program needn't handle non-finite values.
Results may differ from the reference program's by a relative error of at most 0.009.
Values may be sent and summed in bfloat16 or wider, within the bound.
No kernel may reach another device: no remote copies, remote signals or barrier semaphores. Data moves between devices by JAX's collectives and lax.ppermute only.
A program may use at most 128 MiB of HBM per device.

```python
import math
import jax
import jax.numpy as jnp
from jax import lax

NARROW = 320
BROAD = 640
GROUPS = 32
COLUMNS = 128
MICRO = 1
HEIGHT = 32
PACK_ROWS = 11520
N_SECTION = 4


def draw_features(key, part):
    base = jax.random.normal(key, (MICRO, HEIGHT, COLUMNS, NARROW), jnp.float32)
    ramp = lax.broadcasted_iota(jnp.float32, (1, HEIGHT, 1, 1), 1) / (HEIGHT - 1)
    offset = 1.5 + 0.5 * jax.random.normal(jax.random.fold_in(key, 7), (1, 1, 1, NARROW), jnp.float32)
    values = (base + offset) * (1.0 + 2.0 * ramp)
    return jnp.clip(values, -30.0, 30.0).astype(jnp.bfloat16)


def shard_levels(own_key, shape, pieces, least, top_value):
    level = 1.0
    for position, shards_of in pieces:
        heights = jax.random.uniform(jax.random.fold_in(jax.random.fold_in(own_key, 6), position), (shards_of,), jnp.float32, least / len(pieces), top_value / len(pieces))
        level = level * jnp.repeat(jnp.exp(heights), shape[position] // shards_of).reshape((-1,) + (1,) * (len(shape) - 1 - position))
    return level


def centred(rng, shape, scale, most, cuts=(), kind=jnp.bfloat16):
    entries = jax.random.normal(rng, shape, jnp.float32) * scale
    if len(cuts) > 0:
        entries = shard_levels(rng, shape, cuts, -0.22, 0.18) * entries
    return jnp.clip(entries, min=-most, max=most).astype(kind)


def setup_inputs(seed: int = 0) -> dict:
    key_list = jax.random.split(jax.random.key(seed), 3)
    return {
        "features": draw_features(jax.random.fold_in(key_list[2], 71), 0),
        "section_packs": centred(key_list[1], (N_SECTION, PACK_ROWS, BROAD), 1.0, 6.0, ((0, 4), (2, 8))),
    }


EPSILON = 1e-05

def convolve(field_in, kernel, fan_in, stride):
    result = lax.conv_general_dilated(field_in.astype(jnp.float32)[None], kernel.astype(jnp.float32), (stride, stride), ((1, 1), (1, 1)), dimension_numbers=('NHWC', 'HWIO', 'NHWC'), precision=lax.Precision.HIGHEST, preferred_element_type=jnp.float32)[0]
    return result * (1.0 / math.sqrt(fan_in))

def activate(field_in):
    values = field_in.astype(jnp.float32)
    n_rows, n_cols, n_chans = values.shape
    grouped = values.reshape(n_rows * n_cols, GROUPS, n_chans // GROUPS)
    group_mean = lax.optimization_barrier(jnp.mean(grouped, axis=(0, 2)))
    centered = grouped - group_mean[None, :, None]
    group_var = lax.optimization_barrier(jnp.mean(jnp.square(centered), axis=(0, 2)))
    normed = centered / jnp.sqrt(group_var + EPSILON)[None, :, None]
    return jax.nn.silu(normed.reshape(n_rows, n_cols, n_chans)).astype(jnp.bfloat16)

def kernel_at(flat_pack, offset, c_in, c_out):
    return flat_pack[offset:offset + 9 * c_in * c_out].reshape(3, 3, c_in, c_out)

def res_pair(field_in, kernel_one, kernel_two):
    c_in = field_in.shape[-1]
    c_out = kernel_two.shape[-1]
    hidden = convolve(activate(field_in), kernel_one, 9 * c_in, 1).astype(jnp.bfloat16)
    return (field_in.astype(jnp.float32) + convolve(activate(hidden), kernel_two, 9 * c_out, 1)).astype(jnp.bfloat16)

def reference(features, section_packs):
    narrow = NARROW
    wide_ch = BROAD
    square = narrow * narrow
    pack_zero = section_packs[0].reshape(-1)
    pack_one = section_packs[1].reshape(-1)
    pack_two = section_packs[2].reshape(-1)
    pack_three = section_packs[3].reshape(-1)

    def one_micro(field_in):
        skip = res_pair(field_in, kernel_at(pack_zero, 0, narrow, narrow), kernel_at(pack_zero, 9 * square, narrow, narrow))
        coarse = convolve(skip, kernel_at(pack_zero, 18 * square, narrow, wide_ch), 9 * narrow, 2).astype(jnp.bfloat16)
        coarse = res_pair(coarse, kernel_at(pack_one, 0, wide_ch, wide_ch), kernel_at(pack_one, 36 * square, wide_ch, wide_ch))
        coarse = res_pair(coarse, kernel_at(pack_two, 0, wide_ch, wide_ch), kernel_at(pack_two, 36 * square, wide_ch, wide_ch))
        upsampled = jnp.repeat(jnp.repeat(coarse, 2, 0), 2, 1)
        upper = convolve(upsampled, kernel_at(pack_three, 0, wide_ch, narrow), 9 * wide_ch, 1).astype(jnp.bfloat16)
        joined = jnp.concatenate([upper, skip], -1)
        hidden = convolve(activate(joined), kernel_at(pack_three, 18 * square, wide_ch, narrow), 9 * wide_ch, 1).astype(jnp.bfloat16)
        projection = jnp.dot(joined.reshape(-1, wide_ch), pack_three[45 * square:47 * square].reshape(wide_ch, narrow), preferred_element_type=jnp.float32)
        projection = projection.reshape(upper.shape) * (1.0 / math.sqrt(wide_ch))
        return (projection + convolve(activate(hidden), kernel_at(pack_three, 36 * square, narrow, narrow), 9 * narrow, 1)).astype(jnp.bfloat16)
    return lax.map(one_micro, features)
```

```python
from functools import partial
import math

import jax
import jax.numpy as jnp
from jax import lax
from jax.experimental import pallas as pl
from jax.experimental.pallas import tpu as pltpu
from jax.sharding import PartitionSpec as P

GROUPS = 32
EPSILON = 1e-05
TAIL = 16
BF16 = jnp.bfloat16
F32 = jnp.float32
VMEM_LIMIT = 60 * 1024 * 1024


def row_stack(rows, count, width):
    ids = lax.broadcasted_iota(jnp.int32, (count, width), 0)
    total = jnp.zeros((count, width), F32)
    for place, row in enumerate(rows):
        total = jnp.where(ids == place, row, total)
    return total


def bf16_terms(row):
    high = row.astype(BF16).astype(F32)
    rest = row - high
    mid = rest.astype(BF16).astype(F32)
    return [high, mid, (rest - mid).astype(BF16).astype(F32)]


def moments_of(value):
    return [
        jnp.sum(value, axis=0, keepdims=True),
        jnp.sum(value * value, axis=0, keepdims=True),
    ]


def group_terms(sums, count):
    width = sums.shape[1]
    size = width // GROUPS
    terms = row_stack(bf16_terms(sums[0:1]) + bf16_terms(sums[1:2]), 16, width).astype(BF16)
    left = lax.broadcasted_iota(jnp.int32, (width, width), 0) // size
    right = lax.broadcasted_iota(jnp.int32, (width, width), 1) // size
    together = jnp.where(left == right, 1.0, 0.0).astype(BF16)
    summed = jnp.dot(terms, together, preferred_element_type=F32) * (1.0 / (count * size))
    mean = summed[0:1] + summed[1:2] + summed[2:3]
    square = summed[3:4] + summed[4:5] + summed[5:6]
    variance = jnp.maximum(square - mean * mean, 0.0)
    return mean, lax.rsqrt(variance + EPSILON)


def silu(z):
    half = 0.5 * z
    return half + half * jnp.tanh(half)


def parity_matrix(width):
    source = lax.broadcasted_iota(jnp.int32, (width, width), 0)
    target = lax.broadcasted_iota(jnp.int32, (width, width), 1)
    half = width // 2
    wanted = jnp.where(target < half, 2 * target, 2 * (target - half) + 1)
    return jnp.where(source == wanted, 1.0, 0.0).astype(BF16)


def shifted(value, step):
    rows = value.shape[0]
    ids = lax.broadcasted_iota(jnp.int32, value.shape, 0)
    if step == 1:
        return jnp.where(ids == 0, 0.0, pltpu.roll(value, 1, 0))
    return jnp.where(ids == rows - 1, 0.0, pltpu.roll(value, rows - 1, 0))


class Shape:
    def __init__(self, features, packs, n):
        self.n = n
        self.rows = features.shape[1]
        self.cols = features.shape[2]
        self.half = self.cols // 2
        self.narrow = features.shape[3]
        self.wide = 2 * self.narrow
        self.m = min(n, 8)
        self.lanes = self.wide // self.m
        self.fine_count = self.rows * n * self.cols
        self.coarse_count = self.fine_count // 4


def emit(flags, out_ref, outer_ref, inner_ref, stats_ref, keep, rows, width, sums):
    channels = out_ref.shape[1]
    core0 = flags[0] == 0
    tail = row_stack(bf16_terms(sums[0]) + bf16_terms(sums[1]), TAIL, channels).astype(BF16)
    out_ref[rows * width :, :] = tail
    stats_ref[...] = row_stack(sums, 8, channels)
    size = keep * width
    first = out_ref[0:size, :].astype(F32)
    last = out_ref[(rows - keep) * width : rows * width, :].astype(F32)
    outer_ref[0:size, :] = jnp.where(core0, first, last).astype(BF16)
    outer_ref[size:, :] = tail
    inner_ref[...] = jnp.where(core0, last, first).astype(BF16)


def ext_row(index, block_ref, outer_ref, inner_ref, flags, rows, halo, width):
    if index < halo:
        span = slice(index * width, (index + 1) * width)
        pick = jnp.where(flags[0] == 0, outer_ref[span, :].astype(F32), inner_ref[span, :].astype(F32))
        return pick, flags[1] != 0
    index -= halo
    if index < rows:
        return block_ref[index * width : (index + 1) * width, :].astype(F32), None
    index -= rows
    span = slice(index * width, (index + 1) * width)
    pick = jnp.where(flags[0] == 0, inner_ref[span, :].astype(F32), outer_ref[span, :].astype(F32))
    return pick, flags[2] != 0


def masked(value, outside):
    if outside is None:
        return value
    return jnp.where(outside, 0.0, value)


class Weights:
    def __init__(self, shape, bounds, start, c_in, c_out, parts):
        self.shape = shape
        self.c_in = c_in
        self.c_out = c_out
        self.split = c_out != shape.wide
        self.per_dy = 3 * c_in * c_out // shape.wide
        self.parts = parts
        self.start = start
        self.bounds = bounds

    def copies(self, piece_refs, buffer, sems):
        made = []
        for dy in range(3):
            begin = self.start + dy * self.per_dy
            end = begin + self.per_dy
            mine = []
            for (low, high), ref in zip(self.bounds, piece_refs, strict=True):
                a, b = max(begin, low), min(end, high)
                if a < b:
                    mine.append(
                        pltpu.make_async_copy(
                            ref.at[:, a - low : b - low, :],
                            buffer.at[dy, :, a - begin : b - begin, :],
                            sems.at[dy, len(mine)],
                        )
                    )
            made.append(mine)
        return made

    def assemble(self, buffer, dy, target):
        n = self.shape.m
        if not self.split:
            target[...] = jnp.concatenate([buffer[dy, k] for k in range(n)], axis=1)
            return
        place = 0
        for dx in range(3):
            offset = dx * self.c_in // 2
            for part in self.parts:
                for odd in range(2):
                    rows = part // 2
                    target[place : place + rows, :] = jnp.concatenate(
                        [
                            buffer[dy, odd * (n // 2) + k, offset : offset + rows, :]
                            for k in range(n // 2)
                        ],
                        axis=1,
                    )
                    place += rows
                offset += part // 2


def fine_columns(store, row, width, even, odd):
    half = even.shape[0]
    store(row, 0, half, 0, shifted(odd, 1))
    store(row, 0, half, 1, even)
    store(row, 0, half, 2, odd)
    store(row, half, half, 0, even)
    store(row, half, half, 1, odd)
    store(row, half, half, 2, shifted(even, -1))


def run_conv(weights, piece_refs, buffer, wbuf, sems, image, acc, copies, rows, width):
    c_in = weights.c_in
    for dy in range(3):
        for copy in copies[dy]:
            copy.wait()
        weights.assemble(buffer, dy, wbuf)
        left = image[dy : dy + rows].reshape(rows * width, 3 * c_in)
        made = jnp.dot(left, wbuf[...], preferred_element_type=F32)
        if dy == 0:
            acc[...] = made
        else:
            acc[...] += made


def scratch_of(weights, image_rows, out_rows, width, extra=()):
    return [
        pltpu.VMEM((3, weights.shape.m, weights.per_dy, weights.shape.lanes), BF16),
        pltpu.VMEM((3 * weights.c_in, weights.c_out), BF16),
        pltpu.VMEM((image_rows, width, 3 * weights.c_in), BF16),
        pltpu.VMEM((out_rows * width, weights.c_out), F32),
        pltpu.SemaphoreType.DMA((3, 4)),
    ] + list(extra)


def call(body, name, n_smem, n_vmem, n_any, outs, scratch, flops):
    specs = (
        [pl.BlockSpec(memory_space=pltpu.SMEM)] * n_smem
        + [pl.BlockSpec(memory_space=pltpu.VMEM)] * n_vmem
        + [pl.BlockSpec(memory_space=pl.ANY)] * n_any
    )
    return pl.pallas_call(
        body,
        out_shape=[jax.ShapeDtypeStruct(s, d) for s, d in outs],
        in_specs=specs,
        out_specs=[pl.BlockSpec(memory_space=pltpu.VMEM)] * len(outs),
        scratch_shapes=scratch,
        compiler_params=pltpu.CompilerParams(vmem_limit_bytes=VMEM_LIMIT),
        cost_estimate=pl.CostEstimate(flops=flops, bytes_accessed=4_000_000, transcendentals=0),
        name=name,
    )


def message_outs(rows, width, channels, keep):
    return [
        ((rows * width + TAIL, channels), BF16),
        ((keep * width + TAIL, channels), BF16),
        ((keep * width, channels), BF16),
        ((8, channels), F32),
    ]


def prepare(shape, flags, x, keep):
    rows, width, c = shape.rows, shape.cols, shape.narrow

    def body(flags, x_ref, out_ref, outer_ref, inner_ref, stats_ref):
        out_ref[0 : rows * width, :] = x_ref[...]
        sums = moments_of(x_ref[...].astype(F32))
        emit(flags, out_ref, outer_ref, inner_ref, stats_ref, keep, rows, width, sums)

    return call(body, "prepare", 1, 1, 0, message_outs(rows, width, c, keep), [], 1000)(flags, x)


def fine_conv(shape, flags, weights, pieces, got, halo, out_halo, keep, residual=None, name="fine"):
    rows, width, half, c = shape.rows, shape.cols, shape.half, shape.narrow
    out_rows = rows + 2 * out_halo
    image_rows = out_rows + 2
    n_pieces = len(pieces)
    extra = 0 if residual is None else 3

    def body(flags, block, outer, inner, sa, sb, *rest):
        res = rest[:extra]
        piece_refs = rest[extra : extra + n_pieces]
        rest = rest[extra + n_pieces :]
        outs = rest[:-5]
        buffer, wbuf, image, acc, sems = rest[-5:]
        copies = weights.copies(piece_refs, buffer, sems)
        for mine in copies:
            for copy in mine:
                copy.start()
        mean, inv = group_terms(sa[...] + sb[...], shape.fine_count)
        mix = parity_matrix(c)

        def store(row, place, size, tap, value):
            image[row, place : place + size, tap * c : (tap + 1) * c] = value.astype(BF16)

        for row in range(image_rows):
            value, outside = ext_row(row + halo - out_halo - 1, block, outer, inner, flags, rows, halo, width)
            value = masked(silu((value - mean) * inv), outside).astype(BF16)
            value = jnp.dot(value, mix, preferred_element_type=F32)
            fine_columns(store, row, width, value[:half], value[half:])
        run_conv(weights, piece_refs, buffer, wbuf, sems, image, acc, copies, out_rows, width)
        scale = 1.0 / math.sqrt(9 * c)
        if residual is None:
            out_ref, outer_ref, inner_ref, stats_ref = outs
            value = (acc[...] * scale).astype(BF16)
            out_ref[0 : rows * width, :] = value
            emit(flags, out_ref, outer_ref, inner_ref, stats_ref, keep, rows, width, moments_of(value.astype(F32)))
        else:
            (out_ref,) = outs
            for row in range(out_rows):
                own, _ = ext_row(row, res[0], res[1], res[2], flags, rows, out_halo, width)
                span = slice(row * width, (row + 1) * width)
                out_ref[span, :] = (own + acc[span, :] * scale).astype(BF16)

    outs = message_outs(rows, width, c, keep) if residual is None else [((out_rows * width, c), BF16)]
    args = (flags,) + tuple(got) + (() if residual is None else tuple(residual)) + tuple(pieces)
    flops = 2 * out_rows * width * 9 * c * c
    return call(body, name, 1, 5 + extra, n_pieces, outs, scratch_of(weights, image_rows, out_rows, width), flops)(*args)


def down_conv(shape, flags, weights, pieces, skip, keep):
    rows, width, half, c = shape.rows, shape.cols, shape.half, shape.narrow
    out_rows = rows // 2

    def body(flags, skip_ref, *rest):
        piece_refs = rest[: len(pieces)]
        outs = rest[len(pieces) : -5]
        buffer, wbuf, image, acc, sems = rest[-5:]
        copies = weights.copies(piece_refs, buffer, sems)
        for mine in copies:
            for copy in mine:
                copy.start()
        for row in range(rows + 1):
            value = skip_ref[row * width : (row + 1) * width, :].astype(F32)
            if row == 0:
                value = masked(value, flags[1] != 0)
            even, odd = value[:half], value[half:]
            place = (row % 2) * (out_rows + 1) + row // 2
            image[place, :, 0:c] = shifted(odd, 1).astype(BF16)
            image[place, :, c : 2 * c] = even.astype(BF16)
            image[place, :, 2 * c :] = odd.astype(BF16)
        for dy in range(3):
            for copy in copies[dy]:
                copy.wait()
            weights.assemble(buffer, dy, wbuf)
            begin = (0, out_rows + 1, 1)[dy]
            left = image[begin : begin + out_rows].reshape(out_rows * half, 3 * c)
            made = jnp.dot(left, wbuf[...], preferred_element_type=F32)
            if dy == 0:
                acc[...] = made
            else:
                acc[...] += made
        out_ref, outer_ref, inner_ref, stats_ref = outs
        value = (acc[...] * (1.0 / math.sqrt(9 * c))).astype(BF16)
        out_ref[0 : out_rows * half, :] = value
        emit(flags, out_ref, outer_ref, inner_ref, stats_ref, keep, out_rows, half, moments_of(value.astype(F32)))

    scratch = scratch_of(weights, 2 * (out_rows + 1), out_rows, half)
    outs = message_outs(out_rows, half, shape.wide, keep)
    return call(body, "down", 1, 1, len(pieces), outs, scratch, 2 * out_rows * half * 9 * c * shape.wide)(flags, skip, *pieces)


def coarse_conv(shape, flags, weights, pieces, got, keep, residual=None, name="coarse"):
    rows, width, c = shape.rows // 2, shape.half, shape.wide
    extra = 0 if residual is None else 1

    def body(flags, block, outer, inner, sa, sb, *rest):
        res = rest[:extra]
        piece_refs = rest[extra : extra + len(pieces)]
        outs = rest[extra + len(pieces) : -5]
        buffer, wbuf, image, acc, sems = rest[-5:]
        copies = weights.copies(piece_refs, buffer, sems)
        for mine in copies:
            for copy in mine:
                copy.start()
        mean, inv = group_terms(sa[...] + sb[...], shape.coarse_count)
        for row in range(rows + 2):
            value, outside = ext_row(row, block, outer, inner, flags, rows, 1, width)
            value = masked(silu((value - mean) * inv), outside)
            image[row, :, 0:c] = shifted(value, 1).astype(BF16)
            image[row, :, c : 2 * c] = value.astype(BF16)
            image[row, :, 2 * c :] = shifted(value, -1).astype(BF16)
        run_conv(weights, piece_refs, buffer, wbuf, sems, image, acc, copies, rows, width)
        out_ref, outer_ref, inner_ref, stats_ref = outs
        value = acc[...] * (1.0 / math.sqrt(9 * c))
        if residual is not None:
            value = res[0][0 : rows * width, :].astype(F32) + value
        value = value.astype(BF16)
        out_ref[0 : rows * width, :] = value
        emit(flags, out_ref, outer_ref, inner_ref, stats_ref, keep, rows, width, moments_of(value.astype(F32)))

    args = (flags,) + tuple(got) + (() if residual is None else (residual,)) + tuple(pieces)
    outs = message_outs(rows, width, c, keep)
    flops = 2 * rows * width * 9 * c * c
    return call(body, name, 1, 5 + extra, len(pieces), outs, scratch_of(weights, rows + 2, rows, width), flops)(*args)


def up_conv(shape, flags, weights, pieces, got, skip, keep):
    rows, width, half = shape.rows, shape.cols, shape.half
    c, c_out = shape.wide, shape.narrow

    def body(flags, block, outer, inner, skip_ref, *rest):
        piece_refs = rest[: len(pieces)]
        outs = rest[len(pieces) : -5]
        buffer, wbuf, image, acc, sems = rest[-5:]
        copies = weights.copies(piece_refs, buffer, sems)
        for mine in copies:
            for copy in mine:
                copy.start()
        mix = parity_matrix(c)
        for row in range(rows // 2 + 2):
            value, outside = ext_row(row, block, outer, inner, flags, rows // 2, 1, half)
            value = masked(value, outside).astype(BF16)
            value = jnp.dot(value, mix, preferred_element_type=F32)
            before, after = shifted(value, 1).astype(BF16), shifted(value, -1).astype(BF16)
            value = value.astype(BF16)
            for fine in (2 * row - 1, 2 * row):
                if 0 <= fine < rows + 2:
                    image[fine, 0:half, 0:c] = before
                    image[fine, 0:half, c : 2 * c] = value
                    image[fine, 0:half, 2 * c :] = value
                    image[fine, half:, 0:c] = value
                    image[fine, half:, c : 2 * c] = value
                    image[fine, half:, 2 * c :] = after
        run_conv(weights, piece_refs, buffer, wbuf, sems, image, acc, copies, rows, width)
        out_ref, outer_ref, inner_ref, stats_ref, skip_stats_ref = outs
        value = (acc[...] * (1.0 / math.sqrt(9 * c))).astype(BF16)
        out_ref[0 : rows * width, :] = value
        emit(flags, out_ref, outer_ref, inner_ref, stats_ref, keep, rows, width, moments_of(value.astype(F32)))
        own = skip_ref[width : (rows + 1) * width, :].astype(F32)
        skip_stats_ref[...] = row_stack(moments_of(own), 8, c_out)

    outs = message_outs(rows, width, c_out, keep) + [((8, c_out), F32)]
    flops = 2 * rows * width * 9 * c * c_out
    scratch = scratch_of(weights, rows + 2, rows, width)
    return call(body, "up", 1, 4, len(pieces), outs, scratch, flops)(flags, *got, skip, *pieces)


def join_conv(shape, flags, weights, pieces, got, skip, skip_sums, keep):
    rows, width, half, c = shape.rows, shape.cols, shape.half, shape.narrow

    def body(flags, block, outer, inner, sa, sb, skip_ref, skip_sum, *rest):
        piece_refs = rest[: len(pieces)]
        outs = rest[len(pieces) : -5]
        buffer, wbuf, image, acc, sems = rest[-5:]
        copies = weights.copies(piece_refs, buffer, sems)
        for mine in copies:
            for copy in mine:
                copy.start()
        mix = parity_matrix(c)
        for part in range(2):
            sums = sa[...] + sb[...] if part == 0 else skip_sum[...]
            mean, inv = pair_terms(sums, shape.fine_count)

            def store(row, place, size, tap, value, part=part):
                begin = (2 * tap + part) * c
                image[row, place : place + size, begin : begin + c] = value.astype(BF16)

            for row in range(rows + 2):
                if part == 0:
                    value, outside = ext_row(row, block, outer, inner, flags, rows, 1, width)
                else:
                    value = skip_ref[row * width : (row + 1) * width, :].astype(F32)
                    outside = flags[1] != 0 if row == 0 else flags[2] != 0 if row == rows + 1 else None
                value = masked(silu((value - mean) * inv), outside).astype(BF16)
                value = jnp.dot(value, mix, preferred_element_type=F32)
                fine_columns(store, row, width, value[:half], value[half:])
        run_conv(weights, piece_refs, buffer, wbuf, sems, image, acc, copies, rows, width)
        out_ref, outer_ref, inner_ref, stats_ref = outs
        value = (acc[...] * (1.0 / math.sqrt(18 * c))).astype(BF16)
        out_ref[0 : rows * width, :] = value
        emit(flags, out_ref, outer_ref, inner_ref, stats_ref, keep, rows, width, moments_of(value.astype(F32)))

    outs = message_outs(rows, width, c, keep)
    flops = 2 * rows * width * 18 * c * c
    scratch = scratch_of(weights, rows + 2, rows, width)
    return call(body, "join", 1, 7, len(pieces), outs, scratch, flops)(flags, *got, skip, skip_sums, *pieces)


def pair_terms(sums, count):
    width = sums.shape[1]
    size = 2 * width // GROUPS
    terms = row_stack(bf16_terms(sums[0:1]) + bf16_terms(sums[1:2]), 16, width).astype(BF16)
    left = lax.broadcasted_iota(jnp.int32, (width, width), 0) // size
    right = lax.broadcasted_iota(jnp.int32, (width, width), 1) // size
    together = jnp.where(left == right, 1.0, 0.0).astype(BF16)
    summed = jnp.dot(terms, together, preferred_element_type=F32) * (1.0 / (count * size))
    mean = summed[0:1] + summed[1:2] + summed[2:3]
    square = summed[3:4] + summed[4:5] + summed[5:6]
    variance = jnp.maximum(square - mean * mean, 0.0)
    return mean, lax.rsqrt(variance + EPSILON)


def last_conv(shape, flags, weights, pieces, got, u, skip, j_start, n_quarters):
    rows, width, half, c = shape.rows, shape.cols, shape.half, shape.narrow
    j_rows = c
    quarter = half // n_quarters
    n = shape.m
    where = [i for i, (low, high) in enumerate(weights.bounds) if low <= j_start and j_start + j_rows <= high][0]
    j_low = j_start - weights.bounds[where][0]

    def body(flags, block, outer, inner, sa, sb, u_ref, skip_ref, *rest):
        piece_refs = rest[: len(pieces)]
        outs = rest[len(pieces) : -8]
        buffer, wbuf, image, acc, sems, jbuf, jsem, jmat = rest[-8:]
        copies = weights.copies(piece_refs, buffer, sems)
        for mine in copies:
            for copy in mine:
                copy.start()
        jcopy = pltpu.make_async_copy(piece_refs[where].at[:, j_low : j_low + j_rows, :], jbuf, jsem)
        jcopy.start()
        mean, inv = group_terms(sa[...] + sb[...], shape.fine_count)
        mix = parity_matrix(c)

        def store(row, place, size, tap, value):
            image[row, place : place + size, tap * c : (tap + 1) * c] = value.astype(BF16)

        for row in range(rows + 2):
            value, outside = ext_row(row, block, outer, inner, flags, rows, 1, width)
            value = masked(silu((value - mean) * inv), outside).astype(BF16)
            value = jnp.dot(value, mix, preferred_element_type=F32)
            fine_columns(store, row, width, value[:half], value[half:])
        run_conv(weights, piece_refs, buffer, wbuf, sems, image, acc, copies, rows, width)
        jcopy.wait()
        for part in range(2):
            for odd in range(2):
                place = part * c + odd * (c // 2)
                jmat[place : place + c // 2, :] = jnp.concatenate(
                    [jbuf[odd * (n // 2) + k, part * c // 2 : (part + 1) * c // 2, :] for k in range(n // 2)], axis=1
                )
        mine = jnp.dot(u_ref[0 : rows * width, :], mix, preferred_element_type=F32).astype(BF16)
        made = jnp.dot(mine, jmat[0:c, :], preferred_element_type=F32)
        mine = jnp.dot(skip_ref[width : (rows + 1) * width, :], mix, preferred_element_type=F32).astype(BF16)
        made += jnp.dot(mine, jmat[c:, :], preferred_element_type=F32)
        value = made * (1.0 / math.sqrt(2 * c)) + acc[...] * (1.0 / math.sqrt(9 * c))
        value = value.reshape(2 * rows, half, c).astype(BF16)
        for q, out in enumerate(outs):
            out[...] = value[:, q * quarter : (q + 1) * quarter, :]

    outs = [((2 * rows, quarter, c), BF16)] * n_quarters
    flops = 2 * rows * width * 11 * c * c
    extra = [pltpu.VMEM((n, j_rows, shape.lanes), BF16), pltpu.SemaphoreType.DMA(()), pltpu.VMEM((2 * c, c), BF16)]
    scratch = scratch_of(weights, rows + 2, rows, width, extra)
    return call(body, "last", 1, 7, len(pieces), outs, scratch, flops)(flags, *got, u, skip, *pieces)


def shards(n, n_section, features, section_packs):
    section_id = lax.axis_index("section")
    w = lax.axis_index("space")
    shape = Shape(features, section_packs, n)
    q_rows = shape.narrow * shape.narrow // shape.wide
    pack = section_packs[0]
    flags = jnp.stack([w % 2, (w == 0).astype(jnp.int32), (w == n - 1).astype(jnp.int32), section_id]).astype(jnp.int32)

    cuts = [0, 9 * q_rows, 18 * q_rows, 36 * q_rows, pack.shape[0]]
    bounds = list(zip(cuts[:-1], cuts[1:], strict=True))
    pieces = [lax.all_gather(pack[a:b], "space") for a, b in bounds]
    if shape.m != n:
        pieces = [
            p.reshape(shape.m, n // shape.m, p.shape[1], p.shape[2]).swapaxes(1, 2).reshape(shape.m, p.shape[1], -1)
            for p in pieces
        ]

    def weights(start, c_in, c_out, parts):
        end = start + 9 * c_in * c_out // shape.wide
        used = [i for i, (a, b) in enumerate(bounds) if a < end and b > start]
        made = Weights(shape, [bounds[i] for i in used], start, c_in, c_out, parts)
        return made, [pieces[i] for i in used]

    def permute(value, source, target, move):
        pairs = [(source * n + i, target * n + move(i)) for i in range(n)]
        return lax.ppermute(value, ("section", "space"), pairs)

    def to_outer(i):
        return (i + 1) % n if i % 2 else (i - 1) % n

    def ahead(i):
        return (i - 2) % n if i % 2 else (i + 2) % n

    def across(i):
        return (i + 4) % n

    def partner(i):
        return i ^ 1

    def sums_of(tail):
        tail = tail.astype(F32)
        first = tail[0:1] + tail[1:2] + tail[2:3]
        second = tail[3:4] + tail[4:5] + tail[5:6]
        return jnp.concatenate([first, second, jnp.zeros((6, tail.shape[1]), F32)], 0)

    def exchange(made, source, target, extra_stats=None, with_stats=True):
        block, outer, inner, stats = made
        if source != target:
            block = permute(block, source, target, lambda i: i)
            stats = None
        outer = permute(outer, source, target, to_outer)
        inner = permute(inner, source, target, partner)
        if not with_stats:
            return block, outer, inner
        own = made[3] if stats is not None else sums_of(block[-TAIL:])
        size = own.shape[1]
        sent = made[3] if extra_stats is None else jnp.concatenate([made[3], extra_stats], 1)
        if n == 8:
            b = permute(sent, source, target, ahead)
            c = permute(sent, source, target, across)
            if extra_stats is None:
                near = sums_of(outer[-TAIL:])
            else:
                own = sent
                near = permute(sent, source, target, to_outer)
            mine = own + near + b + c
            other = permute(mine, target, target, partner)
        else:
            mine = lax.psum(sent if stats is not None else own, "space")
            other = jnp.zeros_like(mine)
        if extra_stats is None:
            return block, outer, inner, mine, other
        total = mine[:, size:] + other[:, size:]
        return (block, outer, inner, mine[:, :size], other[:, :size]), total

    narrow, wide = shape.narrow, shape.wide
    x = features[0].reshape(shape.rows, shape.half, 2, narrow).transpose(0, 2, 1, 3).reshape(-1, narrow)
    first = exchange(prepare(shape, flags, x, 1), 0, 0)
    hidden = fine_conv(shape, flags, *weights(0, narrow, narrow, (narrow,)), first, 1, 0, 2, name="c00")
    second = exchange(hidden, 0, 0)
    (skip,) = fine_conv(
        shape, flags, *weights(9 * q_rows, narrow, narrow, (narrow,)), second, 2, 1, 0, residual=first[:3], name="c01"
    )
    coarse = down_conv(shape, flags, *weights(18 * q_rows, narrow, wide, (narrow,)), skip, 1)
    for section in (1, 2):
        got = exchange(coarse, section - 1, section)
        if section == 1:
            skip, got = lax.optimization_barrier((skip, got))
            skip = permute(skip, 0, 3, lambda i: i)
        hidden = coarse_conv(shape, flags, *weights(0, wide, wide, (wide,)), got, 1, name=f"c{section}0")
        then = exchange(hidden, section, section)
        coarse = coarse_conv(
            shape, flags, *weights(36 * q_rows, wide, wide, (wide,)), then, 1, residual=got[0], name=f"c{section}1"
        )
    got = exchange(coarse, 2, 3, with_stats=False)
    *up, skip_stats = up_conv(shape, flags, *weights(0, wide, narrow, (wide,)), got, skip, 1)
    got, skip_sums = exchange(up, 3, 3, extra_stats=skip_stats)
    hidden = join_conv(shape, flags, *weights(18 * q_rows, wide, narrow, (narrow, narrow)), got, skip, skip_sums, 1)
    then = exchange(hidden, 3, 3)
    outs = last_conv(
        shape, flags, *weights(36 * q_rows, narrow, narrow, (narrow,)), then, got[0], skip, 45 * q_rows, n_section
    )
    result = jnp.where(section_id == 3, outs[3], jnp.zeros_like(outs[3]))
    for target in range(3):
        result = result + permute(outs[target], 3, target, lambda i: i)
    quarter = shape.half // n_section
    result = result.reshape(shape.rows, 2, quarter, narrow).transpose(0, 2, 1, 3)
    return result.reshape(1, shape.rows, 2 * quarter, narrow)


def solution(mesh):
    n, n_section = mesh.shape["space"], mesh.shape["section"]

    def body(features, section_packs):
        return shards(n, n_section, features, section_packs)

    return jax.shard_map(
        body,
        mesh=mesh,
        in_specs=(P(None, "space", None, None), P("section", None, "space")),
        out_specs=P(None, "space", "section", None),
        check_vma=False,
    )
```

```python
from functools import partial
import math

import jax
import jax.numpy as jnp
from jax import lax
from jax.experimental import pallas as pl
from jax.experimental.pallas import tpu as pltpu
from jax.sharding import PartitionSpec as P

GROUPS = 32
EPSILON = 1e-05
TAIL = 16
BF16 = jnp.bfloat16
F32 = jnp.float32


def row_stack(rows, count, width):
    ids = lax.broadcasted_iota(jnp.int32, (count, width), 0)
    total = jnp.zeros((count, width), F32)
    for place, row in enumerate(rows):
        total = jnp.where(ids == place, row, total)
    return total


def bf16_terms(row):
    high = row.astype(BF16).astype(F32)
    rest = row - high
    mid = rest.astype(BF16).astype(F32)
    return [high, mid, (rest - mid).astype(BF16).astype(F32)]


def moments_of(value):
    return [
        jnp.sum(value, axis=0, keepdims=True),
        jnp.sum(value * value, axis=0, keepdims=True),
    ]


def group_terms(sums, count):
    width = sums.shape[1]
    size = width // GROUPS
    terms = row_stack(bf16_terms(sums[0:1]) + bf16_terms(sums[1:2]), 16, width).astype(BF16)
    left = lax.broadcasted_iota(jnp.int32, (width, width), 0) // size
    right = lax.broadcasted_iota(jnp.int32, (width, width), 1) // size
    together = jnp.where(left == right, 1.0, 0.0).astype(BF16)
    summed = jnp.dot(terms, together, preferred_element_type=F32) * (1.0 / (count * size))
    mean = summed[0:1] + summed[1:2] + summed[2:3]
    square = summed[3:4] + summed[4:5] + summed[5:6]
    variance = jnp.maximum(square - mean * mean, 0.0)
    return mean, lax.rsqrt(variance + EPSILON)


def silu(z):
    half = 0.5 * z
    return half + half * jnp.tanh(half)


def parity_matrix(width):
    source = lax.broadcasted_iota(jnp.int32, (width, width), 0)
    target = lax.broadcasted_iota(jnp.int32, (width, width), 1)
    half = width // 2
    wanted = jnp.where(target < half, 2 * target, 2 * (target - half) + 1)
    return jnp.where(source == wanted, 1.0, 0.0).astype(BF16)


def shifted(value, step):
    rows = value.shape[0]
    ids = lax.broadcasted_iota(jnp.int32, value.shape, 0)
    if step == 1:
        return jnp.where(ids == 0, 0.0, pltpu.roll(value, 1, 0))
    return jnp.where(ids == rows - 1, 0.0, pltpu.roll(value, rows - 1, 0))


class Shape:
    def __init__(self, features, packs, n):
        self.n = n
        self.rows = features.shape[1]
        self.cols = features.shape[2]
        self.half = self.cols // 2
        self.narrow = features.shape[3]
        self.wide = 2 * self.narrow
        self.m = min(n, 8)
        self.cols_of = self.wide // self.m
        self.blk = 3 * self.narrow // 2
        self.lanes = -(-self.blk // 128) * 128
        self.fine_count = self.rows * n * self.cols
        self.coarse_count = self.fine_count // 4


def emit(flags, out_ref, outer_ref, inner_ref, stats_ref, keep, rows, width, sums):
    channels = out_ref.shape[1]
    core0 = flags[0] == 0
    tail = row_stack(bf16_terms(sums[0]) + bf16_terms(sums[1]), TAIL, channels).astype(BF16)
    out_ref[rows * width :, :] = tail
    stats_ref[...] = row_stack(sums, 8, channels)
    size = keep * width
    first = out_ref[0:size, :].astype(F32)
    last = out_ref[(rows - keep) * width : rows * width, :].astype(F32)
    outer_ref[0:size, :] = jnp.where(core0, first, last).astype(BF16)
    outer_ref[size:, :] = tail
    inner_ref[...] = jnp.where(core0, last, first).astype(BF16)


def ext_row(index, block_ref, outer_ref, inner_ref, flags, rows, halo, width):
    if index < halo:
        span = slice(index * width, (index + 1) * width)
        pick = jnp.where(flags[0] == 0, outer_ref[span, :].astype(F32), inner_ref[span, :].astype(F32))
        return pick, flags[1] != 0
    index -= halo
    if index < rows:
        return block_ref[index * width : (index + 1) * width, :].astype(F32), None
    index -= rows
    span = slice(index * width, (index + 1) * width)
    pick = jnp.where(flags[0] == 0, inner_ref[span, :].astype(F32), outer_ref[span, :].astype(F32))
    return pick, flags[2] != 0


def masked(value, outside):
    if outside is None:
        return value
    return jnp.where(outside, 0.0, value)


class Weights:
    def __init__(self, shape, bounds, start, c_in, c_out):
        self.shape = shape
        self.c_in = c_in
        self.c_out = c_out
        self.split = c_out != shape.wide
        self.blocks = 3 * c_in * c_out // shape.wide // shape.blk
        self.start = start // shape.blk
        self.bounds = bounds
        self.depth = self.blocks * shape.lanes
        self.width = (2 if self.split else 1) * self.depth

    def stacks(self, refs):
        refs = list(refs)
        return {low: [refs.pop(0) for _ in owners] for low, _, owners in self.bounds}

    def copies(self, flags, stack_refs, buffer, sems):
        made = []
        for dy in range(3):
            mine = []
            for block in range(self.blocks):
                at = self.start + dy * self.blocks + block
                for low, high, owners in self.bounds:
                    if low <= at < high:
                        for ref, owner in zip(stack_refs[low], owners, strict=True):
                            for j in range(ref.shape[0]):
                                mine.append(
                                    pltpu.make_async_copy(
                                        ref.at[j, at - low],
                                        buffer.at[dy, block, owner(flags, j)],
                                        sems.at[dy, len(mine)],
                                    )
                                )
            made.append(mine)
        return made

    def product(self, left, buffer, dy):
        shape = self.shape
        rows = shape.m * shape.cols_of
        total = None
        for block in range(self.blocks):
            right = buffer[dy, block].reshape(rows, shape.lanes)
            for odd in range(2 if self.split else 1):
                part = right[odd * self.c_out : (odd + 1) * self.c_out] if self.split else right
                begin = (odd * self.blocks + block) * shape.lanes
                made = lax.dot_general(
                    left[:, begin : begin + shape.lanes], part, (((1,), (1,)), ((), ())), preferred_element_type=F32
                )
                total = made if total is None else total + made
        return total

    def put(self, image, row, place, tap, value, first=0, channels=None):
        shape = self.shape
        size = value.shape[0]
        half = self.c_in // 2
        runs = []
        if self.split:
            c = value.shape[1] // 2
            runs = [(odd, tap * half + first // 2, odd * c, c) for odd in range(2)]
        else:
            runs = [(0, tap * self.c_in + first, 0, value.shape[1])]
        for odd, index, at, left in runs:
            while left > 0:
                step = min(left, shape.blk - index % shape.blk)
                lane = odd * self.depth + index // shape.blk * shape.lanes + index % shape.blk
                image[row, place : place + size, lane : lane + step] = value[:, at : at + step]
                index, at, left = index + step, at + step, left - step

    def clear(self, image):
        shape = self.shape
        for block in range(self.width // shape.lanes):
            begin = block * shape.lanes + shape.blk
            end = (block + 1) * shape.lanes
            image[:, :, begin:end] = jnp.zeros((image.shape[0], image.shape[1], end - begin), BF16)


def fine_columns(store, row, width, even, odd):
    half = even.shape[0]
    store(row, 0, half, 0, shifted(odd, 1))
    store(row, 0, half, 1, even)
    store(row, 0, half, 2, odd)
    store(row, half, half, 0, even)
    store(row, half, half, 1, odd)
    store(row, half, half, 2, shifted(even, -1))


def run_conv(weights, buffer, image, acc, copies, rows, width):
    for dy in range(3):
        for copy in copies[dy]:
            copy.wait()
        left = image[dy : dy + rows].reshape(rows * width, weights.width)
        made = weights.product(left, buffer, dy)
        if dy == 0:
            acc[...] = made
        else:
            acc[...] += made


def scratch_of(weights, image_rows, out_rows, width, extra=()):
    return [
        pltpu.VMEM((3, weights.blocks, weights.shape.m, weights.shape.cols_of, weights.shape.lanes), BF16),
        pltpu.VMEM((image_rows, width, weights.width), BF16),
        pltpu.VMEM((out_rows * width, weights.c_out), F32),
        pltpu.SemaphoreType.DMA((3, 8 * weights.blocks)),
    ] + list(extra)


def call(body, name, n_smem, n_vmem, n_any, outs, scratch, flops, limit=24 * 1024 * 1024):
    specs = (
        [pl.BlockSpec(memory_space=pltpu.SMEM)] * n_smem
        + [pl.BlockSpec(memory_space=pltpu.VMEM)] * n_vmem
        + [pl.BlockSpec(memory_space=pl.ANY)] * n_any
    )
    return pl.pallas_call(
        body,
        out_shape=[jax.ShapeDtypeStruct(s, d) for s, d in outs],
        in_specs=specs,
        out_specs=[pl.BlockSpec(memory_space=pltpu.VMEM)] * len(outs),
        scratch_shapes=scratch,
        compiler_params=pltpu.CompilerParams(vmem_limit_bytes=limit),
        cost_estimate=pl.CostEstimate(flops=flops, bytes_accessed=4_000_000, transcendentals=0),
        name=name,
    )


def message_outs(rows, width, channels, keep):
    return [
        ((rows * width + TAIL, channels), BF16),
        ((keep * width + TAIL, channels), BF16),
        ((keep * width, channels), BF16),
        ((8, channels), F32),
    ]


def prepare(shape, flags, x, keep):
    rows, width, c = shape.rows, shape.cols, shape.narrow

    def body(flags, x_ref, out_ref, outer_ref, inner_ref, stats_ref):
        out_ref[0 : rows * width, :] = x_ref[...]
        sums = moments_of(x_ref[...].astype(F32))
        emit(flags, out_ref, outer_ref, inner_ref, stats_ref, keep, rows, width, sums)

    return call(body, "prepare", 1, 1, 0, message_outs(rows, width, c, keep), [], 1000)(flags, x)


def fine_conv(shape, flags, weights, pieces, got, halo, out_halo, keep, residual=None, name="fine"):
    rows, width, half, c = shape.rows, shape.cols, shape.half, shape.narrow
    out_rows = rows + 2 * out_halo
    image_rows = out_rows + 2
    n_pieces = len(pieces)
    extra = 0 if residual is None else 3

    def body(flags, block, outer, inner, sa, sb, *rest):
        res = rest[:extra]
        piece_refs = rest[extra : extra + n_pieces]
        rest = rest[extra + n_pieces :]
        outs = rest[:-4]
        buffer, image, acc, sems = rest[-4:]
        copies = weights.copies(flags, weights.stacks(piece_refs), buffer, sems)
        for mine in copies:
            for copy in mine:
                copy.start()
        weights.clear(image)
        mean, inv = group_terms(sa[...] + sb[...], shape.fine_count)
        mix = parity_matrix(c)

        def store(row, place, size, tap, value):
            weights.put(image, row, place, tap, value.astype(BF16))

        for row in range(image_rows):
            value, outside = ext_row(row + halo - out_halo - 1, block, outer, inner, flags, rows, halo, width)
            value = masked(silu((value - mean) * inv), outside).astype(BF16)
            value = jnp.dot(value, mix, preferred_element_type=F32)
            fine_columns(store, row, width, value[:half], value[half:])
        run_conv(weights, buffer, image, acc, copies, out_rows, width)
        scale = 1.0 / math.sqrt(9 * c)
        if residual is None:
            out_ref, outer_ref, inner_ref, stats_ref = outs
            value = (acc[...] * scale).astype(BF16)
            out_ref[0 : rows * width, :] = value
            emit(flags, out_ref, outer_ref, inner_ref, stats_ref, keep, rows, width, moments_of(value.astype(F32)))
        else:
            (out_ref,) = outs
            for row in range(out_rows):
                own, _ = ext_row(row, res[0], res[1], res[2], flags, rows, out_halo, width)
                span = slice(row * width, (row + 1) * width)
                out_ref[span, :] = (own + acc[span, :] * scale).astype(BF16)

    outs = message_outs(rows, width, c, keep) if residual is None else [((out_rows * width, c), BF16)]
    args = (flags,) + tuple(got) + (() if residual is None else tuple(residual)) + tuple(pieces)
    flops = 2 * out_rows * width * 9 * c * c
    return call(body, name, 1, 5 + extra, n_pieces, outs, scratch_of(weights, image_rows, out_rows, width), flops)(*args)


def down_conv(shape, flags, weights, pieces, skip, keep):
    rows, width, half, c = shape.rows, shape.cols, shape.half, shape.narrow
    out_rows = rows // 2

    def body(flags, skip_ref, *rest):
        piece_refs = rest[: len(pieces)]
        outs = rest[len(pieces) : -4]
        buffer, image, acc, sems = rest[-4:]
        copies = weights.copies(flags, weights.stacks(piece_refs), buffer, sems)
        for mine in copies:
            for copy in mine:
                copy.start()
        weights.clear(image)
        for row in range(rows + 1):
            value = skip_ref[row * width : (row + 1) * width, :].astype(F32)
            if row == 0:
                value = masked(value, flags[1] != 0)
            even, odd = value[:half], value[half:]
            place = (row % 2) * (out_rows + 1) + row // 2
            weights.put(image, place, 0, 0, shifted(odd, 1).astype(BF16))
            weights.put(image, place, 0, 1, even.astype(BF16))
            weights.put(image, place, 0, 2, odd.astype(BF16))
        for dy in range(3):
            for copy in copies[dy]:
                copy.wait()
            begin = (0, out_rows + 1, 1)[dy]
            left = image[begin : begin + out_rows].reshape(out_rows * half, weights.width)
            made = weights.product(left, buffer, dy)
            if dy == 0:
                acc[...] = made
            else:
                acc[...] += made
        out_ref, outer_ref, inner_ref, stats_ref = outs
        value = (acc[...] * (1.0 / math.sqrt(9 * c))).astype(BF16)
        out_ref[0 : out_rows * half, :] = value
        emit(flags, out_ref, outer_ref, inner_ref, stats_ref, keep, out_rows, half, moments_of(value.astype(F32)))

    scratch = scratch_of(weights, 2 * (out_rows + 1), out_rows, half)
    outs = message_outs(out_rows, half, shape.wide, keep)
    return call(body, "down", 1, 1, len(pieces), outs, scratch, 2 * out_rows * half * 9 * c * shape.wide)(flags, skip, *pieces)


def coarse_conv(shape, flags, weights, pieces, got, keep, residual=None, name="coarse"):
    rows, width, c = shape.rows // 2, shape.half, shape.wide
    extra = 0 if residual is None else 1

    def body(flags, block, outer, inner, sa, sb, *rest):
        res = rest[:extra]
        piece_refs = rest[extra : extra + len(pieces)]
        outs = rest[extra + len(pieces) : -4]
        buffer, image, acc, sems = rest[-4:]
        copies = weights.copies(flags, weights.stacks(piece_refs), buffer, sems)
        for mine in copies:
            for copy in mine:
                copy.start()
        weights.clear(image)
        mean, inv = group_terms(sa[...] + sb[...], shape.coarse_count)
        for row in range(rows + 2):
            value, outside = ext_row(row, block, outer, inner, flags, rows, 1, width)
            value = masked(silu((value - mean) * inv), outside)
            weights.put(image, row, 0, 0, shifted(value, 1).astype(BF16))
            weights.put(image, row, 0, 1, value.astype(BF16))
            weights.put(image, row, 0, 2, shifted(value, -1).astype(BF16))
        run_conv(weights, buffer, image, acc, copies, rows, width)
        out_ref, outer_ref, inner_ref, stats_ref = outs
        value = acc[...] * (1.0 / math.sqrt(9 * c))
        if residual is not None:
            value = res[0][0 : rows * width, :].astype(F32) + value
        value = value.astype(BF16)
        out_ref[0 : rows * width, :] = value
        emit(flags, out_ref, outer_ref, inner_ref, stats_ref, keep, rows, width, moments_of(value.astype(F32)))

    args = (flags,) + tuple(got) + (() if residual is None else (residual,)) + tuple(pieces)
    outs = message_outs(rows, width, c, keep)
    flops = 2 * rows * width * 9 * c * c
    return call(body, name, 1, 5 + extra, len(pieces), outs, scratch_of(weights, rows + 2, rows, width), flops)(*args)


def up_conv(shape, flags, weights, pieces, got, skip, keep):
    rows, width, half = shape.rows, shape.cols, shape.half
    c, c_out = shape.wide, shape.narrow

    def body(flags, block, outer, inner, skip_ref, *rest):
        piece_refs = rest[: len(pieces)]
        outs = rest[len(pieces) : -4]
        buffer, image, acc, sems = rest[-4:]
        copies = weights.copies(flags, weights.stacks(piece_refs), buffer, sems)
        for mine in copies:
            for copy in mine:
                copy.start()
        weights.clear(image)
        mix = parity_matrix(c)
        for row in range(rows // 2 + 2):
            value, outside = ext_row(row, block, outer, inner, flags, rows // 2, 1, half)
            value = masked(value, outside).astype(BF16)
            value = jnp.dot(value, mix, preferred_element_type=F32)
            before, after = shifted(value, 1).astype(BF16), shifted(value, -1).astype(BF16)
            value = value.astype(BF16)
            for fine in (2 * row - 1, 2 * row):
                if 0 <= fine < rows + 2:
                    for tap, (even, odd) in enumerate(((before, value), (value, value), (value, after))):
                        weights.put(image, fine, 0, tap, even)
                        weights.put(image, fine, half, tap, odd)
        run_conv(weights, buffer, image, acc, copies, rows, width)
        out_ref, outer_ref, inner_ref, stats_ref, skip_stats_ref = outs
        value = (acc[...] * (1.0 / math.sqrt(9 * c))).astype(BF16)
        out_ref[0 : rows * width, :] = value
        emit(flags, out_ref, outer_ref, inner_ref, stats_ref, keep, rows, width, moments_of(value.astype(F32)))
        own = skip_ref[width : (rows + 1) * width, :].astype(F32)
        skip_stats_ref[...] = row_stack(moments_of(own), 8, c_out)

    outs = message_outs(rows, width, c_out, keep) + [((8, c_out), F32)]
    flops = 2 * rows * width * 9 * c * c_out
    scratch = scratch_of(weights, rows + 2, rows, width)
    return call(body, "up", 1, 4, len(pieces), outs, scratch, flops)(flags, *got, skip, *pieces)


def join_conv(shape, flags, weights, pieces, got, skip, skip_sums, keep):
    rows, width, half, c = shape.rows, shape.cols, shape.half, shape.narrow

    def body(flags, block, outer, inner, sa, sb, skip_ref, skip_sum, *rest):
        piece_refs = rest[: len(pieces)]
        outs = rest[len(pieces) : -4]
        buffer, image, acc, sems = rest[-4:]
        copies = weights.copies(flags, weights.stacks(piece_refs), buffer, sems)
        for mine in copies:
            for copy in mine:
                copy.start()
        weights.clear(image)
        mix = parity_matrix(c)
        for part in range(2):
            sums = sa[...] + sb[...] if part == 0 else skip_sum[...]
            mean, inv = pair_terms(sums, shape.fine_count)

            def store(row, place, size, tap, value, part=part):
                weights.put(image, row, place, tap, value.astype(BF16), first=part * c)

            for row in range(rows + 2):
                if part == 0:
                    value, outside = ext_row(row, block, outer, inner, flags, rows, 1, width)
                else:
                    value = skip_ref[row * width : (row + 1) * width, :].astype(F32)
                    outside = flags[1] != 0 if row == 0 else flags[2] != 0 if row == rows + 1 else None
                value = masked(silu((value - mean) * inv), outside).astype(BF16)
                value = jnp.dot(value, mix, preferred_element_type=F32)
                fine_columns(store, row, width, value[:half], value[half:])
        run_conv(weights, buffer, image, acc, copies, rows, width)
        out_ref, outer_ref, inner_ref, stats_ref = outs
        value = (acc[...] * (1.0 / math.sqrt(18 * c))).astype(BF16)
        out_ref[0 : rows * width, :] = value
        emit(flags, out_ref, outer_ref, inner_ref, stats_ref, keep, rows, width, moments_of(value.astype(F32)))

    outs = message_outs(rows, width, c, keep)
    flops = 2 * rows * width * 18 * c * c
    scratch = scratch_of(weights, rows + 2, rows, width)
    return call(body, "join", 1, 7, len(pieces), outs, scratch, flops)(flags, *got, skip, skip_sums, *pieces)


def pair_terms(sums, count):
    width = sums.shape[1]
    size = 2 * width // GROUPS
    terms = row_stack(bf16_terms(sums[0:1]) + bf16_terms(sums[1:2]), 16, width).astype(BF16)
    left = lax.broadcasted_iota(jnp.int32, (width, width), 0) // size
    right = lax.broadcasted_iota(jnp.int32, (width, width), 1) // size
    together = jnp.where(left == right, 1.0, 0.0).astype(BF16)
    summed = jnp.dot(terms, together, preferred_element_type=F32) * (1.0 / (count * size))
    mean = summed[0:1] + summed[1:2] + summed[2:3]
    square = summed[3:4] + summed[4:5] + summed[5:6]
    variance = jnp.maximum(square - mean * mean, 0.0)
    return mean, lax.rsqrt(variance + EPSILON)


def last_conv(shape, flags, weights, pieces, got, u, skip, j_start, n_quarters):
    rows, width, half, c = shape.rows, shape.cols, shape.half, shape.narrow
    quarter = half // n_quarters
    j_block = j_start // shape.blk

    def body(flags, block, outer, inner, sa, sb, u_ref, skip_ref, *rest):
        piece_refs = rest[: len(pieces)]
        outs = rest[len(pieces) : -6]
        buffer, image, acc, sems, jbuf, jsem = rest[-6:]
        copies = weights.copies(flags, weights.stacks(piece_refs), buffer, sems)
        for mine in copies:
            for copy in mine:
                copy.start()
        weights.clear(image)
        jcopies = []
        for low, high, owners in weights.bounds:
            if low <= j_block < high:
                for ref, owner in zip(weights.stacks(piece_refs)[low], owners, strict=True):
                    for j in range(ref.shape[0]):
                        copy = pltpu.make_async_copy(
                            ref.at[j, j_block - low], jbuf.at[owner(flags, j)], jsem.at[len(jcopies)]
                        )
                        copy.start()
                        jcopies.append(copy)
        mean, inv = group_terms(sa[...] + sb[...], shape.fine_count)
        mix = parity_matrix(c)

        def store(row, place, size, tap, value):
            weights.put(image, row, place, tap, value.astype(BF16))

        for row in range(rows + 2):
            value, outside = ext_row(row, block, outer, inner, flags, rows, 1, width)
            value = masked(silu((value - mean) * inv), outside).astype(BF16)
            value = jnp.dot(value, mix, preferred_element_type=F32)
            fine_columns(store, row, width, value[:half], value[half:])
        run_conv(weights, buffer, image, acc, copies, rows, width)
        for copy in jcopies:
            copy.wait()
        right = jbuf[...].reshape(2 * c, shape.lanes)
        left = [u_ref[0 : rows * width, :], skip_ref[width : (rows + 1) * width, :]]
        left = [jnp.dot(part, mix, preferred_element_type=F32).astype(BF16) for part in left]
        made = jnp.zeros((rows * width, c), F32)
        for odd in range(2):
            mine = jnp.concatenate(
                [part[:, odd * (c // 2) : (odd + 1) * (c // 2)] for part in left]
                + [jnp.zeros((rows * width, shape.lanes - c), BF16)],
                axis=1,
            )
            made += lax.dot_general(
                mine, right[odd * c : (odd + 1) * c], (((1,), (1,)), ((), ())), preferred_element_type=F32
            )
        value = made * (1.0 / math.sqrt(2 * c)) + acc[...] * (1.0 / math.sqrt(9 * c))
        value = value.reshape(2 * rows, half, c).astype(BF16)
        for q, out in enumerate(outs):
            out[...] = value[:, q * quarter : (q + 1) * quarter, :]

    outs = [((2 * rows, quarter, c), BF16)] * n_quarters
    flops = 2 * rows * width * 11 * c * c
    extra = [pltpu.VMEM((shape.m, shape.cols_of, shape.lanes), BF16), pltpu.SemaphoreType.DMA((8,))]
    scratch = scratch_of(weights, rows + 2, rows, width, extra)
    return call(body, "last", 1, 7, len(pieces), outs, scratch, flops)(flags, *got, u, skip, *pieces)


def pack_blocks(shape, pack, low, high):
    count, columns = high - low, pack.shape[1]

    def body(pack_ref, out_ref, rows, sem):
        copy = pltpu.make_async_copy(pack_ref.at[low * shape.blk : high * shape.blk, :], rows, sem)
        copy.start()
        left = lax.broadcasted_iota(jnp.int32, (columns, columns), 0)
        right = lax.broadcasted_iota(jnp.int32, (columns, columns), 1)
        same = jnp.where(left == right, 1.0, 0.0).astype(BF16)
        copy.wait()
        for block in range(count):
            part = rows[block * shape.blk : (block + 1) * shape.blk, :]
            made = lax.dot_general(same, part, (((1,), (1,)), ((), ())), preferred_element_type=F32)
            out_ref[block, :, 0 : shape.blk] = made.astype(BF16)
            out_ref[block, :, shape.blk :] = jnp.zeros((columns, shape.lanes - shape.blk), BF16)

    scratch = [pltpu.VMEM((count * shape.blk, columns), BF16), pltpu.SemaphoreType.DMA(())]
    outs = [((count, columns, shape.lanes), BF16)]
    return call(body, f"pack{low}", 0, 0, 1, outs, scratch, 1000, 16 * 1024 * 1024)(pack)[0]


def shards(n, n_section, features, section_packs):
    section_id = lax.axis_index("section")
    w = lax.axis_index("space")
    shape = Shape(features, section_packs, n)
    q_rows = shape.narrow * shape.narrow // shape.wide
    pack = section_packs[0]
    flags = jnp.stack([w % 2, (w == 0).astype(jnp.int32), (w == n - 1).astype(jnp.int32), section_id, w]).astype(jnp.int32)

    total = pack.shape[0] // shape.blk
    cuts = [0, 9 * q_rows // shape.blk, 18 * q_rows // shape.blk, 36 * q_rows // shape.blk, total]
    bounds = list(zip(cuts[:-1], cuts[1:], strict=True))

    def permute(value, source, target, move):
        pairs = [(source * n + i, target * n + move(i)) for i in range(n)]
        return lax.ppermute(value, ("section", "space"), pairs)

    def to_outer(i):
        return (i + 1) % n if i % 2 else (i - 1) % n

    def ahead(i):
        return (i - 2) % n if i % 2 else (i + 2) % n

    def across(i):
        return (i + 4) % n

    def partner(i):
        return i ^ 1

    def sums_of(tail):
        tail = tail.astype(F32)
        first = tail[0:1] + tail[1:2] + tail[2:3]
        second = tail[3:4] + tail[4:5] + tail[5:6]
        return jnp.concatenate([first, second, jnp.zeros((6, tail.shape[1]), F32)], 0)

    def exchange(made, source, target, extra_stats=None, with_stats=True):
        block, outer, inner, stats = made
        if source != target:
            block = permute(block, source, target, lambda i: i)
            stats = None
        outer = permute(outer, source, target, to_outer)
        inner = permute(inner, source, target, partner)
        if not with_stats:
            return block, outer, inner
        own = made[3] if stats is not None else sums_of(block[-TAIL:])
        size = own.shape[1]
        sent = made[3] if extra_stats is None else jnp.concatenate([made[3], extra_stats], 1)
        if n == 8:
            b = permute(sent, source, target, ahead)
            c = permute(sent, source, target, across)
            if extra_stats is None:
                near = sums_of(outer[-TAIL:])
            else:
                own = sent
                near = permute(sent, source, target, to_outer)
            mine = own + near + b + c
            other = permute(mine, target, target, partner)
        else:
            mine = lax.psum(sent if stats is not None else own, "space")
            other = jnp.zeros_like(mine)
        if extra_stats is None:
            return block, outer, inner, mine, other
        total = mine[:, size:] + other[:, size:]
        return (block, outer, inner, mine[:, :size], other[:, :size]), total

    def within(value, planes, move):
        pairs = [(s * n + i, s * n + move(i)) for s in planes for i in range(n)]
        return lax.ppermute(value, ("section", "space"), pairs)

    def owner_near(flags, j):
        return ((flags[4] // 2) ^ j) * 2 + flags[0]

    def owner_far(flags, j):
        return ((flags[4] // 2) ^ j) * 2 + 1 - flags[0]

    pieces = []
    previous = None
    for number, (low, high) in enumerate(bounds):
        if n == 8:
            planes = range(n_section) if number < 3 else range(1, n_section)
            own = pack_blocks(shape, pack, low, high)
            if previous is not None:
                own, _ = lax.optimization_barrier((own, previous))
            got = [within(own, planes, lambda i, k=k: i ^ (2 * k)) for k in range(1, 4)]
            previous = got
            near = jnp.stack([own] + got)
            far = within(near, planes, partner)
            pieces.append(([near, far], [owner_near, owner_far]))
        else:
            got = lax.all_gather(pack[low * shape.blk : high * shape.blk], "space")
            got = got.reshape(shape.m, n // shape.m, high - low, shape.blk, -1).transpose(0, 2, 1, 4, 3)
            got = got.reshape(shape.m, high - low, shape.cols_of, shape.blk)
            got = jnp.pad(got, ((0, 0), (0, 0), (0, 0), (0, shape.lanes - shape.blk)))
            pieces.append(([got], [lambda flags, j: j]))

    def weights(start, c_in, c_out, parts):
        first = start // shape.blk
        end = (start + 9 * c_in * c_out // shape.wide) // shape.blk
        used = [i for i, (a, b) in enumerate(bounds) if a < end and b > first]
        made = Weights(shape, [bounds[i] + (pieces[i][1],) for i in used], start, c_in, c_out)
        return made, [stack for i in used for stack in pieces[i][0]]

    narrow, wide = shape.narrow, shape.wide
    x = features[0].reshape(shape.rows, shape.half, 2, narrow).transpose(0, 2, 1, 3).reshape(-1, narrow)
    first = exchange(prepare(shape, flags, x, 1), 0, 0)
    hidden = fine_conv(shape, flags, *weights(0, narrow, narrow, (narrow,)), first, 1, 0, 2, name="c00")
    second = exchange(hidden, 0, 0)
    (skip,) = fine_conv(
        shape, flags, *weights(9 * q_rows, narrow, narrow, (narrow,)), second, 2, 1, 0, residual=first[:3], name="c01"
    )
    coarse = down_conv(shape, flags, *weights(18 * q_rows, narrow, wide, (narrow,)), skip, 1)
    for section in (1, 2):
        got = exchange(coarse, section - 1, section)
        if section == 1:
            skip, got = lax.optimization_barrier((skip, got))
            skip = permute(skip, 0, 3, lambda i: i)
        hidden = coarse_conv(shape, flags, *weights(0, wide, wide, (wide,)), got, 1, name=f"c{section}0")
        then = exchange(hidden, section, section)
        coarse = coarse_conv(
            shape, flags, *weights(36 * q_rows, wide, wide, (wide,)), then, 1, residual=got[0], name=f"c{section}1"
        )
    got = exchange(coarse, 2, 3, with_stats=False)
    *up, skip_stats = up_conv(shape, flags, *weights(0, wide, narrow, (wide,)), got, skip, 1)
    got, skip_sums = exchange(up, 3, 3, extra_stats=skip_stats)
    hidden = join_conv(shape, flags, *weights(18 * q_rows, wide, narrow, (narrow, narrow)), got, skip, skip_sums, 1)
    then = exchange(hidden, 3, 3)
    outs = last_conv(
        shape, flags, *weights(36 * q_rows, narrow, narrow, (narrow,)), then, got[0], skip, 45 * q_rows, n_section
    )
    result = jnp.where(section_id == 3, outs[3], jnp.zeros_like(outs[3]))
    for target in range(3):
        result = result + permute(outs[target], 3, target, lambda i: i)
    quarter = shape.half // n_section
    result = result.reshape(shape.rows, 2, quarter, narrow).transpose(0, 2, 1, 3)
    return result.reshape(1, shape.rows, 2 * quarter, narrow)


def solution(mesh):
    n, n_section = mesh.shape["space"], mesh.shape["section"]

    def body(features, section_packs):
        return shards(n, n_section, features, section_packs)

    return jax.shard_map(
        body,
        mesh=mesh,
        in_specs=(P(None, "space", None, None), P("section", None, "space")),
        out_specs=P(None, "space", "section", None),
        check_vma=False,
    )
```

```python
from functools import partial
import math

import jax
import jax.numpy as jnp
from jax import lax
from jax.experimental import pallas as pl
from jax.experimental.pallas import tpu as pltpu
from jax.sharding import PartitionSpec as P

GROUPS = 32
EPSILON = 1e-05
TAIL = 16
BF16 = jnp.bfloat16
F32 = jnp.float32


def row_stack(rows, count, width):
    ids = lax.broadcasted_iota(jnp.int32, (count, width), 0)
    total = jnp.zeros((count, width), F32)
    for place, row in enumerate(rows):
        total = jnp.where(ids == place, row, total)
    return total


def bf16_terms(row):
    high = row.astype(BF16).astype(F32)
    rest = row - high
    mid = rest.astype(BF16).astype(F32)
    return [high, mid, (rest - mid).astype(BF16).astype(F32)]


def moments_of(value):
    return [
        jnp.sum(value, axis=0, keepdims=True),
        jnp.sum(value * value, axis=0, keepdims=True),
    ]


def group_terms(sums, count):
    width = sums.shape[1]
    size = width // GROUPS
    terms = row_stack(bf16_terms(sums[0:1]) + bf16_terms(sums[1:2]), 16, width).astype(BF16)
    left = lax.broadcasted_iota(jnp.int32, (width, width), 0) // size
    right = lax.broadcasted_iota(jnp.int32, (width, width), 1) // size
    together = jnp.where(left == right, 1.0, 0.0).astype(BF16)
    summed = jnp.dot(terms, together, preferred_element_type=F32) * (1.0 / (count * size))
    mean = summed[0:1] + summed[1:2] + summed[2:3]
    square = summed[3:4] + summed[4:5] + summed[5:6]
    variance = jnp.maximum(square - mean * mean, 0.0)
    return mean, lax.rsqrt(variance + EPSILON)


def silu(z):
    half = 0.5 * z
    return half + half * jnp.tanh(half)


def parity_matrix(width):
    source = lax.broadcasted_iota(jnp.int32, (width, width), 0)
    target = lax.broadcasted_iota(jnp.int32, (width, width), 1)
    half = width // 2
    wanted = jnp.where(target < half, 2 * target, 2 * (target - half) + 1)
    return jnp.where(source == wanted, 1.0, 0.0).astype(BF16)


def shifted(value, step):
    rows = value.shape[0]
    ids = lax.broadcasted_iota(jnp.int32, value.shape, 0)
    if step == 1:
        return jnp.where(ids == 0, 0.0, pltpu.roll(value, 1, 0))
    return jnp.where(ids == rows - 1, 0.0, pltpu.roll(value, rows - 1, 0))


class Shape:
    def __init__(self, features, packs, n):
        self.n = n
        self.rows = features.shape[1]
        self.cols = features.shape[2]
        self.half = self.cols // 2
        self.narrow = features.shape[3]
        self.wide = 2 * self.narrow
        self.m = min(n, 8)
        self.cols_of = self.wide // self.m
        self.blk = 3 * self.narrow // 2
        self.lanes = -(-self.blk // 128) * 128
        self.fine_count = self.rows * n * self.cols
        self.coarse_count = self.fine_count // 4


def emit(flags, out_ref, outer_ref, inner_ref, stats_ref, keep, rows, width, sums):
    channels = out_ref.shape[1]
    core0 = flags[0] == 0
    tail = row_stack(bf16_terms(sums[0]) + bf16_terms(sums[1]), TAIL, channels).astype(BF16)
    out_ref[rows * width :, :] = tail
    stats_ref[...] = row_stack(sums, 8, channels)
    size = keep * width
    first = out_ref[0:size, :].astype(F32)
    last = out_ref[(rows - keep) * width : rows * width, :].astype(F32)
    outer_ref[0:size, :] = jnp.where(core0, first, last).astype(BF16)
    outer_ref[size:, :] = tail
    inner_ref[...] = jnp.where(core0, last, first).astype(BF16)


def ext_row(index, block_ref, outer_ref, inner_ref, flags, rows, halo, width):
    if index < halo:
        span = slice(index * width, (index + 1) * width)
        pick = jnp.where(flags[0] == 0, outer_ref[span, :].astype(F32), inner_ref[span, :].astype(F32))
        return pick, flags[1] != 0
    index -= halo
    if index < rows:
        return block_ref[index * width : (index + 1) * width, :].astype(F32), None
    index -= rows
    span = slice(index * width, (index + 1) * width)
    pick = jnp.where(flags[0] == 0, inner_ref[span, :].astype(F32), outer_ref[span, :].astype(F32))
    return pick, flags[2] != 0


def masked(value, outside):
    if outside is None:
        return value
    return jnp.where(outside, 0.0, value)


class Weights:
    def __init__(self, shape, bounds, start, c_in, c_out):
        self.shape = shape
        self.c_in = c_in
        self.c_out = c_out
        self.split = c_out != shape.wide
        self.blocks = 3 * c_in * c_out // shape.wide // shape.blk
        self.start = start // shape.blk
        self.bounds = bounds
        self.depth = self.blocks * shape.lanes
        self.width = (2 if self.split else 1) * self.depth

    def stacks(self, refs):
        refs = list(refs)
        return {low: [refs.pop(0) for _ in owners] for low, _, owners in self.bounds}

    def copies(self, flags, stack_refs, buffer, sems):
        made = []
        lanes = self.shape.lanes
        for dy in range(3):
            mine = []
            begin = self.start + dy * self.blocks
            for low, high, owners in self.bounds:
                a, b = max(begin, low), min(begin + self.blocks, high)
                if a >= b:
                    continue
                for ref, owner in zip(stack_refs[low], owners, strict=True):
                    for j in range(ref.shape[0]):
                        mine.append(
                            pltpu.make_async_copy(
                                ref.at[j, :, (a - low) * lanes : (b - low) * lanes],
                                self.slot(buffer.at[dy], owner(flags, j), a - begin, b - begin),
                                sems.at[dy, len(mine)],
                            )
                        )
            made.append(mine)
        return made

    def slot(self, target, owner, first, last):
        lanes = self.shape.lanes
        if not self.split:
            return target.at[owner, :, first * lanes : last * lanes]
        half = self.shape.m // 2
        shift = pl.multiple_of(owner // half * self.depth, lanes)
        return target.at[owner % half, :, pl.ds(first * lanes + shift, (last - first) * lanes)]

    def product(self, left, buffer, dy):
        right = buffer[dy].reshape(self.c_out, self.width)
        return lax.dot_general(left, right, (((1,), (1,)), ((), ())), preferred_element_type=F32)

    def put(self, image, row, place, tap, value, first=0, channels=None):
        shape = self.shape
        size = value.shape[0]
        half = self.c_in // 2
        runs = []
        if self.split:
            c = value.shape[1] // 2
            runs = [(odd, tap * half + first // 2, odd * c, c) for odd in range(2)]
        else:
            runs = [(0, tap * self.c_in + first, 0, value.shape[1])]
        for odd, index, at, left in runs:
            while left > 0:
                step = min(left, shape.blk - index % shape.blk)
                lane = odd * self.depth + index // shape.blk * shape.lanes + index % shape.blk
                image[row, place : place + size, lane : lane + step] = value[:, at : at + step]
                index, at, left = index + step, at + step, left - step

    def clear(self, image):
        shape = self.shape
        for block in range(self.width // shape.lanes):
            begin = block * shape.lanes + shape.blk
            end = (block + 1) * shape.lanes
            image[:, :, begin:end] = jnp.zeros((image.shape[0], image.shape[1], end - begin), BF16)


def fine_columns(store, row, width, even, odd):
    half = even.shape[0]
    store(row, 0, half, 0, shifted(odd, 1))
    store(row, 0, half, 1, even)
    store(row, 0, half, 2, odd)
    store(row, half, half, 0, even)
    store(row, half, half, 1, odd)
    store(row, half, half, 2, shifted(even, -1))


def run_conv(weights, buffer, image, acc, copies, rows, width):
    for dy in range(3):
        for copy in copies[dy]:
            copy.wait()
        left = image[dy : dy + rows].reshape(rows * width, weights.width)
        made = weights.product(left, buffer, dy)
        if dy == 0:
            acc[...] = made
        else:
            acc[...] += made


def scratch_of(weights, image_rows, out_rows, width, extra=()):
    return [
        pltpu.VMEM((3, weights.c_out // weights.shape.cols_of, weights.shape.cols_of, weights.width), BF16),
        pltpu.VMEM((image_rows, width, weights.width), BF16),
        pltpu.VMEM((out_rows * width, weights.c_out), F32),
        pltpu.SemaphoreType.DMA((3, 16)),
    ] + list(extra)


def call(body, name, n_smem, n_vmem, n_any, outs, scratch, flops, limit=60 * 1024 * 1024):
    specs = (
        [pl.BlockSpec(memory_space=pltpu.SMEM)] * n_smem
        + [pl.BlockSpec(memory_space=pltpu.VMEM)] * n_vmem
        + [pl.BlockSpec(memory_space=pltpu.HBM)] * n_any
    )
    return pl.pallas_call(
        body,
        out_shape=[jax.ShapeDtypeStruct(s, d) for s, d in outs],
        in_specs=specs,
        out_specs=[pl.BlockSpec(memory_space=pltpu.VMEM)] * len(outs),
        scratch_shapes=scratch,
        compiler_params=pltpu.CompilerParams(vmem_limit_bytes=limit),
        cost_estimate=pl.CostEstimate(flops=flops, bytes_accessed=4_000_000, transcendentals=0),
        name=name,
    )


def message_outs(rows, width, channels, keep):
    return [
        ((rows * width + TAIL, channels), BF16),
        ((keep * width + TAIL, channels), BF16),
        ((keep * width, channels), BF16),
        ((8, channels), F32),
    ]


def prepare(shape, flags, x, keep):
    rows, width, c = shape.rows, shape.cols, shape.narrow

    def body(flags, x_ref, out_ref, outer_ref, inner_ref, stats_ref):
        out_ref[0 : rows * width, :] = x_ref[...]
        sums = moments_of(x_ref[...].astype(F32))
        emit(flags, out_ref, outer_ref, inner_ref, stats_ref, keep, rows, width, sums)

    return call(body, "prepare", 1, 1, 0, message_outs(rows, width, c, keep), [], 1000)(flags, x)


def fine_conv(shape, flags, weights, pieces, got, halo, out_halo, keep, residual=None, name="fine"):
    rows, width, half, c = shape.rows, shape.cols, shape.half, shape.narrow
    out_rows = rows + 2 * out_halo
    image_rows = out_rows + 2
    n_pieces = len(pieces)
    extra = 0 if residual is None else 3

    def body(flags, block, outer, inner, sa, sb, *rest):
        res = rest[:extra]
        piece_refs = rest[extra : extra + n_pieces]
        rest = rest[extra + n_pieces :]
        outs = rest[:-4]
        buffer, image, acc, sems = rest[-4:]
        copies = weights.copies(flags, weights.stacks(piece_refs), buffer, sems)
        for mine in copies:
            for copy in mine:
                copy.start()
        weights.clear(image)
        mean, inv = group_terms(sa[...] + sb[...], shape.fine_count)
        mix = parity_matrix(c)

        def store(row, place, size, tap, value):
            weights.put(image, row, place, tap, value.astype(BF16))

        for row in range(image_rows):
            value, outside = ext_row(row + halo - out_halo - 1, block, outer, inner, flags, rows, halo, width)
            value = masked(silu((value - mean) * inv), outside).astype(BF16)
            value = jnp.dot(value, mix, preferred_element_type=F32)
            fine_columns(store, row, width, value[:half], value[half:])
        run_conv(weights, buffer, image, acc, copies, out_rows, width)
        scale = 1.0 / math.sqrt(9 * c)
        if residual is None:
            out_ref, outer_ref, inner_ref, stats_ref = outs
            value = (acc[...] * scale).astype(BF16)
            out_ref[0 : rows * width, :] = value
            emit(flags, out_ref, outer_ref, inner_ref, stats_ref, keep, rows, width, moments_of(value.astype(F32)))
        else:
            (out_ref,) = outs
            for row in range(out_rows):
                own, _ = ext_row(row, res[0], res[1], res[2], flags, rows, out_halo, width)
                span = slice(row * width, (row + 1) * width)
                out_ref[span, :] = (own + acc[span, :] * scale).astype(BF16)

    outs = message_outs(rows, width, c, keep) if residual is None else [((out_rows * width, c), BF16)]
    args = (flags,) + tuple(got) + (() if residual is None else tuple(residual)) + tuple(pieces)
    flops = 2 * out_rows * width * 9 * c * c
    return call(body, name, 1, 5 + extra, n_pieces, outs, scratch_of(weights, image_rows, out_rows, width), flops)(*args)


def down_conv(shape, flags, weights, pieces, skip, keep):
    rows, width, half, c = shape.rows, shape.cols, shape.half, shape.narrow
    out_rows = rows // 2

    def body(flags, skip_ref, *rest):
        piece_refs = rest[: len(pieces)]
        outs = rest[len(pieces) : -4]
        buffer, image, acc, sems = rest[-4:]
        copies = weights.copies(flags, weights.stacks(piece_refs), buffer, sems)
        for mine in copies:
            for copy in mine:
                copy.start()
        weights.clear(image)
        for row in range(rows + 1):
            value = skip_ref[row * width : (row + 1) * width, :].astype(F32)
            if row == 0:
                value = masked(value, flags[1] != 0)
            even, odd = value[:half], value[half:]
            place = (row % 2) * (out_rows + 1) + row // 2
            weights.put(image, place, 0, 0, shifted(odd, 1).astype(BF16))
            weights.put(image, place, 0, 1, even.astype(BF16))
            weights.put(image, place, 0, 2, odd.astype(BF16))
        for dy in range(3):
            for copy in copies[dy]:
                copy.wait()
            begin = (0, out_rows + 1, 1)[dy]
            left = image[begin : begin + out_rows].reshape(out_rows * half, weights.width)
            made = weights.product(left, buffer, dy)
            if dy == 0:
                acc[...] = made
            else:
                acc[...] += made
        out_ref, outer_ref, inner_ref, stats_ref = outs
        value = (acc[...] * (1.0 / math.sqrt(9 * c))).astype(BF16)
        out_ref[0 : out_rows * half, :] = value
        emit(flags, out_ref, outer_ref, inner_ref, stats_ref, keep, out_rows, half, moments_of(value.astype(F32)))

    scratch = scratch_of(weights, 2 * (out_rows + 1), out_rows, half)
    outs = message_outs(out_rows, half, shape.wide, keep)
    return call(body, "down", 1, 1, len(pieces), outs, scratch, 2 * out_rows * half * 9 * c * shape.wide)(flags, skip, *pieces)


def coarse_conv(shape, flags, weights, pieces, got, keep, residual=None, name="coarse"):
    rows, width, c = shape.rows // 2, shape.half, shape.wide
    extra = 0 if residual is None else 1

    def body(flags, block, outer, inner, sa, sb, *rest):
        res = rest[:extra]
        piece_refs = rest[extra : extra + len(pieces)]
        outs = rest[extra + len(pieces) : -4]
        buffer, image, acc, sems = rest[-4:]
        copies = weights.copies(flags, weights.stacks(piece_refs), buffer, sems)
        for mine in copies:
            for copy in mine:
                copy.start()
        weights.clear(image)
        mean, inv = group_terms(sa[...] + sb[...], shape.coarse_count)
        for row in range(rows + 2):
            value, outside = ext_row(row, block, outer, inner, flags, rows, 1, width)
            value = masked(silu((value - mean) * inv), outside)
            weights.put(image, row, 0, 0, shifted(value, 1).astype(BF16))
            weights.put(image, row, 0, 1, value.astype(BF16))
            weights.put(image, row, 0, 2, shifted(value, -1).astype(BF16))
        run_conv(weights, buffer, image, acc, copies, rows, width)
        out_ref, outer_ref, inner_ref, stats_ref = outs
        value = acc[...] * (1.0 / math.sqrt(9 * c))
        if residual is not None:
            value = res[0][0 : rows * width, :].astype(F32) + value
        value = value.astype(BF16)
        out_ref[0 : rows * width, :] = value
        emit(flags, out_ref, outer_ref, inner_ref, stats_ref, keep, rows, width, moments_of(value.astype(F32)))

    args = (flags,) + tuple(got) + (() if residual is None else (residual,)) + tuple(pieces)
    outs = message_outs(rows, width, c, keep)
    flops = 2 * rows * width * 9 * c * c
    return call(body, name, 1, 5 + extra, len(pieces), outs, scratch_of(weights, rows + 2, rows, width), flops)(*args)


def up_conv(shape, flags, weights, pieces, got, skip, keep):
    rows, width, half = shape.rows, shape.cols, shape.half
    c, c_out = shape.wide, shape.narrow

    def body(flags, block, outer, inner, skip_ref, *rest):
        piece_refs = rest[: len(pieces)]
        outs = rest[len(pieces) : -4]
        buffer, image, acc, sems = rest[-4:]
        copies = weights.copies(flags, weights.stacks(piece_refs), buffer, sems)
        for mine in copies:
            for copy in mine:
                copy.start()
        weights.clear(image)
        mix = parity_matrix(c)
        for row in range(rows // 2 + 2):
            value, outside = ext_row(row, block, outer, inner, flags, rows // 2, 1, half)
            value = masked(value, outside).astype(BF16)
            value = jnp.dot(value, mix, preferred_element_type=F32)
            before, after = shifted(value, 1).astype(BF16), shifted(value, -1).astype(BF16)
            value = value.astype(BF16)
            for fine in (2 * row - 1, 2 * row):
                if 0 <= fine < rows + 2:
                    for tap, (even, odd) in enumerate(((before, value), (value, value), (value, after))):
                        weights.put(image, fine, 0, tap, even)
                        weights.put(image, fine, half, tap, odd)
        run_conv(weights, buffer, image, acc, copies, rows, width)
        out_ref, outer_ref, inner_ref, stats_ref, skip_stats_ref = outs
        value = (acc[...] * (1.0 / math.sqrt(9 * c))).astype(BF16)
        out_ref[0 : rows * width, :] = value
        emit(flags, out_ref, outer_ref, inner_ref, stats_ref, keep, rows, width, moments_of(value.astype(F32)))
        own = skip_ref[width : (rows + 1) * width, :].astype(F32)
        skip_stats_ref[...] = row_stack(moments_of(own), 8, c_out)

    outs = message_outs(rows, width, c_out, keep) + [((8, c_out), F32)]
    flops = 2 * rows * width * 9 * c * c_out
    scratch = scratch_of(weights, rows + 2, rows, width)
    return call(body, "up", 1, 4, len(pieces), outs, scratch, flops)(flags, *got, skip, *pieces)


def join_conv(shape, flags, weights, pieces, got, skip, skip_sums, keep):
    rows, width, half, c = shape.rows, shape.cols, shape.half, shape.narrow

    def body(flags, block, outer, inner, sa, sb, skip_ref, skip_sum, *rest):
        piece_refs = rest[: len(pieces)]
        outs = rest[len(pieces) : -4]
        buffer, image, acc, sems = rest[-4:]
        copies = weights.copies(flags, weights.stacks(piece_refs), buffer, sems)
        for mine in copies:
            for copy in mine:
                copy.start()
        weights.clear(image)
        mix = parity_matrix(c)
        for part in range(2):
            sums = sa[...] + sb[...] if part == 0 else skip_sum[...]
            mean, inv = pair_terms(sums, shape.fine_count)

            def store(row, place, size, tap, value, part=part):
                weights.put(image, row, place, tap, value.astype(BF16), first=part * c)

            for row in range(rows + 2):
                if part == 0:
                    value, outside = ext_row(row, block, outer, inner, flags, rows, 1, width)
                else:
                    value = skip_ref[row * width : (row + 1) * width, :].astype(F32)
                    outside = flags[1] != 0 if row == 0 else flags[2] != 0 if row == rows + 1 else None
                value = masked(silu((value - mean) * inv), outside).astype(BF16)
                value = jnp.dot(value, mix, preferred_element_type=F32)
                fine_columns(store, row, width, value[:half], value[half:])
        run_conv(weights, buffer, image, acc, copies, rows, width)
        out_ref, outer_ref, inner_ref, stats_ref = outs
        value = (acc[...] * (1.0 / math.sqrt(18 * c))).astype(BF16)
        out_ref[0 : rows * width, :] = value
        emit(flags, out_ref, outer_ref, inner_ref, stats_ref, keep, rows, width, moments_of(value.astype(F32)))

    outs = message_outs(rows, width, c, keep)
    flops = 2 * rows * width * 18 * c * c
    scratch = scratch_of(weights, rows + 2, rows, width)
    return call(body, "join", 1, 7, len(pieces), outs, scratch, flops)(flags, *got, skip, skip_sums, *pieces)


def pair_terms(sums, count):
    width = sums.shape[1]
    size = 2 * width // GROUPS
    terms = row_stack(bf16_terms(sums[0:1]) + bf16_terms(sums[1:2]), 16, width).astype(BF16)
    left = lax.broadcasted_iota(jnp.int32, (width, width), 0) // size
    right = lax.broadcasted_iota(jnp.int32, (width, width), 1) // size
    together = jnp.where(left == right, 1.0, 0.0).astype(BF16)
    summed = jnp.dot(terms, together, preferred_element_type=F32) * (1.0 / (count * size))
    mean = summed[0:1] + summed[1:2] + summed[2:3]
    square = summed[3:4] + summed[4:5] + summed[5:6]
    variance = jnp.maximum(square - mean * mean, 0.0)
    return mean, lax.rsqrt(variance + EPSILON)


def last_conv(shape, flags, weights, pieces, got, u, skip, j_start, n_quarters):
    rows, width, half, c = shape.rows, shape.cols, shape.half, shape.narrow
    quarter = half // n_quarters
    j_block = j_start // shape.blk

    def body(flags, block, outer, inner, sa, sb, u_ref, skip_ref, *rest):
        piece_refs = rest[: len(pieces)]
        outs = rest[len(pieces) : -6]
        buffer, image, acc, sems, jbuf, jsem = rest[-6:]
        copies = weights.copies(flags, weights.stacks(piece_refs), buffer, sems)
        for mine in copies:
            for copy in mine:
                copy.start()
        weights.clear(image)
        jcopies = []
        for low, high, owners in weights.bounds:
            if low <= j_block < high:
                for ref, owner in zip(weights.stacks(piece_refs)[low], owners, strict=True):
                    for j in range(ref.shape[0]):
                        copy = pltpu.make_async_copy(
                            ref.at[j, :, (j_block - low) * shape.lanes : (j_block - low + 1) * shape.lanes],
                            jbuf.at[owner(flags, j)],
                            jsem.at[len(jcopies)],
                        )
                        copy.start()
                        jcopies.append(copy)
        mean, inv = group_terms(sa[...] + sb[...], shape.fine_count)
        mix = parity_matrix(c)

        def store(row, place, size, tap, value):
            weights.put(image, row, place, tap, value.astype(BF16))

        for row in range(rows + 2):
            value, outside = ext_row(row, block, outer, inner, flags, rows, 1, width)
            value = masked(silu((value - mean) * inv), outside).astype(BF16)
            value = jnp.dot(value, mix, preferred_element_type=F32)
            fine_columns(store, row, width, value[:half], value[half:])
        run_conv(weights, buffer, image, acc, copies, rows, width)
        for copy in jcopies:
            copy.wait()
        right = jbuf[...].reshape(2 * c, shape.lanes)
        left = [u_ref[0 : rows * width, :], skip_ref[width : (rows + 1) * width, :]]
        left = [jnp.dot(part, mix, preferred_element_type=F32).astype(BF16) for part in left]
        made = jnp.zeros((rows * width, c), F32)
        for odd in range(2):
            mine = jnp.concatenate(
                [part[:, odd * (c // 2) : (odd + 1) * (c // 2)] for part in left]
                + [jnp.zeros((rows * width, shape.lanes - c), BF16)],
                axis=1,
            )
            made += lax.dot_general(
                mine, right[odd * c : (odd + 1) * c], (((1,), (1,)), ((), ())), preferred_element_type=F32
            )
        value = made * (1.0 / math.sqrt(2 * c)) + acc[...] * (1.0 / math.sqrt(9 * c))
        value = value.reshape(2 * rows, half, c).astype(BF16)
        for q, out in enumerate(outs):
            out[...] = value[:, q * quarter : (q + 1) * quarter, :]

    outs = [((2 * rows, quarter, c), BF16)] * n_quarters
    flops = 2 * rows * width * 11 * c * c
    extra = [pltpu.VMEM((shape.m, shape.cols_of, shape.lanes), BF16), pltpu.SemaphoreType.DMA((8,))]
    scratch = scratch_of(weights, rows + 2, rows, width, extra)
    return call(body, "last", 1, 7, len(pieces), outs, scratch, flops)(flags, *got, u, skip, *pieces)


def pack_blocks(shape, pack, low, high):
    count, columns = high - low, pack.shape[1]

    def body(pack_ref, out_ref, rows, sem):
        copy = pltpu.make_async_copy(pack_ref.at[low * shape.blk : high * shape.blk, :], rows, sem)
        copy.start()
        left = lax.broadcasted_iota(jnp.int32, (columns, columns), 0)
        right = lax.broadcasted_iota(jnp.int32, (columns, columns), 1)
        same = jnp.where(left == right, 1.0, 0.0).astype(BF16)
        copy.wait()
        for block in range(count):
            part = rows[block * shape.blk : (block + 1) * shape.blk, :]
            made = lax.dot_general(same, part, (((1,), (1,)), ((), ())), preferred_element_type=F32)
            begin, end = block * shape.lanes, (block + 1) * shape.lanes
            out_ref[:, begin : begin + shape.blk] = made.astype(BF16)
            out_ref[:, begin + shape.blk : end] = jnp.zeros((columns, shape.lanes - shape.blk), BF16)

    scratch = [pltpu.VMEM((count * shape.blk, columns), BF16), pltpu.SemaphoreType.DMA(())]
    outs = [((columns, count * shape.lanes), BF16)]
    return call(body, f"pack{low}", 0, 0, 1, outs, scratch, 1000)(pack)[0]


def shards(n, n_section, features, section_packs):
    section_id = lax.axis_index("section")
    w = lax.axis_index("space")
    shape = Shape(features, section_packs, n)
    q_rows = shape.narrow * shape.narrow // shape.wide
    pack = section_packs[0]
    flags = jnp.stack([w % 2, (w == 0).astype(jnp.int32), (w == n - 1).astype(jnp.int32), section_id, w]).astype(jnp.int32)

    total = pack.shape[0] // shape.blk
    cuts = [0, 9 * q_rows // shape.blk, 36 * q_rows // shape.blk, total]
    bounds = list(zip(cuts[:-1], cuts[1:], strict=True))

    def permute(value, source, target, move):
        pairs = [(source * n + i, target * n + move(i)) for i in range(n)]
        return lax.ppermute(value, ("section", "space"), pairs)

    def to_outer(i):
        return (i + 1) % n if i % 2 else (i - 1) % n

    def ahead(i):
        return (i - 2) % n if i % 2 else (i + 2) % n

    def across(i):
        return (i + 4) % n

    def partner(i):
        return i ^ 1

    def sums_of(tail):
        tail = tail.astype(F32)
        first = tail[0:1] + tail[1:2] + tail[2:3]
        second = tail[3:4] + tail[4:5] + tail[5:6]
        return jnp.concatenate([first, second, jnp.zeros((6, tail.shape[1]), F32)], 0)

    def exchange(made, source, target, extra_stats=None, with_stats=True):
        block, outer, inner, stats = made
        if source != target:
            block = permute(block, source, target, lambda i: i)
            stats = None
        outer = permute(outer, source, target, to_outer)
        inner = permute(inner, source, target, partner)
        if not with_stats:
            return block, outer, inner
        own = made[3] if stats is not None else sums_of(block[-TAIL:])
        size = own.shape[1]
        sent = made[3] if extra_stats is None else jnp.concatenate([made[3], extra_stats], 1)
        if n == 8:
            b = permute(sent, source, target, ahead)
            c = permute(sent, source, target, across)
            if extra_stats is None:
                near = sums_of(outer[-TAIL:])
            else:
                own = sent
                near = permute(sent, source, target, to_outer)
            mine = own + near + b + c
            other = permute(mine, target, target, partner)
        else:
            mine = lax.psum(sent if stats is not None else own, "space")
            other = jnp.zeros_like(mine)
        if extra_stats is None:
            return block, outer, inner, mine, other
        total = mine[:, size:] + other[:, size:]
        return (block, outer, inner, mine[:, :size], other[:, :size]), total

    def within(value, planes, move):
        pairs = [(s * n + i, s * n + move(i)) for s in planes for i in range(n)]
        return lax.ppermute(value, ("section", "space"), pairs)

    def owner_near(flags, j):
        return ((flags[4] // 2) ^ j) * 2 + flags[0]

    def owner_far(flags, j):
        return ((flags[4] // 2) ^ j) * 2 + 1 - flags[0]

    def after(value, *deps):
        return lax.optimization_barrier((value,) + deps)[0]

    pieces = {}

    def send(number, *deps):
        low, high = bounds[number]
        if n == 8:
            planes = range(n_section) if number < 2 else range(1, n_section)
            own = after(pack_blocks(shape, pack, low, high), *deps)
            return [own] + [within(own, planes, lambda i, k=k: i ^ (2 * k)) for k in range(1, 4)]
        got = lax.all_gather(pack[low * shape.blk : high * shape.blk], "space")
        got = got.reshape(shape.m, n // shape.m, high - low, shape.blk, -1).transpose(0, 1, 4, 2, 3)
        got = got.reshape(shape.m, shape.cols_of, high - low, shape.blk)
        got = jnp.pad(got, ((0, 0), (0, 0), (0, 0), (0, shape.lanes - shape.blk)))
        return [got.reshape(shape.m, shape.cols_of, -1)]

    def finish(number, got, *deps):
        if n == 8:
            near = after(jnp.stack(got), *deps)
            far = within(near, range(n_section) if number < 2 else range(1, n_section), partner)
            pieces[number] = ([near, far], [owner_near, owner_far])
        else:
            pieces[number] = (got, [lambda flags, j: j])

    def weights(start, c_in, c_out, parts):
        first = start // shape.blk
        end = (start + 9 * c_in * c_out // shape.wide) // shape.blk
        used = [i for i, (a, b) in enumerate(bounds) if a < end and b > first]
        made = Weights(shape, [bounds[i] + (pieces[i][1],) for i in used], start, c_in, c_out)
        return made, [stack for i in used for stack in pieces[i][0]]

    narrow, wide = shape.narrow, shape.wide
    x = features[0].reshape(shape.rows, shape.half, 2, narrow).transpose(0, 2, 1, 3).reshape(-1, narrow)
    sent = send(0)
    first = exchange(prepare(shape, flags, after(x, sent[0]), 1), 0, 0)
    finish(0, sent)
    sent = send(1, sent, first)
    hidden = fine_conv(shape, flags, *weights(0, narrow, narrow, (narrow,)), first, 1, 0, 2, name="c00")
    second = exchange(hidden, 0, 0)
    finish(1, sent, second)
    sent = send(2, sent, pieces[1][0])
    (skip,) = fine_conv(
        shape, flags, *weights(9 * q_rows, narrow, narrow, (narrow,)), second, 2, 1, 0, residual=first[:3], name="c01"
    )
    coarse = down_conv(shape, flags, *weights(18 * q_rows, narrow, wide, (narrow,)), skip, 1)
    for section in (1, 2):
        got = exchange(coarse, section - 1, section)
        if section == 1:
            skip, got = lax.optimization_barrier((skip, got))
            skip = permute(skip, 0, 3, lambda i: i)
        hidden = coarse_conv(shape, flags, *weights(0, wide, wide, (wide,)), got, 1, name=f"c{section}0")
        if section == 1:
            finish(2, sent, hidden[3])
        then = exchange(hidden, section, section)
        coarse = coarse_conv(
            shape, flags, *weights(36 * q_rows, wide, wide, (wide,)), then, 1, residual=got[0], name=f"c{section}1"
        )
    got = exchange(coarse, 2, 3, with_stats=False)
    *up, skip_stats = up_conv(shape, flags, *weights(0, wide, narrow, (wide,)), got, skip, 1)
    got, skip_sums = exchange(up, 3, 3, extra_stats=skip_stats)
    hidden = join_conv(shape, flags, *weights(18 * q_rows, wide, narrow, (narrow, narrow)), got, skip, skip_sums, 1)
    then = exchange(hidden, 3, 3)
    outs = last_conv(
        shape, flags, *weights(36 * q_rows, narrow, narrow, (narrow,)), then, got[0], skip, 45 * q_rows, n_section
    )
    result = jnp.where(section_id == 3, outs[3], jnp.zeros_like(outs[3]))
    for target in range(3):
        result = result + permute(outs[target], 3, target, lambda i: i)
    quarter = shape.half // n_section
    result = result.reshape(shape.rows, 2, quarter, narrow).transpose(0, 2, 1, 3)
    return result.reshape(1, shape.rows, 2 * quarter, narrow)


def solution(mesh):
    n, n_section = mesh.shape["space"], mesh.shape["section"]

    def body(features, section_packs):
        return shards(n, n_section, features, section_packs)

    return jax.shard_map(
        body,
        mesh=mesh,
        in_specs=(P(None, "space", None, None), P("section", None, "space")),
        out_specs=P(None, "space", "section", None),
        check_vma=False,
    )
```

```python
import math

import jax
import jax.numpy as jnp
from jax import lax
from jax.experimental import pallas as pl
from jax.experimental.pallas import tpu as pltpu
from jax.sharding import PartitionSpec as P


GROUPS = 32
EPSILON = 1e-05
TAIL = 16
BF16 = jnp.bfloat16
F32 = jnp.float32


def row_stack(rows, count, width):
    ids = lax.broadcasted_iota(jnp.int32, (count, width), 0)
    total = jnp.zeros((count, width), F32)
    for place, row in enumerate(rows):
        total = jnp.where(ids == place, row, total)
    return total


def bf16_terms(row):
    high = row.astype(BF16).astype(F32)
    rest = row - high
    mid = rest.astype(BF16).astype(F32)
    return [high, mid, (rest - mid).astype(BF16).astype(F32)]


def moments_of(value):
    return [
        jnp.sum(value, axis=0, keepdims=True),
        jnp.sum(value * value, axis=0, keepdims=True),
    ]


def group_terms(sums, count):
    width = sums.shape[1]
    size = width // GROUPS
    terms = row_stack(bf16_terms(sums[0:1]) + bf16_terms(sums[1:2]), 16, width).astype(BF16)
    left = lax.broadcasted_iota(jnp.int32, (width, width), 0) // size
    right = lax.broadcasted_iota(jnp.int32, (width, width), 1) // size
    together = jnp.where(left == right, 1.0, 0.0).astype(BF16)
    summed = jnp.dot(terms, together, preferred_element_type=F32) * (1.0 / (count * size))
    mean = summed[0:1] + summed[1:2] + summed[2:3]
    square = summed[3:4] + summed[4:5] + summed[5:6]
    variance = jnp.maximum(square - mean * mean, 0.0)
    return mean, lax.rsqrt(variance + EPSILON)


def silu(z):
    half = 0.5 * z
    return half + half * jnp.tanh(half)


def parity_matrix(width):
    source = lax.broadcasted_iota(jnp.int32, (width, width), 0)
    target = lax.broadcasted_iota(jnp.int32, (width, width), 1)
    half = width // 2
    wanted = jnp.where(target < half, 2 * target, 2 * (target - half) + 1)
    return jnp.where(source == wanted, 1.0, 0.0).astype(BF16)


def shifted(value, step):
    rows = value.shape[0]
    ids = lax.broadcasted_iota(jnp.int32, value.shape, 0)
    if step == 1:
        return jnp.where(ids == 0, 0.0, pltpu.roll(value, 1, 0))
    return jnp.where(ids == rows - 1, 0.0, pltpu.roll(value, rows - 1, 0))


class Shape:
    def __init__(self, features, n):
        self.rows = features.shape[1]
        self.cols = features.shape[2]
        self.half = self.cols // 2
        self.narrow = features.shape[3]
        self.wide = 2 * self.narrow
        self.m = min(n, 8)
        self.cols_of = self.wide // self.m
        self.blk = 3 * self.narrow // 2
        self.lanes = -(-self.blk // 128) * 128
        self.fine_count = self.rows * n * self.cols
        self.coarse_count = self.fine_count // 4


def emit(flags, out_ref, outer_ref, inner_ref, stats_ref, keep, rows, width, sums):
    channels = out_ref.shape[1]
    core0 = flags[0] == 0
    tail = row_stack(bf16_terms(sums[0]) + bf16_terms(sums[1]), TAIL, channels).astype(BF16)
    out_ref[rows * width :, :] = tail
    stats_ref[...] = row_stack(sums, 8, channels)
    size = keep * width
    first = out_ref[0:size, :].astype(F32)
    last = out_ref[(rows - keep) * width : rows * width, :].astype(F32)
    outer_ref[0:size, :] = jnp.where(core0, first, last).astype(BF16)
    outer_ref[size:, :] = tail
    inner_ref[...] = jnp.where(core0, last, first).astype(BF16)


def ext_row(index, block_ref, outer_ref, inner_ref, flags, rows, halo, width):
    if index < halo:
        span = slice(index * width, (index + 1) * width)
        pick = jnp.where(flags[0] == 0, outer_ref[span, :].astype(F32), inner_ref[span, :].astype(F32))
        return pick, flags[1] != 0
    index -= halo
    if index < rows:
        return block_ref[index * width : (index + 1) * width, :].astype(F32), None
    index -= rows
    span = slice(index * width, (index + 1) * width)
    pick = jnp.where(flags[0] == 0, inner_ref[span, :].astype(F32), outer_ref[span, :].astype(F32))
    return pick, flags[2] != 0


def masked(value, outside):
    if outside is None:
        return value
    return jnp.where(outside, 0.0, value)


class Weights:
    def __init__(self, shape, bounds, start, c_in, c_out):
        self.shape = shape
        self.c_in = c_in
        self.c_out = c_out
        self.split = c_out != shape.wide
        self.blocks = 3 * c_in * c_out // shape.wide // shape.blk
        self.start = start // shape.blk
        self.bounds = bounds
        self.depth = self.blocks * shape.lanes
        self.width = (2 if self.split else 1) * self.depth

    def stacks(self, refs):
        refs = list(refs)
        return {low: [refs.pop(0) for _ in owners] for low, _, owners in self.bounds}

    def copies(self, flags, stack_refs, buffer, sems):
        made = []
        lanes = self.shape.lanes
        for dy in range(3):
            mine = []
            begin = self.start + dy * self.blocks
            for low, high, owners in self.bounds:
                a, b = max(begin, low), min(begin + self.blocks, high)
                if a >= b:
                    continue
                for ref, owner in zip(stack_refs[low], owners, strict=True):
                    for j in range(ref.shape[0]):
                        mine.append(
                            pltpu.make_async_copy(
                                ref.at[j, :, (a - low) * lanes : (b - low) * lanes],
                                self.slot(buffer.at[dy], owner(flags, j), a - begin, b - begin),
                                sems.at[dy, len(mine)],
                            )
                        )
            made.append(mine)
        return made

    def slot(self, target, owner, first, last):
        lanes = self.shape.lanes
        if not self.split:
            return target.at[owner, :, first * lanes : last * lanes]
        half = self.shape.m // 2
        shift = pl.multiple_of(owner // half * self.depth, lanes)
        return target.at[owner % half, :, pl.ds(first * lanes + shift, (last - first) * lanes)]

    def product(self, left, buffer, dy):
        right = buffer[dy].reshape(self.c_out, self.width)
        return lax.dot_general(left, right, (((1,), (1,)), ((), ())), preferred_element_type=F32)

    def put(self, image, row, place, tap, value, first=0, channels=None):
        shape = self.shape
        size = value.shape[0]
        half = self.c_in // 2
        runs = []
        if self.split:
            c = value.shape[1] // 2
            runs = [(odd, tap * half + first // 2, odd * c, c) for odd in range(2)]
        else:
            runs = [(0, tap * self.c_in + first, 0, value.shape[1])]
        for odd, index, at, left in runs:
            while left > 0:
                step = min(left, shape.blk - index % shape.blk)
                lane = odd * self.depth + index // shape.blk * shape.lanes + index % shape.blk
                image[row, place : place + size, lane : lane + step] = value[:, at : at + step]
                index, at, left = index + step, at + step, left - step

    def clear(self, image):
        shape = self.shape
        for block in range(self.width // shape.lanes):
            begin = block * shape.lanes + shape.blk
            end = (block + 1) * shape.lanes
            image[:, :, begin:end] = jnp.zeros((image.shape[0], image.shape[1], end - begin), BF16)


def fine_columns(store, row, even, odd):
    half = even.shape[0]
    store(row, 0, half, 0, shifted(odd, 1))
    store(row, 0, half, 1, even)
    store(row, 0, half, 2, odd)
    store(row, half, half, 0, even)
    store(row, half, half, 1, odd)
    store(row, half, half, 2, shifted(even, -1))


def run_conv(weights, buffer, image, acc, copies, rows, width):
    for dy in range(3):
        for copy in copies[dy]:
            copy.wait()
        left = image[dy : dy + rows].reshape(rows * width, weights.width)
        made = weights.product(left, buffer, dy)
        if dy == 0:
            acc[...] = made
        else:
            acc[...] += made


def scratch_of(weights, image_rows, out_rows, width, extra=()):
    return [
        pltpu.VMEM((3, weights.c_out // weights.shape.cols_of, weights.shape.cols_of, weights.width), BF16),
        pltpu.VMEM((image_rows, width, weights.width), BF16),
        pltpu.VMEM((out_rows * width, weights.c_out), F32),
        pltpu.SemaphoreType.DMA((3, 16)),
    ] + list(extra)


def call(body, n_smem, n_vmem, n_any, outs, scratch, flops, limit=60 * 1024 * 1024):
    specs = (
        [pl.BlockSpec(memory_space=pltpu.SMEM)] * n_smem
        + [pl.BlockSpec(memory_space=pltpu.VMEM)] * n_vmem
        + [pl.BlockSpec(memory_space=pltpu.HBM)] * n_any
    )
    return pl.pallas_call(
        body,
        out_shape=[jax.ShapeDtypeStruct(s, d) for s, d in outs],
        in_specs=specs,
        out_specs=[pl.BlockSpec(memory_space=pltpu.VMEM)] * len(outs),
        scratch_shapes=scratch,
        compiler_params=pltpu.CompilerParams(vmem_limit_bytes=limit),
        cost_estimate=pl.CostEstimate(flops=flops, bytes_accessed=4_000_000, transcendentals=0),
    )


def message_outs(rows, width, channels, keep):
    return [
        ((rows * width + TAIL, channels), BF16),
        ((keep * width + TAIL, channels), BF16),
        ((keep * width, channels), BF16),
        ((8, channels), F32),
    ]


def prepare(shape, flags, x, keep):
    rows, width, c = shape.rows, shape.cols, shape.narrow

    def body(flags, x_ref, out_ref, outer_ref, inner_ref, stats_ref):
        out_ref[0 : rows * width, :] = x_ref[...]
        sums = moments_of(x_ref[...].astype(F32))
        emit(flags, out_ref, outer_ref, inner_ref, stats_ref, keep, rows, width, sums)

    return call(body, 1, 1, 0, message_outs(rows, width, c, keep), [], 1000)(flags, x)


def fine_conv(shape, flags, weights, pieces, got, halo, out_halo, keep, residual=None):
    rows, width, half, c = shape.rows, shape.cols, shape.half, shape.narrow
    out_rows = rows + 2 * out_halo
    image_rows = out_rows + 2
    n_pieces = len(pieces)
    extra = 0 if residual is None else 3

    def body(flags, block, outer, inner, sa, sb, *rest):
        res = rest[:extra]
        piece_refs = rest[extra : extra + n_pieces]
        rest = rest[extra + n_pieces :]
        outs = rest[:-4]
        buffer, image, acc, sems = rest[-4:]
        copies = weights.copies(flags, weights.stacks(piece_refs), buffer, sems)
        for mine in copies:
            for copy in mine:
                copy.start()
        weights.clear(image)
        mean, inv = group_terms(sa[...] + sb[...], shape.fine_count)
        mix = parity_matrix(c)

        def store(row, place, size, tap, value):
            weights.put(image, row, place, tap, value.astype(BF16))

        for row in range(image_rows):
            value, outside = ext_row(row + halo - out_halo - 1, block, outer, inner, flags, rows, halo, width)
            value = masked(silu((value - mean) * inv), outside).astype(BF16)
            value = jnp.dot(value, mix, preferred_element_type=F32)
            fine_columns(store, row, value[:half], value[half:])
        run_conv(weights, buffer, image, acc, copies, out_rows, width)
        scale = 1.0 / math.sqrt(9 * c)
        if residual is None:
            out_ref, outer_ref, inner_ref, stats_ref = outs
            value = (acc[...] * scale).astype(BF16)
            out_ref[0 : rows * width, :] = value
            emit(flags, out_ref, outer_ref, inner_ref, stats_ref, keep, rows, width, moments_of(value.astype(F32)))
        else:
            (out_ref,) = outs
            for row in range(out_rows):
                own, _ = ext_row(row, res[0], res[1], res[2], flags, rows, out_halo, width)
                span = slice(row * width, (row + 1) * width)
                out_ref[span, :] = (own + acc[span, :] * scale).astype(BF16)

    outs = message_outs(rows, width, c, keep) if residual is None else [((out_rows * width, c), BF16)]
    args = (flags,) + tuple(got) + (() if residual is None else tuple(residual)) + tuple(pieces)
    flops = 2 * out_rows * width * 9 * c * c
    return call(body, 1, 5 + extra, n_pieces, outs, scratch_of(weights, image_rows, out_rows, width), flops)(*args)


def down_conv(shape, flags, weights, pieces, skip, keep):
    rows, width, half, c = shape.rows, shape.cols, shape.half, shape.narrow
    out_rows = rows // 2

    def body(flags, skip_ref, *rest):
        piece_refs = rest[: len(pieces)]
        outs = rest[len(pieces) : -4]
        buffer, image, acc, sems = rest[-4:]
        copies = weights.copies(flags, weights.stacks(piece_refs), buffer, sems)
        for mine in copies:
            for copy in mine:
                copy.start()
        weights.clear(image)
        for row in range(rows + 1):
            value = skip_ref[row * width : (row + 1) * width, :].astype(F32)
            if row == 0:
                value = masked(value, flags[1] != 0)
            even, odd = value[:half], value[half:]
            place = (row % 2) * (out_rows + 1) + row // 2
            weights.put(image, place, 0, 0, shifted(odd, 1).astype(BF16))
            weights.put(image, place, 0, 1, even.astype(BF16))
            weights.put(image, place, 0, 2, odd.astype(BF16))
        for dy in range(3):
            for copy in copies[dy]:
                copy.wait()
            begin = (0, out_rows + 1, 1)[dy]
            left = image[begin : begin + out_rows].reshape(out_rows * half, weights.width)
            made = weights.product(left, buffer, dy)
            if dy == 0:
                acc[...] = made
            else:
                acc[...] += made
        out_ref, outer_ref, inner_ref, stats_ref = outs
        value = (acc[...] * (1.0 / math.sqrt(9 * c))).astype(BF16)
        out_ref[0 : out_rows * half, :] = value
        emit(flags, out_ref, outer_ref, inner_ref, stats_ref, keep, out_rows, half, moments_of(value.astype(F32)))

    scratch = scratch_of(weights, 2 * (out_rows + 1), out_rows, half)
    outs = message_outs(out_rows, half, shape.wide, keep)
    return call(body, 1, 1, len(pieces), outs, scratch, 2 * out_rows * half * 9 * c * shape.wide)(flags, skip, *pieces)


def coarse_conv(shape, flags, weights, pieces, got, keep, residual=None):
    rows, width, c = shape.rows // 2, shape.half, shape.wide
    extra = 0 if residual is None else 1

    def body(flags, block, outer, inner, sa, sb, *rest):
        res = rest[:extra]
        piece_refs = rest[extra : extra + len(pieces)]
        outs = rest[extra + len(pieces) : -4]
        buffer, image, acc, sems = rest[-4:]
        copies = weights.copies(flags, weights.stacks(piece_refs), buffer, sems)
        for mine in copies:
            for copy in mine:
                copy.start()
        weights.clear(image)
        mean, inv = group_terms(sa[...] + sb[...], shape.coarse_count)
        for row in range(rows + 2):
            value, outside = ext_row(row, block, outer, inner, flags, rows, 1, width)
            value = masked(silu((value - mean) * inv), outside)
            weights.put(image, row, 0, 0, shifted(value, 1).astype(BF16))
            weights.put(image, row, 0, 1, value.astype(BF16))
            weights.put(image, row, 0, 2, shifted(value, -1).astype(BF16))
        run_conv(weights, buffer, image, acc, copies, rows, width)
        out_ref, outer_ref, inner_ref, stats_ref = outs
        value = acc[...] * (1.0 / math.sqrt(9 * c))
        if residual is not None:
            value = res[0][0 : rows * width, :].astype(F32) + value
        value = value.astype(BF16)
        out_ref[0 : rows * width, :] = value
        emit(flags, out_ref, outer_ref, inner_ref, stats_ref, keep, rows, width, moments_of(value.astype(F32)))

    args = (flags,) + tuple(got) + (() if residual is None else (residual,)) + tuple(pieces)
    outs = message_outs(rows, width, c, keep)
    flops = 2 * rows * width * 9 * c * c
    return call(body, 1, 5 + extra, len(pieces), outs, scratch_of(weights, rows + 2, rows, width), flops)(*args)


def up_conv(shape, flags, weights, pieces, got, skip, keep):
    rows, width, half = shape.rows, shape.cols, shape.half
    c, c_out = shape.wide, shape.narrow

    def body(flags, block, outer, inner, skip_ref, *rest):
        piece_refs = rest[: len(pieces)]
        outs = rest[len(pieces) : -4]
        buffer, image, acc, sems = rest[-4:]
        copies = weights.copies(flags, weights.stacks(piece_refs), buffer, sems)
        for mine in copies:
            for copy in mine:
                copy.start()
        weights.clear(image)
        mix = parity_matrix(c)
        for row in range(rows // 2 + 2):
            value, outside = ext_row(row, block, outer, inner, flags, rows // 2, 1, half)
            value = masked(value, outside).astype(BF16)
            value = jnp.dot(value, mix, preferred_element_type=F32)
            before, after = shifted(value, 1).astype(BF16), shifted(value, -1).astype(BF16)
            value = value.astype(BF16)
            for fine in (2 * row - 1, 2 * row):
                if 0 <= fine < rows + 2:
                    for tap, (even, odd) in enumerate(((before, value), (value, value), (value, after))):
                        weights.put(image, fine, 0, tap, even)
                        weights.put(image, fine, half, tap, odd)
        run_conv(weights, buffer, image, acc, copies, rows, width)
        out_ref, outer_ref, inner_ref, stats_ref, skip_stats_ref = outs
        value = (acc[...] * (1.0 / math.sqrt(9 * c))).astype(BF16)
        out_ref[0 : rows * width, :] = value
        emit(flags, out_ref, outer_ref, inner_ref, stats_ref, keep, rows, width, moments_of(value.astype(F32)))
        own = skip_ref[width : (rows + 1) * width, :].astype(F32)
        skip_stats_ref[...] = row_stack(moments_of(own), 8, c_out)

    outs = message_outs(rows, width, c_out, keep) + [((8, c_out), F32)]
    flops = 2 * rows * width * 9 * c * c_out
    scratch = scratch_of(weights, rows + 2, rows, width)
    return call(body, 1, 4, len(pieces), outs, scratch, flops)(flags, *got, skip, *pieces)


def join_conv(shape, flags, weights, pieces, got, skip, skip_sums, keep):
    rows, width, half, c = shape.rows, shape.cols, shape.half, shape.narrow

    def body(flags, block, outer, inner, sa, sb, skip_ref, skip_sum, *rest):
        piece_refs = rest[: len(pieces)]
        outs = rest[len(pieces) : -4]
        buffer, image, acc, sems = rest[-4:]
        copies = weights.copies(flags, weights.stacks(piece_refs), buffer, sems)
        for mine in copies:
            for copy in mine:
                copy.start()
        weights.clear(image)
        mix = parity_matrix(c)
        for part in range(2):
            sums = sa[...] + sb[...] if part == 0 else skip_sum[...]
            mean, inv = pair_terms(sums, shape.fine_count)

            def store(row, place, size, tap, value, part=part):
                weights.put(image, row, place, tap, value.astype(BF16), first=part * c)

            for row in range(rows + 2):
                if part == 0:
                    value, outside = ext_row(row, block, outer, inner, flags, rows, 1, width)
                else:
                    value = skip_ref[row * width : (row + 1) * width, :].astype(F32)
                    outside = flags[1] != 0 if row == 0 else flags[2] != 0 if row == rows + 1 else None
                value = masked(silu((value - mean) * inv), outside).astype(BF16)
                value = jnp.dot(value, mix, preferred_element_type=F32)
                fine_columns(store, row, value[:half], value[half:])
        run_conv(weights, buffer, image, acc, copies, rows, width)
        out_ref, outer_ref, inner_ref, stats_ref = outs
        value = (acc[...] * (1.0 / math.sqrt(18 * c))).astype(BF16)
        out_ref[0 : rows * width, :] = value
        emit(flags, out_ref, outer_ref, inner_ref, stats_ref, keep, rows, width, moments_of(value.astype(F32)))

    outs = message_outs(rows, width, c, keep)
    flops = 2 * rows * width * 18 * c * c
    scratch = scratch_of(weights, rows + 2, rows, width)
    return call(body, 1, 7, len(pieces), outs, scratch, flops)(flags, *got, skip, skip_sums, *pieces)


def pair_terms(sums, count):
    width = sums.shape[1]
    size = 2 * width // GROUPS
    terms = row_stack(bf16_terms(sums[0:1]) + bf16_terms(sums[1:2]), 16, width).astype(BF16)
    left = lax.broadcasted_iota(jnp.int32, (width, width), 0) // size
    right = lax.broadcasted_iota(jnp.int32, (width, width), 1) // size
    together = jnp.where(left == right, 1.0, 0.0).astype(BF16)
    summed = jnp.dot(terms, together, preferred_element_type=F32) * (1.0 / (count * size))
    mean = summed[0:1] + summed[1:2] + summed[2:3]
    square = summed[3:4] + summed[4:5] + summed[5:6]
    variance = jnp.maximum(square - mean * mean, 0.0)
    return mean, lax.rsqrt(variance + EPSILON)


def last_conv(shape, flags, weights, pieces, got, u, skip, j_start, n_quarters):
    rows, width, half, c = shape.rows, shape.cols, shape.half, shape.narrow
    quarter = half // n_quarters
    j_block = j_start // shape.blk

    def body(flags, block, outer, inner, sa, sb, u_ref, skip_ref, *rest):
        piece_refs = rest[: len(pieces)]
        outs = rest[len(pieces) : -6]
        buffer, image, acc, sems, jbuf, jsem = rest[-6:]
        copies = weights.copies(flags, weights.stacks(piece_refs), buffer, sems)
        for mine in copies:
            for copy in mine:
                copy.start()
        weights.clear(image)
        jcopies = []
        for low, high, owners in weights.bounds:
            if low <= j_block < high:
                for ref, owner in zip(weights.stacks(piece_refs)[low], owners, strict=True):
                    for j in range(ref.shape[0]):
                        copy = pltpu.make_async_copy(
                            ref.at[j, :, (j_block - low) * shape.lanes : (j_block - low + 1) * shape.lanes],
                            jbuf.at[owner(flags, j)],
                            jsem.at[len(jcopies)],
                        )
                        copy.start()
                        jcopies.append(copy)
        mean, inv = group_terms(sa[...] + sb[...], shape.fine_count)
        mix = parity_matrix(c)

        def store(row, place, size, tap, value):
            weights.put(image, row, place, tap, value.astype(BF16))

        for row in range(rows + 2):
            value, outside = ext_row(row, block, outer, inner, flags, rows, 1, width)
            value = masked(silu((value - mean) * inv), outside).astype(BF16)
            value = jnp.dot(value, mix, preferred_element_type=F32)
            fine_columns(store, row, value[:half], value[half:])
        run_conv(weights, buffer, image, acc, copies, rows, width)
        for copy in jcopies:
            copy.wait()
        right = jbuf[...].reshape(2 * c, shape.lanes)
        left = [u_ref[0 : rows * width, :], skip_ref[width : (rows + 1) * width, :]]
        left = [jnp.dot(part, mix, preferred_element_type=F32).astype(BF16) for part in left]
        made = jnp.zeros((rows * width, c), F32)
        for odd in range(2):
            mine = jnp.concatenate(
                [part[:, odd * (c // 2) : (odd + 1) * (c // 2)] for part in left]
                + [jnp.zeros((rows * width, shape.lanes - c), BF16)],
                axis=1,
            )
            made += lax.dot_general(
                mine, right[odd * c : (odd + 1) * c], (((1,), (1,)), ((), ())), preferred_element_type=F32
            )
        value = made * (1.0 / math.sqrt(2 * c)) + acc[...] * (1.0 / math.sqrt(9 * c))
        value = value.reshape(2 * rows, half, c).astype(BF16)
        for q, out in enumerate(outs):
            out[...] = value[:, q * quarter : (q + 1) * quarter, :]

    outs = [((2 * rows, quarter, c), BF16)] * n_quarters
    flops = 2 * rows * width * 11 * c * c
    extra = [pltpu.VMEM((shape.m, shape.cols_of, shape.lanes), BF16), pltpu.SemaphoreType.DMA((8,))]
    scratch = scratch_of(weights, rows + 2, rows, width, extra)
    return call(body, 1, 7, len(pieces), outs, scratch, flops)(flags, *got, u, skip, *pieces)


def pack_blocks(shape, pack, low, high):
    count, columns = high - low, pack.shape[0]
    first = low * shape.blk // 128 * 128
    last = min(-(-high * shape.blk // 128) * 128, pack.shape[1])

    def body(pack_ref, out_ref, rows, sem):
        copy = pltpu.make_async_copy(pack_ref.at[:, first:last], rows, sem)
        copy.start()
        copy.wait()
        for block in range(count):
            begin, end = block * shape.lanes, (block + 1) * shape.lanes
            at = (low + block) * shape.blk - first
            out_ref[:, begin : begin + shape.blk] = rows[:, at : at + shape.blk]
            out_ref[:, begin + shape.blk : end] = jnp.zeros((columns, shape.lanes - shape.blk), BF16)

    scratch = [pltpu.VMEM((columns, last - first), BF16), pltpu.SemaphoreType.DMA(())]
    outs = [((columns, count * shape.lanes), BF16)]
    return call(body, 0, 0, 1, outs, scratch, 1000)(pack)[0]


def shards(n, n_section, features, section_packs):
    section_id = lax.axis_index("section")
    w = lax.axis_index("space")
    shape = Shape(features, n)
    q_rows = shape.narrow * shape.narrow // shape.wide
    pack = section_packs[0]
    flags = jnp.stack([w % 2, (w == 0).astype(jnp.int32), (w == n - 1).astype(jnp.int32), section_id, w]).astype(jnp.int32)

    total = pack.shape[0] // shape.blk
    cuts = [0, 9 * q_rows // shape.blk, 18 * q_rows // shape.blk, 36 * q_rows // shape.blk, total]
    bounds = list(zip(cuts[:-1], cuts[1:], strict=True))

    def permute(value, source, target, move):
        if source == target:
            return within(value, range(n_section), move)
        pairs = [(source * n + i, target * n + move(i)) for i in range(n)]
        return lax.ppermute(value, ("section", "space"), pairs)

    def within(value, planes, move):
        pairs = [(s * n + i, s * n + move(i)) for s in planes for i in range(n)]
        return lax.ppermute(value, ("section", "space"), pairs)

    def to_outer(i):
        return (i + 1) % n if i % 2 else (i - 1) % n

    def ahead(i):
        return (i - 2) % n if i % 2 else (i + 2) % n

    def across(i):
        return (i + 4) % n

    def partner(i):
        return i ^ 1

    def sums_of(tail):
        tail = tail.astype(F32)
        first = tail[0:1] + tail[1:2] + tail[2:3]
        second = tail[3:4] + tail[4:5] + tail[5:6]
        return jnp.concatenate([first, second, jnp.zeros((6, tail.shape[1]), F32)], 0)

    def exchange(made, source, target, extra_stats=None, with_stats=True):
        block, outer, inner, stats = made
        if source != target:
            block = permute(block, source, target, lambda i: i)
            stats = None
        outer = permute(outer, source, target, to_outer)
        inner = permute(inner, source, target, partner)
        if not with_stats:
            return block, outer, inner
        own = made[3] if stats is not None else sums_of(block[-TAIL:])
        size = own.shape[1]
        sent = made[3] if extra_stats is None else jnp.concatenate([made[3], extra_stats], 1)
        if n == 8:
            b = permute(sent, source, target, ahead)
            c = permute(sent, source, target, across)
            if extra_stats is None:
                near = sums_of(outer[-TAIL:])
            else:
                own = sent
                near = permute(sent, source, target, to_outer)
            mine = own + near + b + c
            other = permute(mine, target, target, partner)
        else:
            mine = lax.psum(sent if stats is not None else own, "space")
            other = jnp.zeros_like(mine)
        if extra_stats is None:
            return block, outer, inner, mine, other
        total = mine[:, size:] + other[:, size:]
        return (block, outer, inner, mine[:, :size], other[:, :size]), total

    def owner_near(flags, j):
        return ((flags[4] // 2) ^ j) * 2 + flags[0]

    def owner_far(flags, j):
        return ((flags[4] // 2) ^ j) * 2 + 1 - flags[0]

    def after(value, *deps):
        return lax.optimization_barrier((value,) + deps)[0]

    pieces = {}

    def send(number, *deps):
        low, high = bounds[number]
        if n == 8:
            planes = range(n_section)
            own = after(pack_blocks(shape, pack.T, low, high), *deps)
            got = [own]
            for k in range(1, 4):
                got.append(within(own, planes, lambda i, k=k: i ^ (2 * k)))
            return got
        got = lax.all_gather(pack[low * shape.blk : high * shape.blk], "space")
        got = got.reshape(shape.m, n // shape.m, high - low, shape.blk, -1).transpose(0, 1, 4, 2, 3)
        got = got.reshape(shape.m, shape.cols_of, high - low, shape.blk)
        got = jnp.pad(got, ((0, 0), (0, 0), (0, 0), (0, shape.lanes - shape.blk)))
        return [got.reshape(shape.m, shape.cols_of, -1)]

    def finish(number, got, *deps):
        if n == 8:
            near = jnp.stack(after(got, *deps))
            far = within(near, range(n_section), partner)
            pieces[number] = ([near, far], [owner_near, owner_far])
        else:
            pieces[number] = (got, [lambda flags, j: j])

    def weights(start, c_in, c_out):
        first = start // shape.blk
        end = (start + 9 * c_in * c_out // shape.wide) // shape.blk
        used = [i for i, (a, b) in enumerate(bounds) if a < end and b > first]
        made = Weights(shape, [bounds[i] + (pieces[i][1],) for i in used], start, c_in, c_out)
        return made, [stack for i in used for stack in pieces[i][0]]

    narrow, wide = shape.narrow, shape.wide
    x = features[0].reshape(shape.rows, shape.half, 2, narrow).transpose(0, 2, 1, 3).reshape(-1, narrow)
    sent = send(0)
    first = exchange(prepare(shape, flags, after(x, sent[0]), 1), 0, 0)
    finish(0, sent, first[3])
    sent = send(1, sent, first)
    first = (after(first[0], sent[0]),) + first[1:]
    hidden = fine_conv(shape, flags, *weights(0, narrow, narrow), first, 1, 0, 2)
    second = exchange(hidden, 0, 0)
    finish(1, sent, second[3])
    sent = send(2, sent, second)
    second = (after(second[0], sent[0]),) + second[1:]
    (skip,) = fine_conv(shape, flags, *weights(9 * q_rows, narrow, narrow), second, 2, 1, 0, residual=first[:3])
    finish(2, sent, skip)
    sent = send(3, sent)
    skip = after(skip, sent[0])
    coarse = down_conv(shape, flags, *weights(18 * q_rows, narrow, wide), skip, 1)
    for section in (1, 2):
        got = exchange(coarse, section - 1, section)
        if section == 1:
            skip, got = lax.optimization_barrier((skip, got))
            last = n_section - 1
            pairs = [(s * n + i, (last - s if s in (0, last) else s) * n + i) for s in range(n_section) for i in range(n)]
            skip = lax.ppermute(skip, ("section", "space"), pairs)
        hidden = coarse_conv(shape, flags, *weights(0, wide, wide), got, 1)
        if section == 1:
            finish(3, sent, hidden[3])
            hidden, skip = lax.optimization_barrier((hidden, skip))
        then = exchange(hidden, section, section)
        coarse = coarse_conv(shape, flags, *weights(36 * q_rows, wide, wide), then, 1, residual=got[0])
    got = exchange(coarse, 2, 3, with_stats=False)
    *up, skip_stats = up_conv(shape, flags, *weights(0, wide, narrow), got, skip, 1)
    got, skip_sums = exchange(up, 3, 3, extra_stats=skip_stats)
    hidden = join_conv(shape, flags, *weights(18 * q_rows, wide, narrow), got, skip, skip_sums, 1)
    then = exchange(hidden, 3, 3)
    outs = last_conv(shape, flags, *weights(36 * q_rows, narrow, narrow), then, got[0], skip, 45 * q_rows, n_section)
    result = jnp.where(section_id == 3, outs[3], jnp.zeros_like(outs[3]))
    for target in range(3):
        result = result + permute(outs[target], 3, target, lambda i: i)
    quarter = shape.half // n_section
    result = result.reshape(shape.rows, 2, quarter, narrow).transpose(0, 2, 1, 3)
    return result.reshape(1, shape.rows, 2 * quarter, narrow)


def solution(mesh):
    n, n_section = mesh.shape["space"], mesh.shape["section"]

    def body(features, section_packs):
        return shards(n, n_section, features, section_packs)

    return jax.shard_map(
        body,
        mesh=mesh,
        in_specs=(P(None, "space", None, None), P("section", None, "space")),
        out_specs=P(None, "space", "section", None),
        check_vma=False,
    )
```

```python
import math

import jax
import jax.numpy as jnp
from jax import lax
from jax.experimental import pallas as pl
from jax.experimental.pallas import tpu as pltpu
from jax.sharding import PartitionSpec as P


GROUPS = 32
EPSILON = 1e-05
TAIL = 16
BF16 = jnp.bfloat16
F32 = jnp.float32


def row_stack(rows, count, width):
    ids = lax.broadcasted_iota(jnp.int32, (count, width), 0)
    total = jnp.zeros((count, width), F32)
    for place, row in enumerate(rows):
        total = jnp.where(ids == place, row, total)
    return total


def bf16_terms(row):
    high = row.astype(BF16).astype(F32)
    rest = row - high
    mid = rest.astype(BF16).astype(F32)
    return [high, mid, (rest - mid).astype(BF16).astype(F32)]


def moments_of(value):
    return [
        jnp.sum(value, axis=0, keepdims=True),
        jnp.sum(value * value, axis=0, keepdims=True),
    ]


def group_terms(sums, count):
    width = sums.shape[1]
    size = width // GROUPS
    terms = row_stack(bf16_terms(sums[0:1]) + bf16_terms(sums[1:2]), 16, width).astype(BF16)
    left = lax.broadcasted_iota(jnp.int32, (width, width), 0) // size
    right = lax.broadcasted_iota(jnp.int32, (width, width), 1) // size
    together = jnp.where(left == right, 1.0, 0.0).astype(BF16)
    summed = jnp.dot(terms, together, preferred_element_type=F32) * (1.0 / (count * size))
    mean = summed[0:1] + summed[1:2] + summed[2:3]
    square = summed[3:4] + summed[4:5] + summed[5:6]
    variance = jnp.maximum(square - mean * mean, 0.0)
    return mean, lax.rsqrt(variance + EPSILON)


def silu(z):
    half = 0.5 * z
    return half + half * jnp.tanh(half)


def parity_matrix(width):
    source = lax.broadcasted_iota(jnp.int32, (width, width), 0)
    target = lax.broadcasted_iota(jnp.int32, (width, width), 1)
    half = width // 2
    wanted = jnp.where(target < half, 2 * target, 2 * (target - half) + 1)
    return jnp.where(source == wanted, 1.0, 0.0).astype(BF16)


def shifted(value, step):
    rows = value.shape[0]
    ids = lax.broadcasted_iota(jnp.int32, value.shape, 0)
    if step == 1:
        return jnp.where(ids == 0, 0.0, pltpu.roll(value, 1, 0))
    return jnp.where(ids == rows - 1, 0.0, pltpu.roll(value, rows - 1, 0))


class Shape:
    def __init__(self, features, n):
        self.rows = features.shape[1]
        self.cols = features.shape[2]
        self.half = self.cols // 2
        self.narrow = features.shape[3]
        self.wide = 2 * self.narrow
        self.m = min(n, 8)
        self.cols_of = self.wide // self.m
        self.blk = 3 * self.narrow // 2
        self.lanes = -(-self.blk // 128) * 128
        self.fine_count = self.rows * n * self.cols
        self.coarse_count = self.fine_count // 4


def emit(flags, out_ref, outer_ref, inner_ref, stats_ref, keep, rows, width, sums):
    channels = out_ref.shape[1]
    core0 = flags[0] == 0
    tail = row_stack([term for row in sums for term in bf16_terms(row)], TAIL, channels).astype(BF16)
    out_ref[rows * width :, :] = tail
    stats_ref[...] = row_stack(sums, 8, channels)
    size = keep * width
    first = out_ref[0:size, :].astype(F32)
    last = out_ref[(rows - keep) * width : rows * width, :].astype(F32)
    outer_ref[0:size, :] = jnp.where(core0, first, last).astype(BF16)
    outer_ref[size:, :] = tail
    inner_ref[...] = jnp.where(core0, last, first).astype(BF16)


def ext_row(index, block_ref, outer_ref, inner_ref, flags, rows, halo, width):
    if index < halo:
        span = slice(index * width, (index + 1) * width)
        pick = jnp.where(flags[0] == 0, outer_ref[span, :].astype(F32), inner_ref[span, :].astype(F32))
        return pick, flags[1] != 0
    index -= halo
    if index < rows:
        return block_ref[index * width : (index + 1) * width, :].astype(F32), None
    index -= rows
    span = slice(index * width, (index + 1) * width)
    pick = jnp.where(flags[0] == 0, inner_ref[span, :].astype(F32), outer_ref[span, :].astype(F32))
    return pick, flags[2] != 0


def masked(value, outside):
    if outside is None:
        return value
    return jnp.where(outside, 0.0, value)


class Weights:
    def __init__(self, shape, bounds, start, c_in, c_out):
        self.shape = shape
        self.c_in = c_in
        self.c_out = c_out
        self.split = c_out != shape.wide
        self.blocks = 3 * c_in * c_out // shape.wide // shape.blk
        self.start = start // shape.blk
        self.bounds = bounds
        self.depth = self.blocks * shape.lanes
        self.width = (2 if self.split else 1) * self.depth

    def stacks(self, refs):
        refs = list(refs)
        return {low: [refs.pop(0) for _ in owners] for low, _, owners in self.bounds}

    def copies(self, flags, stack_refs, buffer, sems):
        made = []
        lanes = self.shape.lanes
        for dy in range(3):
            mine = []
            begin = self.start + dy * self.blocks
            for low, high, owners in self.bounds:
                a, b = max(begin, low), min(begin + self.blocks, high)
                if a >= b:
                    continue
                for ref, owner in zip(stack_refs[low], owners, strict=True):
                    for j in range(ref.shape[0]):
                        mine.append(
                            pltpu.make_async_copy(
                                ref.at[j, :, (a - low) * lanes : (b - low) * lanes],
                                self.slot(buffer.at[dy], owner(flags, j), a - begin, b - begin),
                                sems.at[dy, len(mine)],
                            )
                        )
            made.append(mine)
        return made

    def slot(self, target, owner, first, last):
        lanes = self.shape.lanes
        if not self.split:
            return target.at[owner, :, first * lanes : last * lanes]
        half = self.shape.m // 2
        shift = pl.multiple_of(owner // half * self.depth, lanes)
        return target.at[owner % half, :, pl.ds(first * lanes + shift, (last - first) * lanes)]

    def product(self, left, buffer, dy):
        right = buffer[dy].reshape(self.c_out, self.width)
        return lax.dot_general(left, right, (((1,), (1,)), ((), ())), preferred_element_type=F32)

    def put(self, image, row, place, tap, value, first=0, channels=None):
        shape = self.shape
        size = value.shape[0]
        half = self.c_in // 2
        runs = []
        if self.split:
            c = value.shape[1] // 2
            runs = [(odd, tap * half + first // 2, odd * c, c) for odd in range(2)]
        else:
            runs = [(0, tap * self.c_in + first, 0, value.shape[1])]
        for odd, index, at, left in runs:
            while left > 0:
                step = min(left, shape.blk - index % shape.blk)
                lane = odd * self.depth + index // shape.blk * shape.lanes + index % shape.blk
                image[row, place : place + size, lane : lane + step] = value[:, at : at + step]
                index, at, left = index + step, at + step, left - step

    def clear(self, image):
        shape = self.shape
        for block in range(self.width // shape.lanes):
            begin = block * shape.lanes + shape.blk
            end = (block + 1) * shape.lanes
            image[:, :, begin:end] = jnp.zeros((image.shape[0], image.shape[1], end - begin), BF16)


def fine_columns(store, row, even, odd):
    half = even.shape[0]
    store(row, 0, half, 0, shifted(odd, 1))
    store(row, 0, half, 1, even)
    store(row, 0, half, 2, odd)
    store(row, half, half, 0, even)
    store(row, half, half, 1, odd)
    store(row, half, half, 2, shifted(even, -1))


def run_conv(weights, buffer, image, acc, copies, rows, width):
    for dy in range(3):
        for copy in copies[dy]:
            copy.wait()
        left = image[dy : dy + rows].reshape(rows * width, weights.width)
        made = weights.product(left, buffer, dy)
        if dy == 0:
            acc[...] = made
        else:
            acc[...] += made


def scratch_of(weights, image_rows, out_rows, width, extra=()):
    return [
        pltpu.VMEM((3, weights.c_out // weights.shape.cols_of, weights.shape.cols_of, weights.width), BF16),
        pltpu.VMEM((image_rows, width, weights.width), BF16),
        pltpu.VMEM((out_rows * width, weights.c_out), F32),
        pltpu.SemaphoreType.DMA((3, 16)),
    ] + list(extra)


def call(body, n_smem, n_vmem, n_any, outs, scratch, flops, limit=60 * 1024 * 1024):
    specs = (
        [pl.BlockSpec(memory_space=pltpu.SMEM)] * n_smem
        + [pl.BlockSpec(memory_space=pltpu.VMEM)] * n_vmem
        + [pl.BlockSpec(memory_space=pltpu.HBM)] * n_any
    )
    return pl.pallas_call(
        body,
        out_shape=[jax.ShapeDtypeStruct(s, d) for s, d in outs],
        in_specs=specs,
        out_specs=[pl.BlockSpec(memory_space=pltpu.VMEM)] * len(outs),
        scratch_shapes=scratch,
        compiler_params=pltpu.CompilerParams(vmem_limit_bytes=limit),
        cost_estimate=pl.CostEstimate(flops=flops, bytes_accessed=4_000_000, transcendentals=0),
    )


def message_outs(rows, width, channels, keep):
    return [
        ((rows * width + TAIL, channels), BF16),
        ((keep * width + TAIL, channels), BF16),
        ((keep * width, channels), BF16),
        ((8, channels), F32),
    ]


def prepare(shape, flags, x, keep):
    rows, width, c = shape.rows, shape.cols, shape.narrow

    def body(flags, x_ref, out_ref, outer_ref, inner_ref, stats_ref):
        out_ref[0 : rows * width, :] = x_ref[...]
        sums = moments_of(x_ref[...].astype(F32))
        emit(flags, out_ref, outer_ref, inner_ref, stats_ref, keep, rows, width, sums)

    return call(body, 1, 1, 0, message_outs(rows, width, c, keep), [], 1000)(flags, x)


def fine_conv(shape, flags, weights, pieces, got, halo, out_halo, keep, residual=None):
    rows, width, half, c = shape.rows, shape.cols, shape.half, shape.narrow
    out_rows = rows + 2 * out_halo
    image_rows = out_rows + 2
    n_pieces = len(pieces)
    extra = 0 if residual is None else 3

    def body(flags, block, outer, inner, sa, sb, *rest):
        res = rest[:extra]
        piece_refs = rest[extra : extra + n_pieces]
        rest = rest[extra + n_pieces :]
        outs = rest[:-4]
        buffer, image, acc, sems = rest[-4:]
        copies = weights.copies(flags, weights.stacks(piece_refs), buffer, sems)
        for mine in copies:
            for copy in mine:
                copy.start()
        weights.clear(image)
        mean, inv = group_terms(sa[...] + sb[...], shape.fine_count)
        mix = parity_matrix(c)

        def store(row, place, size, tap, value):
            weights.put(image, row, place, tap, value.astype(BF16))

        for row in range(image_rows):
            value, outside = ext_row(row + halo - out_halo - 1, block, outer, inner, flags, rows, halo, width)
            value = masked(silu((value - mean) * inv), outside).astype(BF16)
            value = jnp.dot(value, mix, preferred_element_type=F32)
            fine_columns(store, row, value[:half], value[half:])
        run_conv(weights, buffer, image, acc, copies, out_rows, width)
        scale = 1.0 / math.sqrt(9 * c)
        if residual is None:
            out_ref, outer_ref, inner_ref, stats_ref = outs
            value = (acc[...] * scale).astype(BF16)
            out_ref[0 : rows * width, :] = value
            emit(flags, out_ref, outer_ref, inner_ref, stats_ref, keep, rows, width, moments_of(value.astype(F32)))
        else:
            (out_ref,) = outs
            for row in range(out_rows):
                own, _ = ext_row(row, res[0], res[1], res[2], flags, rows, out_halo, width)
                span = slice(row * width, (row + 1) * width)
                out_ref[span, :] = (own + acc[span, :] * scale).astype(BF16)

    outs = message_outs(rows, width, c, keep) if residual is None else [((out_rows * width, c), BF16)]
    args = (flags,) + tuple(got) + (() if residual is None else tuple(residual)) + tuple(pieces)
    flops = 2 * out_rows * width * 9 * c * c
    return call(body, 1, 5 + extra, n_pieces, outs, scratch_of(weights, image_rows, out_rows, width), flops)(*args)


def down_conv(shape, flags, weights, pieces, skip, keep):
    rows, width, half, c = shape.rows, shape.cols, shape.half, shape.narrow
    out_rows = rows // 2

    def body(flags, skip_ref, *rest):
        piece_refs = rest[: len(pieces)]
        outs = rest[len(pieces) : -4]
        buffer, image, acc, sems = rest[-4:]
        copies = weights.copies(flags, weights.stacks(piece_refs), buffer, sems)
        for mine in copies:
            for copy in mine:
                copy.start()
        weights.clear(image)
        for row in range(rows + 1):
            value = skip_ref[row * width : (row + 1) * width, :].astype(F32)
            if row == 0:
                value = masked(value, flags[1] != 0)
            even, odd = value[:half], value[half:]
            place = (row % 2) * (out_rows + 1) + row // 2
            weights.put(image, place, 0, 0, shifted(odd, 1).astype(BF16))
            weights.put(image, place, 0, 1, even.astype(BF16))
            weights.put(image, place, 0, 2, odd.astype(BF16))
        for dy in range(3):
            for copy in copies[dy]:
                copy.wait()
            begin = (0, out_rows + 1, 1)[dy]
            left = image[begin : begin + out_rows].reshape(out_rows * half, weights.width)
            made = weights.product(left, buffer, dy)
            if dy == 0:
                acc[...] = made
            else:
                acc[...] += made
        out_ref, outer_ref, inner_ref, stats_ref = outs
        value = (acc[...] * (1.0 / math.sqrt(9 * c))).astype(BF16)
        out_ref[0 : out_rows * half, :] = value
        emit(flags, out_ref, outer_ref, inner_ref, stats_ref, keep, out_rows, half, moments_of(value.astype(F32)))

    scratch = scratch_of(weights, 2 * (out_rows + 1), out_rows, half)
    outs = message_outs(out_rows, half, shape.wide, keep)
    return call(body, 1, 1, len(pieces), outs, scratch, 2 * out_rows * half * 9 * c * shape.wide)(flags, skip, *pieces)


def coarse_conv(shape, flags, weights, pieces, got, keep, residual=None):
    rows, width, c = shape.rows // 2, shape.half, shape.wide
    extra = 0 if residual is None else 1

    def body(flags, block, outer, inner, sa, sb, *rest):
        res = rest[:extra]
        piece_refs = rest[extra : extra + len(pieces)]
        outs = rest[extra + len(pieces) : -4]
        buffer, image, acc, sems = rest[-4:]
        copies = weights.copies(flags, weights.stacks(piece_refs), buffer, sems)
        for mine in copies:
            for copy in mine:
                copy.start()
        weights.clear(image)
        mean, inv = group_terms(sa[...] + sb[...], shape.coarse_count)
        for row in range(rows + 2):
            value, outside = ext_row(row, block, outer, inner, flags, rows, 1, width)
            value = masked(silu((value - mean) * inv), outside)
            weights.put(image, row, 0, 0, shifted(value, 1).astype(BF16))
            weights.put(image, row, 0, 1, value.astype(BF16))
            weights.put(image, row, 0, 2, shifted(value, -1).astype(BF16))
        run_conv(weights, buffer, image, acc, copies, rows, width)
        out_ref, outer_ref, inner_ref, stats_ref = outs
        value = acc[...] * (1.0 / math.sqrt(9 * c))
        if residual is not None:
            value = res[0][0 : rows * width, :].astype(F32) + value
        value = value.astype(BF16)
        out_ref[0 : rows * width, :] = value
        emit(flags, out_ref, outer_ref, inner_ref, stats_ref, keep, rows, width, moments_of(value.astype(F32)))

    args = (flags,) + tuple(got) + (() if residual is None else (residual,)) + tuple(pieces)
    outs = message_outs(rows, width, c, keep)
    flops = 2 * rows * width * 9 * c * c
    return call(body, 1, 5 + extra, len(pieces), outs, scratch_of(weights, rows + 2, rows, width), flops)(*args)


def up_conv(shape, flags, weights, pieces, got, skip, keep):
    rows, width, half = shape.rows, shape.cols, shape.half
    c, c_out = shape.wide, shape.narrow

    def body(flags, block, outer, inner, skip_ref, *rest):
        piece_refs = rest[: len(pieces)]
        outs = rest[len(pieces) : -4]
        buffer, image, acc, sems = rest[-4:]
        copies = weights.copies(flags, weights.stacks(piece_refs), buffer, sems)
        for mine in copies:
            for copy in mine:
                copy.start()
        weights.clear(image)
        mix = parity_matrix(c)
        for row in range(rows // 2 + 2):
            value, outside = ext_row(row, block, outer, inner, flags, rows // 2, 1, half)
            value = masked(value, outside).astype(BF16)
            value = jnp.dot(value, mix, preferred_element_type=F32)
            before, after = shifted(value, 1).astype(BF16), shifted(value, -1).astype(BF16)
            value = value.astype(BF16)
            for fine in (2 * row - 1, 2 * row):
                if 0 <= fine < rows + 2:
                    for tap, (even, odd) in enumerate(((before, value), (value, value), (value, after))):
                        weights.put(image, fine, 0, tap, even)
                        weights.put(image, fine, half, tap, odd)
        run_conv(weights, buffer, image, acc, copies, rows, width)
        out_ref, outer_ref, inner_ref, stats_ref = outs
        value = (acc[...] * (1.0 / math.sqrt(9 * c))).astype(BF16)
        out_ref[0 : rows * width, :] = value
        own = skip_ref[width : (rows + 1) * width, :].astype(F32)
        sums = moments_of(value.astype(F32)) + moments_of(own)
        emit(flags, out_ref, outer_ref, inner_ref, stats_ref, keep, rows, width, sums)

    outs = message_outs(rows, width, c_out, keep)
    flops = 2 * rows * width * 9 * c * c_out
    scratch = scratch_of(weights, rows + 2, rows, width)
    return call(body, 1, 4, len(pieces), outs, scratch, flops)(flags, *got, skip, *pieces)


def join_conv(shape, flags, weights, pieces, got, skip, keep):
    rows, width, half, c = shape.rows, shape.cols, shape.half, shape.narrow

    def body(flags, block, outer, inner, sa, sb, skip_ref, *rest):
        piece_refs = rest[: len(pieces)]
        outs = rest[len(pieces) : -4]
        buffer, image, acc, sems = rest[-4:]
        copies = weights.copies(flags, weights.stacks(piece_refs), buffer, sems)
        for mine in copies:
            for copy in mine:
                copy.start()
        weights.clear(image)
        mix = parity_matrix(c)
        for part in range(2):
            sums = sa[...] + sb[...]
            mean, inv = pair_terms(sums[2 * part : 2 * part + 2], shape.fine_count)

            def store(row, place, size, tap, value, part=part):
                weights.put(image, row, place, tap, value.astype(BF16), first=part * c)

            for row in range(rows + 2):
                if part == 0:
                    value, outside = ext_row(row, block, outer, inner, flags, rows, 1, width)
                else:
                    value = skip_ref[row * width : (row + 1) * width, :].astype(F32)
                    outside = flags[1] != 0 if row == 0 else flags[2] != 0 if row == rows + 1 else None
                value = masked(silu((value - mean) * inv), outside).astype(BF16)
                value = jnp.dot(value, mix, preferred_element_type=F32)
                fine_columns(store, row, value[:half], value[half:])
        run_conv(weights, buffer, image, acc, copies, rows, width)
        out_ref, outer_ref, inner_ref, stats_ref = outs
        value = (acc[...] * (1.0 / math.sqrt(18 * c))).astype(BF16)
        out_ref[0 : rows * width, :] = value
        emit(flags, out_ref, outer_ref, inner_ref, stats_ref, keep, rows, width, moments_of(value.astype(F32)))

    outs = message_outs(rows, width, c, keep)
    flops = 2 * rows * width * 18 * c * c
    scratch = scratch_of(weights, rows + 2, rows, width)
    return call(body, 1, 6, len(pieces), outs, scratch, flops)(flags, *got, skip, *pieces)


def pair_terms(sums, count):
    width = sums.shape[1]
    size = 2 * width // GROUPS
    terms = row_stack(bf16_terms(sums[0:1]) + bf16_terms(sums[1:2]), 16, width).astype(BF16)
    left = lax.broadcasted_iota(jnp.int32, (width, width), 0) // size
    right = lax.broadcasted_iota(jnp.int32, (width, width), 1) // size
    together = jnp.where(left == right, 1.0, 0.0).astype(BF16)
    summed = jnp.dot(terms, together, preferred_element_type=F32) * (1.0 / (count * size))
    mean = summed[0:1] + summed[1:2] + summed[2:3]
    square = summed[3:4] + summed[4:5] + summed[5:6]
    variance = jnp.maximum(square - mean * mean, 0.0)
    return mean, lax.rsqrt(variance + EPSILON)


def last_conv(shape, flags, weights, pieces, got, u, skip, j_start, n_quarters):
    rows, width, half, c = shape.rows, shape.cols, shape.half, shape.narrow
    quarter = half // n_quarters
    j_block = j_start // shape.blk

    def body(flags, block, outer, inner, sa, sb, u_ref, skip_ref, *rest):
        piece_refs = rest[: len(pieces)]
        outs = rest[len(pieces) : -6]
        buffer, image, acc, sems, jbuf, jsem = rest[-6:]
        copies = weights.copies(flags, weights.stacks(piece_refs), buffer, sems)
        for mine in copies:
            for copy in mine:
                copy.start()
        weights.clear(image)
        jcopies = []
        for low, high, owners in weights.bounds:
            if low <= j_block < high:
                for ref, owner in zip(weights.stacks(piece_refs)[low], owners, strict=True):
                    for j in range(ref.shape[0]):
                        copy = pltpu.make_async_copy(
                            ref.at[j, :, (j_block - low) * shape.lanes : (j_block - low + 1) * shape.lanes],
                            jbuf.at[owner(flags, j)],
                            jsem.at[len(jcopies)],
                        )
                        copy.start()
                        jcopies.append(copy)
        mean, inv = group_terms(sa[...] + sb[...], shape.fine_count)
        mix = parity_matrix(c)

        def store(row, place, size, tap, value):
            weights.put(image, row, place, tap, value.astype(BF16))

        for row in range(rows + 2):
            value, outside = ext_row(row, block, outer, inner, flags, rows, 1, width)
            value = masked(silu((value - mean) * inv), outside).astype(BF16)
            value = jnp.dot(value, mix, preferred_element_type=F32)
            fine_columns(store, row, value[:half], value[half:])
        run_conv(weights, buffer, image, acc, copies, rows, width)
        for copy in jcopies:
            copy.wait()
        right = jbuf[...].reshape(2 * c, shape.lanes)
        left = [u_ref[0 : rows * width, :], skip_ref[width : (rows + 1) * width, :]]
        left = [jnp.dot(part, mix, preferred_element_type=F32).astype(BF16) for part in left]
        made = jnp.zeros((rows * width, c), F32)
        for odd in range(2):
            mine = jnp.concatenate(
                [part[:, odd * (c // 2) : (odd + 1) * (c // 2)] for part in left]
                + [jnp.zeros((rows * width, shape.lanes - c), BF16)],
                axis=1,
            )
            made += lax.dot_general(
                mine, right[odd * c : (odd + 1) * c], (((1,), (1,)), ((), ())), preferred_element_type=F32
            )
        value = made * (1.0 / math.sqrt(2 * c)) + acc[...] * (1.0 / math.sqrt(9 * c))
        value = value.reshape(2 * rows, half, c).astype(BF16)
        for q, out in enumerate(outs):
            out[...] = value[:, q * quarter : (q + 1) * quarter, :]

    outs = [((2 * rows, quarter, c), BF16)] * n_quarters
    flops = 2 * rows * width * 11 * c * c
    extra = [pltpu.VMEM((shape.m, shape.cols_of, shape.lanes), BF16), pltpu.SemaphoreType.DMA((8,))]
    scratch = scratch_of(weights, rows + 2, rows, width, extra)
    return call(body, 1, 7, len(pieces), outs, scratch, flops)(flags, *got, u, skip, *pieces)


def pack_blocks(shape, pack, bounds):
    columns = pack.shape[0]
    first = bounds[0][0] * shape.blk // 128 * 128
    last = min(-(-bounds[-1][1] * shape.blk // 128) * 128, pack.shape[1])

    def body(pack_ref, *rest):
        outs, (rows, sem) = rest[:-2], rest[-2:]
        copy = pltpu.make_async_copy(pack_ref.at[:, first:last], rows, sem)
        copy.start()
        copy.wait()
        for (low, high), out_ref in zip(bounds, outs, strict=True):
            for block in range(high - low):
                begin, end = block * shape.lanes, (block + 1) * shape.lanes
                at = (low + block) * shape.blk - first
                out_ref[:, begin : begin + shape.blk] = rows[:, at : at + shape.blk]
                out_ref[:, begin + shape.blk : end] = jnp.zeros((columns, shape.lanes - shape.blk), BF16)

    scratch = [pltpu.VMEM((columns, last - first), BF16), pltpu.SemaphoreType.DMA(())]
    outs = [((columns, (high - low) * shape.lanes), BF16) for low, high in bounds]
    return call(body, 0, 0, 1, outs, scratch, 1000)(pack)


def shards(n, n_section, features, section_packs):
    section_id = lax.axis_index("section")
    w = lax.axis_index("space")
    shape = Shape(features, n)
    q_rows = shape.narrow * shape.narrow // shape.wide
    pack = section_packs[0]
    flags = jnp.stack([w % 2, (w == 0).astype(jnp.int32), (w == n - 1).astype(jnp.int32), section_id, w]).astype(jnp.int32)

    total = pack.shape[0] // shape.blk
    cuts = [0, 9 * q_rows // shape.blk, 18 * q_rows // shape.blk, 36 * q_rows // shape.blk, total]
    bounds = list(zip(cuts[:-1], cuts[1:], strict=True))

    def permute(value, source, target, move):
        if source == target:
            return within(value, range(n_section), move)
        other = {source: target, target: source}
        pairs = [
            (s * n + i, other[s] * n + move(i) if s in other else s * n + i) for s in range(n_section) for i in range(n)
        ]
        return lax.ppermute(value, ("section", "space"), pairs)

    def within(value, planes, move):
        pairs = [(s * n + i, s * n + move(i)) for s in planes for i in range(n)]
        return lax.ppermute(value, ("section", "space"), pairs)

    def to_outer(i):
        return (i + 1) % n if i % 2 else (i - 1) % n

    def ahead(i):
        return (i - 2) % n if i % 2 else (i + 2) % n

    def across(i):
        return (i + 4) % n

    def partner(i):
        return i ^ 1

    def sums_of(tail):
        tail = tail[: TAIL // 4 * 3].astype(F32).reshape(-1, 3, tail.shape[1]).sum(1)
        return jnp.concatenate([tail, jnp.zeros((8 - tail.shape[0], tail.shape[1]), F32)], 0)

    def exchange(made, source, target, with_stats=True):
        block, outer, inner, stats = made
        if source != target:
            block = permute(block, source, target, lambda i: i)
            stats = None
        outer = permute(outer, source, target, to_outer)
        inner = permute(inner, source, target, partner)
        if not with_stats:
            return block, outer, inner
        own = made[3] if stats is not None else sums_of(block[-TAIL:])
        if n == 8:
            b = permute(made[3], source, target, ahead)
            c = permute(made[3], source, target, across)
            mine = own + sums_of(outer[-TAIL:]) + b + c
            other = permute(mine, target, target, partner)
        else:
            mine = lax.psum(own, "space")
            other = jnp.zeros_like(mine)
        return block, outer, inner, mine, other

    def owner_near(flags, j):
        return ((flags[4] // 2) ^ j) * 2 + flags[0]

    def owner_far(flags, j):
        return ((flags[4] // 2) ^ j) * 2 + 1 - flags[0]

    def after(value, *deps):
        return lax.optimization_barrier((value,) + deps)[0]

    pieces = {}
    packed = []
    if n == 8:
        packed = pack_blocks(shape, pack.T, bounds[:1])

    def send(number, *deps):
        low, high = bounds[number]
        if n == 8:
            planes = range(n_section)
            own = after(packed[number], *deps)
            got = [own]
            for k in range(1, 4):
                got.append(within(own, planes, lambda i, k=k: i ^ (2 * k)))
            return got
        got = lax.all_gather(pack[low * shape.blk : high * shape.blk], "space")
        got = got.reshape(shape.m, n // shape.m, high - low, shape.blk, -1).transpose(0, 1, 4, 2, 3)
        got = got.reshape(shape.m, shape.cols_of, high - low, shape.blk)
        got = jnp.pad(got, ((0, 0), (0, 0), (0, 0), (0, shape.lanes - shape.blk)))
        return [got.reshape(shape.m, shape.cols_of, -1)]

    def finish(number, got, *deps):
        if n == 8:
            near = jnp.stack(after(got, *deps))
            far = within(near, range(n_section), partner)
            pieces[number] = ([near, far], [owner_near, owner_far])
        else:
            pieces[number] = (got, [lambda flags, j: j])

    def weights(start, c_in, c_out):
        first = start // shape.blk
        end = (start + 9 * c_in * c_out // shape.wide) // shape.blk
        used = [i for i, (a, b) in enumerate(bounds) if a < end and b > first]
        made = Weights(shape, [bounds[i] + (pieces[i][1],) for i in used], start, c_in, c_out)
        return made, [stack for i in used for stack in pieces[i][0]]

    narrow, wide = shape.narrow, shape.wide
    x = features[0].reshape(shape.rows, shape.half, 2, narrow).transpose(0, 2, 1, 3).reshape(-1, narrow)
    ready = prepare(shape, flags, x, 1)
    sent = send(0, ready[3])
    if n == 8:
        packed += pack_blocks(shape, after(pack.T, sent[0]), bounds[1:])
    first = exchange(ready, 0, 0)
    finish(0, sent, first[3])
    sent = send(1, sent)
    first = (after(first[0], sent[0]),) + first[1:]
    hidden = fine_conv(shape, flags, *weights(0, narrow, narrow), first, 1, 0, 2)
    second = exchange(hidden, 0, 0)
    finish(1, sent, second[3])
    sent = send(2, sent, second[3])
    second = (after(second[0], sent[0]),) + second[1:]
    (skip,) = fine_conv(shape, flags, *weights(9 * q_rows, narrow, narrow), second, 2, 1, 0, residual=first[:3])
    finish(2, sent, skip)
    sent = send(3, sent)
    skip = after(skip, sent[0])
    coarse = down_conv(shape, flags, *weights(18 * q_rows, narrow, wide), skip, 1)
    for section in (1, 2):
        got = exchange(coarse, section - 1, section)
        if section == 1:
            skip, got = lax.optimization_barrier((skip, got))
            skip = permute(skip, 0, n_section - 1, lambda i: i)
        hidden = coarse_conv(shape, flags, *weights(0, wide, wide), got, 1)
        if section == 1:
            finish(3, sent, hidden[3])
            hidden, skip = lax.optimization_barrier((hidden, skip))
        then = exchange(hidden, section, section)
        coarse = coarse_conv(shape, flags, *weights(36 * q_rows, wide, wide), then, 1, residual=got[0])
    got = exchange(coarse, 2, 3, with_stats=False)
    up = up_conv(shape, flags, *weights(0, wide, narrow), got, skip, 1)
    got = exchange(up, 3, 3)
    hidden = join_conv(shape, flags, *weights(18 * q_rows, wide, narrow), got, skip, 1)
    then = exchange(hidden, 3, 3)
    outs = last_conv(shape, flags, *weights(36 * q_rows, narrow, narrow), then, got[0], skip, 45 * q_rows, n_section)
    result = outs[3]
    for target in range(3):
        result = jnp.where(section_id == target, permute(outs[target], 3, target, lambda i: i), result)
    quarter = shape.half // n_section
    result = result.reshape(shape.rows, 2, quarter, narrow).transpose(0, 2, 1, 3)
    return result.reshape(1, shape.rows, 2 * quarter, narrow)


def solution(mesh):
    n, n_section = mesh.shape["space"], mesh.shape["section"]

    def body(features, section_packs):
        return shards(n, n_section, features, section_packs)

    return jax.shard_map(
        body,
        mesh=mesh,
        in_specs=(P(None, "space", None, None), P("section", None, "space")),
        out_specs=P(None, "space", "section", None),
        check_vma=False,
    )
```

```python
import math

import jax
import jax.numpy as jnp
from jax import lax
from jax.experimental import pallas as pl
from jax.experimental.pallas import tpu as pltpu
from jax.sharding import PartitionSpec as P


GROUPS = 32
EPSILON = 1e-05
TAIL = 16
BF16 = jnp.bfloat16
F32 = jnp.float32


def row_stack(rows, count, width):
    ids = lax.broadcasted_iota(jnp.int32, (count, width), 0)
    total = jnp.zeros((count, width), F32)
    for place, row in enumerate(rows):
        total = jnp.where(ids == place, row, total)
    return total


def bf16_terms(row):
    high = row.astype(BF16).astype(F32)
    rest = row - high
    mid = rest.astype(BF16).astype(F32)
    return [high, mid, (rest - mid).astype(BF16).astype(F32)]


def moments_of(value):
    return [
        jnp.sum(value, axis=0, keepdims=True),
        jnp.sum(value * value, axis=0, keepdims=True),
    ]


def group_terms(sums, count):
    width = sums.shape[1]
    size = width // GROUPS
    terms = row_stack(bf16_terms(sums[0:1]) + bf16_terms(sums[1:2]), 16, width).astype(BF16)
    left = lax.broadcasted_iota(jnp.int32, (width, width), 0) // size
    right = lax.broadcasted_iota(jnp.int32, (width, width), 1) // size
    together = jnp.where(left == right, 1.0, 0.0).astype(BF16)
    summed = jnp.dot(terms, together, preferred_element_type=F32) * (1.0 / (count * size))
    mean = summed[0:1] + summed[1:2] + summed[2:3]
    square = summed[3:4] + summed[4:5] + summed[5:6]
    variance = jnp.maximum(square - mean * mean, 0.0)
    return mean, lax.rsqrt(variance + EPSILON)


def silu(z):
    half = 0.5 * z
    return half + half * jnp.tanh(half)


def parity_matrix(width):
    source = lax.broadcasted_iota(jnp.int32, (width, width), 0)
    target = lax.broadcasted_iota(jnp.int32, (width, width), 1)
    half = width // 2
    wanted = jnp.where(target < half, 2 * target, 2 * (target - half) + 1)
    return jnp.where(source == wanted, 1.0, 0.0).astype(BF16)


def shifted(value, step):
    rows = value.shape[0]
    ids = lax.broadcasted_iota(jnp.int32, value.shape, 0)
    if step == 1:
        return jnp.where(ids == 0, 0.0, pltpu.roll(value, 1, 0))
    return jnp.where(ids == rows - 1, 0.0, pltpu.roll(value, rows - 1, 0))


class Shape:
    def __init__(self, features, n):
        self.rows = features.shape[1]
        self.cols = features.shape[2]
        self.half = self.cols // 2
        self.narrow = features.shape[3]
        self.wide = 2 * self.narrow
        self.m = min(n, 8)
        self.cols_of = self.wide // self.m
        self.blk = 3 * self.narrow // 2
        self.lanes = -(-self.blk // 128) * 128
        self.fine_count = self.rows * n * self.cols
        self.coarse_count = self.fine_count // 4


def emit(flags, out_ref, outer_ref, inner_ref, stats_ref, keep, rows, width, sums):
    channels = out_ref.shape[1]
    core0 = flags[0] == 0
    tail = row_stack([term for row in sums for term in bf16_terms(row)], TAIL, channels).astype(BF16)
    out_ref[rows * width :, :] = tail
    stats_ref[...] = row_stack(sums, 8, channels)
    size = keep * width
    first = out_ref[0:size, :].astype(F32)
    last = out_ref[(rows - keep) * width : rows * width, :].astype(F32)
    outer_ref[0:size, :] = jnp.where(core0, first, last).astype(BF16)
    outer_ref[size:, :] = tail
    inner_ref[...] = jnp.where(core0, last, first).astype(BF16)


def ext_row(index, block_ref, outer_ref, inner_ref, flags, rows, halo, width):
    if index < halo:
        span = slice(index * width, (index + 1) * width)
        pick = jnp.where(flags[0] == 0, outer_ref[span, :].astype(F32), inner_ref[span, :].astype(F32))
        return pick, flags[1] != 0
    index -= halo
    if index < rows:
        return block_ref[index * width : (index + 1) * width, :].astype(F32), None
    index -= rows
    span = slice(index * width, (index + 1) * width)
    pick = jnp.where(flags[0] == 0, inner_ref[span, :].astype(F32), outer_ref[span, :].astype(F32))
    return pick, flags[2] != 0


def masked(value, outside):
    if outside is None:
        return value
    return jnp.where(outside, 0.0, value)


class Weights:
    def __init__(self, shape, bounds, start, c_in, c_out):
        self.shape = shape
        self.c_in = c_in
        self.c_out = c_out
        self.split = c_out != shape.wide
        self.blocks = 3 * c_in * c_out // shape.wide // shape.blk
        self.start = start // shape.blk
        self.bounds = bounds
        self.depth = self.blocks * shape.lanes
        self.width = (2 if self.split else 1) * self.depth

    def stacks(self, refs):
        refs = list(refs)
        return {low: [refs.pop(0) for _ in owners] for low, _, owners in self.bounds}

    def copies(self, flags, stack_refs, buffer, sems):
        made = []
        lanes = self.shape.lanes
        for dy in range(3):
            mine = []
            begin = self.start + dy * self.blocks
            for low, high, owners in self.bounds:
                a, b = max(begin, low), min(begin + self.blocks, high)
                if a >= b:
                    continue
                for ref, owner in zip(stack_refs[low], owners, strict=True):
                    mine.append(
                        pltpu.make_async_copy(
                            ref.at[:, (a - low) * lanes : (b - low) * lanes],
                            self.slot(buffer.at[dy], owner(flags), a - begin, b - begin),
                            sems.at[dy],
                        )
                    )
            made.append(mine)
        return made

    def slot(self, target, owner, first, last):
        lanes = self.shape.lanes
        if not self.split:
            return target.at[owner, :, first * lanes : last * lanes]
        half = self.shape.m // 2
        shift = pl.multiple_of(owner // half * self.depth, lanes)
        return target.at[owner % half, :, pl.ds(first * lanes + shift, (last - first) * lanes)]

    def product(self, left, buffer, dy):
        right = buffer[dy].reshape(self.c_out, self.width)
        return lax.dot_general(left, right, (((1,), (1,)), ((), ())), preferred_element_type=F32)

    def put(self, image, row, place, tap, value, first=0, channels=None):
        shape = self.shape
        size = value.shape[0]
        half = self.c_in // 2
        runs = []
        if self.split:
            c = value.shape[1] // 2
            runs = [(odd, tap * half + first // 2, odd * c, c) for odd in range(2)]
        else:
            runs = [(0, tap * self.c_in + first, 0, value.shape[1])]
        for odd, index, at, left in runs:
            while left > 0:
                step = min(left, shape.blk - index % shape.blk)
                lane = odd * self.depth + index // shape.blk * shape.lanes + index % shape.blk
                image[row, place : place + size, lane : lane + step] = value[:, at : at + step]
                index, at, left = index + step, at + step, left - step

    def clear(self, image):
        shape = self.shape
        for block in range(self.width // shape.lanes):
            begin = block * shape.lanes + shape.blk
            end = (block + 1) * shape.lanes
            image[:, :, begin:end] = jnp.zeros((image.shape[0], image.shape[1], end - begin), BF16)


def fine_columns(store, row, even, odd):
    half = even.shape[0]
    store(row, 0, half, 0, shifted(odd, 1))
    store(row, 0, half, 1, even)
    store(row, 0, half, 2, odd)
    store(row, half, half, 0, even)
    store(row, half, half, 1, odd)
    store(row, half, half, 2, shifted(even, -1))


def run_conv(weights, buffer, image, acc, sems, rows, width, begin=lambda dy: dy):
    acc[...] = jnp.zeros(acc.shape, F32)

    def step(dy, carry):
        pltpu.make_async_copy(buffer.at[dy], buffer.at[dy], sems.at[dy]).wait()
        left = image[pl.ds(begin(dy), rows)].reshape(rows * width, weights.width)
        acc[...] += weights.product(left, buffer, dy)
        return carry

    lax.fori_loop(0, 3, step, 0)


def scratch_of(weights, image_rows, out_rows, width, extra=()):
    return [
        pltpu.VMEM((3, weights.c_out // weights.shape.cols_of, weights.shape.cols_of, weights.width), BF16),
        pltpu.VMEM((image_rows, width, weights.width), BF16),
        pltpu.VMEM((out_rows * width, weights.c_out), F32),
        pltpu.SemaphoreType.DMA((3,)),
    ] + list(extra)


def call(body, n_smem, n_vmem, n_any, outs, scratch, flops, limit=60 * 1024 * 1024):
    specs = (
        [pl.BlockSpec(memory_space=pltpu.SMEM)] * n_smem
        + [pl.BlockSpec(memory_space=pltpu.VMEM)] * n_vmem
        + [pl.BlockSpec(memory_space=pltpu.HBM)] * n_any
    )
    return pl.pallas_call(
        body,
        out_shape=[jax.ShapeDtypeStruct(s, d) for s, d in outs],
        in_specs=specs,
        out_specs=[pl.BlockSpec(memory_space=pltpu.VMEM)] * len(outs),
        scratch_shapes=scratch,
        compiler_params=pltpu.CompilerParams(vmem_limit_bytes=limit),
        cost_estimate=pl.CostEstimate(flops=flops, bytes_accessed=4_000_000, transcendentals=0),
    )


def message_outs(rows, width, channels, keep):
    return [
        ((rows * width + TAIL, channels), BF16),
        ((keep * width + TAIL, channels), BF16),
        ((keep * width, channels), BF16),
        ((8, channels), F32),
    ]


def prepare(shape, flags, x, keep):
    rows, width, c = shape.rows, shape.cols, shape.narrow

    def body(flags, x_ref, out_ref, outer_ref, inner_ref, stats_ref):
        out_ref[0 : rows * width, :] = x_ref[...]
        sums = moments_of(x_ref[...].astype(F32))
        emit(flags, out_ref, outer_ref, inner_ref, stats_ref, keep, rows, width, sums)

    return call(body, 1, 1, 0, message_outs(rows, width, c, keep), [], 1000)(flags, x)


def fine_conv(shape, flags, weights, pieces, got, halo, out_halo, keep, residual=None):
    rows, width, half, c = shape.rows, shape.cols, shape.half, shape.narrow
    out_rows = rows + 2 * out_halo
    image_rows = out_rows + 2
    n_pieces = len(pieces)
    extra = 0 if residual is None else 3

    def body(flags, block, outer, inner, sa, sb, *rest):
        res = rest[:extra]
        piece_refs = rest[extra : extra + n_pieces]
        rest = rest[extra + n_pieces :]
        outs = rest[:-4]
        buffer, image, acc, sems = rest[-4:]
        copies = weights.copies(flags, weights.stacks(piece_refs), buffer, sems)
        for mine in copies:
            for copy in mine:
                copy.start()
        weights.clear(image)
        mean, inv = group_terms(sa[...] + sb[...], shape.fine_count)
        mix = parity_matrix(c)

        def store(row, place, size, tap, value):
            weights.put(image, row, place, tap, value.astype(BF16))

        for row in range(image_rows):
            value, outside = ext_row(row + halo - out_halo - 1, block, outer, inner, flags, rows, halo, width)
            value = masked(silu((value - mean) * inv), outside).astype(BF16)
            value = jnp.dot(value, mix, preferred_element_type=F32)
            fine_columns(store, row, value[:half], value[half:])
        run_conv(weights, buffer, image, acc, sems, out_rows, width)
        scale = 1.0 / math.sqrt(9 * c)
        if residual is None:
            out_ref, outer_ref, inner_ref, stats_ref = outs
            value = (acc[...] * scale).astype(BF16)
            out_ref[0 : rows * width, :] = value
            emit(flags, out_ref, outer_ref, inner_ref, stats_ref, keep, rows, width, moments_of(value.astype(F32)))
        else:
            (out_ref,) = outs
            for row in range(out_rows):
                own, _ = ext_row(row, res[0], res[1], res[2], flags, rows, out_halo, width)
                span = slice(row * width, (row + 1) * width)
                out_ref[span, :] = (own + acc[span, :] * scale).astype(BF16)

    outs = message_outs(rows, width, c, keep) if residual is None else [((out_rows * width, c), BF16)]
    args = (flags,) + tuple(got) + (() if residual is None else tuple(residual)) + tuple(pieces)
    flops = 2 * out_rows * width * 9 * c * c
    return call(body, 1, 5 + extra, n_pieces, outs, scratch_of(weights, image_rows, out_rows, width), flops)(*args)


def down_conv(shape, flags, weights, pieces, skip, keep):
    rows, width, half, c = shape.rows, shape.cols, shape.half, shape.narrow
    out_rows = rows // 2

    def body(flags, skip_ref, *rest):
        piece_refs = rest[: len(pieces)]
        outs = rest[len(pieces) : -4]
        buffer, image, acc, sems = rest[-4:]
        copies = weights.copies(flags, weights.stacks(piece_refs), buffer, sems)
        for mine in copies:
            for copy in mine:
                copy.start()
        weights.clear(image)
        for row in range(rows + 1):
            value = skip_ref[row * width : (row + 1) * width, :].astype(F32)
            if row == 0:
                value = masked(value, flags[1] != 0)
            even, odd = value[:half], value[half:]
            place = (row % 2) * (out_rows + 1) + row // 2
            weights.put(image, place, 0, 0, shifted(odd, 1).astype(BF16))
            weights.put(image, place, 0, 1, even.astype(BF16))
            weights.put(image, place, 0, 2, odd.astype(BF16))

        def begin(dy):
            return jnp.where(dy == 1, out_rows + 1, dy // 2)

        run_conv(weights, buffer, image, acc, sems, out_rows, half, begin)
        out_ref, outer_ref, inner_ref, stats_ref = outs
        value = (acc[...] * (1.0 / math.sqrt(9 * c))).astype(BF16)
        out_ref[0 : out_rows * half, :] = value
        emit(flags, out_ref, outer_ref, inner_ref, stats_ref, keep, out_rows, half, moments_of(value.astype(F32)))

    scratch = scratch_of(weights, 2 * (out_rows + 1), out_rows, half)
    outs = message_outs(out_rows, half, shape.wide, keep)
    return call(body, 1, 1, len(pieces), outs, scratch, 2 * out_rows * half * 9 * c * shape.wide)(flags, skip, *pieces)


def coarse_conv(shape, flags, weights, pieces, got, keep, residual=None):
    rows, width, c = shape.rows // 2, shape.half, shape.wide
    extra = 0 if residual is None else 1

    def body(flags, block, outer, inner, sa, sb, *rest):
        res = rest[:extra]
        piece_refs = rest[extra : extra + len(pieces)]
        outs = rest[extra + len(pieces) : -4]
        buffer, image, acc, sems = rest[-4:]
        copies = weights.copies(flags, weights.stacks(piece_refs), buffer, sems)
        for mine in copies:
            for copy in mine:
                copy.start()
        weights.clear(image)
        mean, inv = group_terms(sa[...] + sb[...], shape.coarse_count)
        for row in range(rows + 2):
            value, outside = ext_row(row, block, outer, inner, flags, rows, 1, width)
            value = masked(silu((value - mean) * inv), outside)
            weights.put(image, row, 0, 0, shifted(value, 1).astype(BF16))
            weights.put(image, row, 0, 1, value.astype(BF16))
            weights.put(image, row, 0, 2, shifted(value, -1).astype(BF16))
        run_conv(weights, buffer, image, acc, sems, rows, width)
        out_ref, outer_ref, inner_ref, stats_ref = outs
        value = acc[...] * (1.0 / math.sqrt(9 * c))
        if residual is not None:
            value = res[0][0 : rows * width, :].astype(F32) + value
        value = value.astype(BF16)
        out_ref[0 : rows * width, :] = value
        emit(flags, out_ref, outer_ref, inner_ref, stats_ref, keep, rows, width, moments_of(value.astype(F32)))

    args = (flags,) + tuple(got) + (() if residual is None else (residual,)) + tuple(pieces)
    outs = message_outs(rows, width, c, keep)
    flops = 2 * rows * width * 9 * c * c
    return call(body, 1, 5 + extra, len(pieces), outs, scratch_of(weights, rows + 2, rows, width), flops)(*args)


def up_conv(shape, flags, weights, pieces, got, skip, keep):
    rows, width, half = shape.rows, shape.cols, shape.half
    c, c_out = shape.wide, shape.narrow

    def body(flags, block, outer, inner, skip_ref, *rest):
        piece_refs = rest[: len(pieces)]
        outs = rest[len(pieces) : -4]
        buffer, image, acc, sems = rest[-4:]
        copies = weights.copies(flags, weights.stacks(piece_refs), buffer, sems)
        for mine in copies:
            for copy in mine:
                copy.start()
        weights.clear(image)
        mix = parity_matrix(c)
        for row in range(rows // 2 + 2):
            value, outside = ext_row(row, block, outer, inner, flags, rows // 2, 1, half)
            value = masked(value, outside).astype(BF16)
            value = jnp.dot(value, mix, preferred_element_type=F32)
            before, after = shifted(value, 1).astype(BF16), shifted(value, -1).astype(BF16)
            value = value.astype(BF16)
            for fine in (2 * row - 1, 2 * row):
                if 0 <= fine < rows + 2:
                    for tap, (even, odd) in enumerate(((before, value), (value, value), (value, after))):
                        weights.put(image, fine, 0, tap, even)
                        weights.put(image, fine, half, tap, odd)
        run_conv(weights, buffer, image, acc, sems, rows, width)
        out_ref, outer_ref, inner_ref, stats_ref = outs
        value = (acc[...] * (1.0 / math.sqrt(9 * c))).astype(BF16)
        out_ref[0 : rows * width, :] = value
        own = skip_ref[width : (rows + 1) * width, :].astype(F32)
        sums = moments_of(value.astype(F32)) + moments_of(own)
        emit(flags, out_ref, outer_ref, inner_ref, stats_ref, keep, rows, width, sums)

    outs = message_outs(rows, width, c_out, keep)
    flops = 2 * rows * width * 9 * c * c_out
    scratch = scratch_of(weights, rows + 2, rows, width)
    return call(body, 1, 4, len(pieces), outs, scratch, flops)(flags, *got, skip, *pieces)


def join_conv(shape, flags, weights, pieces, got, skip, keep):
    rows, width, half, c = shape.rows, shape.cols, shape.half, shape.narrow

    def body(flags, block, outer, inner, sa, sb, skip_ref, *rest):
        piece_refs = rest[: len(pieces)]
        outs = rest[len(pieces) : -4]
        buffer, image, acc, sems = rest[-4:]
        copies = weights.copies(flags, weights.stacks(piece_refs), buffer, sems)
        for mine in copies:
            for copy in mine:
                copy.start()
        weights.clear(image)
        mix = parity_matrix(c)
        for part in range(2):
            sums = sa[...] + sb[...]
            mean, inv = pair_terms(sums[2 * part : 2 * part + 2], shape.fine_count)

            def store(row, place, size, tap, value, part=part):
                weights.put(image, row, place, tap, value.astype(BF16), first=part * c)

            for row in range(rows + 2):
                if part == 0:
                    value, outside = ext_row(row, block, outer, inner, flags, rows, 1, width)
                else:
                    value = skip_ref[row * width : (row + 1) * width, :].astype(F32)
                    outside = flags[1] != 0 if row == 0 else flags[2] != 0 if row == rows + 1 else None
                value = masked(silu((value - mean) * inv), outside).astype(BF16)
                value = jnp.dot(value, mix, preferred_element_type=F32)
                fine_columns(store, row, value[:half], value[half:])
        run_conv(weights, buffer, image, acc, sems, rows, width)
        out_ref, outer_ref, inner_ref, stats_ref = outs
        value = (acc[...] * (1.0 / math.sqrt(18 * c))).astype(BF16)
        out_ref[0 : rows * width, :] = value
        emit(flags, out_ref, outer_ref, inner_ref, stats_ref, keep, rows, width, moments_of(value.astype(F32)))

    outs = message_outs(rows, width, c, keep)
    flops = 2 * rows * width * 18 * c * c
    scratch = scratch_of(weights, rows + 2, rows, width)
    return call(body, 1, 6, len(pieces), outs, scratch, flops)(flags, *got, skip, *pieces)


def pair_terms(sums, count):
    width = sums.shape[1]
    size = 2 * width // GROUPS
    terms = row_stack(bf16_terms(sums[0:1]) + bf16_terms(sums[1:2]), 16, width).astype(BF16)
    left = lax.broadcasted_iota(jnp.int32, (width, width), 0) // size
    right = lax.broadcasted_iota(jnp.int32, (width, width), 1) // size
    together = jnp.where(left == right, 1.0, 0.0).astype(BF16)
    summed = jnp.dot(terms, together, preferred_element_type=F32) * (1.0 / (count * size))
    mean = summed[0:1] + summed[1:2] + summed[2:3]
    square = summed[3:4] + summed[4:5] + summed[5:6]
    variance = jnp.maximum(square - mean * mean, 0.0)
    return mean, lax.rsqrt(variance + EPSILON)


def last_conv(shape, flags, weights, pieces, got, u, skip, j_start, n_quarters):
    rows, width, half, c = shape.rows, shape.cols, shape.half, shape.narrow
    quarter = half // n_quarters
    j_block = j_start // shape.blk

    def body(flags, block, outer, inner, sa, sb, u_ref, skip_ref, *rest):
        piece_refs = rest[: len(pieces)]
        outs = rest[len(pieces) : -6]
        buffer, image, acc, sems, jbuf, jsem = rest[-6:]
        copies = weights.copies(flags, weights.stacks(piece_refs), buffer, sems)
        for mine in copies:
            for copy in mine:
                copy.start()
        weights.clear(image)
        for low, high, owners in weights.bounds:
            if low <= j_block < high:
                for ref, owner in zip(weights.stacks(piece_refs)[low], owners, strict=True):
                    pltpu.make_async_copy(
                        ref.at[:, (j_block - low) * shape.lanes : (j_block - low + 1) * shape.lanes],
                        jbuf.at[owner(flags)],
                        jsem,
                    ).start()
        mean, inv = group_terms(sa[...] + sb[...], shape.fine_count)
        mix = parity_matrix(c)

        def store(row, place, size, tap, value):
            weights.put(image, row, place, tap, value.astype(BF16))

        for row in range(rows + 2):
            value, outside = ext_row(row, block, outer, inner, flags, rows, 1, width)
            value = masked(silu((value - mean) * inv), outside).astype(BF16)
            value = jnp.dot(value, mix, preferred_element_type=F32)
            fine_columns(store, row, value[:half], value[half:])
        run_conv(weights, buffer, image, acc, sems, rows, width)
        pltpu.make_async_copy(jbuf, jbuf, jsem).wait()
        right = jbuf[...].reshape(2 * c, shape.lanes)
        left = [u_ref[0 : rows * width, :], skip_ref[width : (rows + 1) * width, :]]
        left = [jnp.dot(part, mix, preferred_element_type=F32).astype(BF16) for part in left]
        made = jnp.zeros((rows * width, c), F32)
        for odd in range(2):
            mine = jnp.concatenate(
                [part[:, odd * (c // 2) : (odd + 1) * (c // 2)] for part in left]
                + [jnp.zeros((rows * width, shape.lanes - c), BF16)],
                axis=1,
            )
            made += lax.dot_general(
                mine, right[odd * c : (odd + 1) * c], (((1,), (1,)), ((), ())), preferred_element_type=F32
            )
        value = made * (1.0 / math.sqrt(2 * c)) + acc[...] * (1.0 / math.sqrt(9 * c))
        value = value.reshape(2 * rows, half, c).astype(BF16)
        for q, out in enumerate(outs):
            out[...] = value[:, q * quarter : (q + 1) * quarter, :]

    outs = [((2 * rows, quarter, c), BF16)] * n_quarters
    flops = 2 * rows * width * 11 * c * c
    extra = [pltpu.VMEM((shape.m, shape.cols_of, shape.lanes), BF16), pltpu.SemaphoreType.DMA(())]
    scratch = scratch_of(weights, rows + 2, rows, width, extra)
    return call(body, 1, 7, len(pieces), outs, scratch, flops)(flags, *got, u, skip, *pieces)


def pack_blocks(shape, pack, bounds):
    columns = pack.shape[0]
    first = bounds[0][0] * shape.blk // 128 * 128
    last = min(-(-bounds[-1][1] * shape.blk // 128) * 128, pack.shape[1])

    def body(pack_ref, *rest):
        outs, (rows, sem) = rest[:-2], rest[-2:]
        copy = pltpu.make_async_copy(pack_ref.at[:, first:last], rows, sem)
        copy.start()
        copy.wait()
        for (low, high), out_ref in zip(bounds, outs, strict=True):
            for block in range(high - low):
                begin, end = block * shape.lanes, (block + 1) * shape.lanes
                at = (low + block) * shape.blk - first
                out_ref[:, begin : begin + shape.blk] = rows[:, at : at + shape.blk]
                out_ref[:, begin + shape.blk : end] = jnp.zeros((columns, shape.lanes - shape.blk), BF16)

    scratch = [pltpu.VMEM((columns, last - first), BF16), pltpu.SemaphoreType.DMA(())]
    outs = [((columns, (high - low) * shape.lanes), BF16) for low, high in bounds]
    return call(body, 0, 0, 1, outs, scratch, 1000)(pack)


def shards(n, n_section, features, section_packs):
    section_id = lax.axis_index("section")
    w = lax.axis_index("space")
    shape = Shape(features, n)
    q_rows = shape.narrow * shape.narrow // shape.wide
    pack = section_packs[0]
    flags = jnp.stack([w % 2, (w == 0).astype(jnp.int32), (w == n - 1).astype(jnp.int32), section_id, w]).astype(jnp.int32)

    total = pack.shape[0] // shape.blk
    cuts = [0, 9 * q_rows // shape.blk, 18 * q_rows // shape.blk, 36 * q_rows // shape.blk, total]
    bounds = list(zip(cuts[:-1], cuts[1:], strict=True))

    def permute(value, source, target, move):
        other = {source: target, target: source}
        pairs = [
            (s * n + i, other[s] * n + move(i) if s in other else s * n + i) for s in range(n_section) for i in range(n)
        ]
        return lax.ppermute(value, ("section", "space"), pairs)

    def within(value, move):
        pairs = [(s * n + i, s * n + move(i)) for s in range(n_section) for i in range(n)]
        return lax.ppermute(value, ("section", "space"), pairs)

    def to_outer(i):
        return (i + 1) % n if i % 2 else (i - 1) % n

    def ahead(i):
        return (i - 2) % n if i % 2 else (i + 2) % n

    def across(i):
        return (i + 4) % n

    def partner(i):
        return i ^ 1

    def sums_of(tail):
        tail = tail[: TAIL // 4 * 3].astype(F32).reshape(-1, 3, tail.shape[1]).sum(1)
        return jnp.concatenate([tail, jnp.zeros((8 - tail.shape[0], tail.shape[1]), F32)], 0)

    def exchange(made, source, target, with_stats=True):
        block, outer, inner, own = made
        if source != target:
            block = permute(block, source, target, lambda i: i)
            rows, size = block.shape[0] - TAIL, inner.shape[0]
            top, bottom, tail = block[:size], block[rows - size : rows], block[rows:]
            outer = jnp.concatenate([jnp.where(flags[0] == 0, top, bottom), tail], 0)
            inner = jnp.where(flags[0] == 0, bottom, top)
            own = sums_of(tail)
        stats = own
        outer = permute(outer, target, target, to_outer)
        inner = permute(inner, target, target, partner)
        if not with_stats:
            return block, outer, inner
        if n == 8:
            b = permute(stats, target, target, ahead)
            c = permute(stats, target, target, across)
            mine = own + sums_of(outer[-TAIL:]) + b + c
            other = permute(mine, target, target, partner)
        else:
            mine = lax.psum(own, "space")
            other = jnp.zeros_like(mine)
        return block, outer, inner, mine, other

    def after(value, *deps):
        return lax.optimization_barrier((value,) + deps)[0]

    pieces = {}
    packed = []
    if n == 8:
        packed = pack_blocks(shape, pack.T, bounds[:1])

    def send(number, *deps):
        low, high = bounds[number]
        if n == 8:
            got = [after(packed[number], *deps)]
            for k in range(1, 4):
                got.append(within(got[0], lambda i, k=k: i ^ (2 * k)))
            return got
        got = lax.all_gather(pack[low * shape.blk : high * shape.blk], "space")
        got = got.reshape(shape.m, n // shape.m, high - low, shape.blk, -1).transpose(0, 1, 4, 2, 3)
        got = got.reshape(shape.m, shape.cols_of, high - low, shape.blk)
        got = jnp.pad(got, ((0, 0), (0, 0), (0, 0), (0, shape.lanes - shape.blk)))
        return list(got.reshape(shape.m, shape.cols_of, -1))

    def finish(number, got, *deps):
        if n == 8:
            got = after(got, *deps)
            shared = [within(part, partner) for part in got]
            near = [lambda flags, j=j: ((flags[4] // 2) ^ j) * 2 + flags[0] for j in range(4)]
            far = [lambda flags, j=j: ((flags[4] // 2) ^ j) * 2 + 1 - flags[0] for j in range(4)]
            pieces[number] = (list(got) + shared, near + far)
        else:
            pieces[number] = (got, [lambda flags, j=j: j for j in range(shape.m)])

    def weights(start, c_in, c_out):
        first = start // shape.blk
        end = (start + 9 * c_in * c_out // shape.wide) // shape.blk
        used = [i for i, (a, b) in enumerate(bounds) if a < end and b > first]
        made = Weights(shape, [bounds[i] + (pieces[i][1],) for i in used], start, c_in, c_out)
        return made, [stack for i in used for stack in pieces[i][0]]

    narrow, wide = shape.narrow, shape.wide
    x = features[0].reshape(shape.rows, shape.half, 2, narrow).transpose(0, 2, 1, 3).reshape(-1, narrow)
    ready = prepare(shape, flags, x, 1)
    sent = send(0, ready[3])
    if n == 8:
        packed += pack_blocks(shape, after(pack.T, sent[0]), bounds[1:])
    first = exchange(ready, 0, 0)
    finish(0, sent, first[3])
    sent = send(1, sent)
    first = (after(first[0], sent[0]),) + first[1:]
    hidden = fine_conv(shape, flags, *weights(0, narrow, narrow), first, 1, 0, 2)
    second = exchange(hidden, 0, 0)
    finish(1, sent, second[3])
    sent = send(2, sent, second[3])
    second = (after(second[0], sent[0]),) + second[1:]
    (skip,) = fine_conv(shape, flags, *weights(9 * q_rows, narrow, narrow), second, 2, 1, 0, residual=first[:3])
    finish(2, sent, skip)
    sent = send(3, sent)
    skip = after(skip, sent[0])
    coarse = down_conv(shape, flags, *weights(18 * q_rows, narrow, wide), skip, 1)
    for section in (1, 2):
        got = exchange(coarse, section - 1, section)
        if section == 1:
            skip, got = lax.optimization_barrier((skip, got))
            skip = permute(skip, 0, n_section - 1, lambda i: i)
        hidden = coarse_conv(shape, flags, *weights(0, wide, wide), got, 1)
        if section == 1:
            finish(3, sent, hidden[3])
            hidden, skip = lax.optimization_barrier((hidden, skip))
        then = exchange(hidden, section, section)
        coarse = coarse_conv(shape, flags, *weights(36 * q_rows, wide, wide), then, 1, residual=got[0])
    got = exchange(coarse, 2, 3, with_stats=False)
    up = up_conv(shape, flags, *weights(0, wide, narrow), got, skip, 1)
    got = exchange(up, 3, 3)
    hidden = join_conv(shape, flags, *weights(18 * q_rows, wide, narrow), got, skip, 1)
    then = exchange(hidden, 3, 3)
    outs = last_conv(shape, flags, *weights(36 * q_rows, narrow, narrow), then, got[0], skip, 45 * q_rows, n_section)
    result = outs[3]
    for target in range(3):
        result = jnp.where(section_id == target, permute(outs[target], 3, target, lambda i: i), result)
    quarter = shape.half // n_section
    result = result.reshape(shape.rows, 2, quarter, narrow).transpose(0, 2, 1, 3)
    return result.reshape(1, shape.rows, 2 * quarter, narrow)


def solution(mesh):
    n, n_section = mesh.shape["space"], mesh.shape["section"]

    def body(features, section_packs):
        return shards(n, n_section, features, section_packs)

    return jax.shard_map(
        body,
        mesh=mesh,
        in_specs=(P(None, "space", None, None), P("section", None, "space")),
        out_specs=P(None, "space", "section", None),
        check_vma=False,
    )
```

```python
import math

import jax
import jax.numpy as jnp
from jax import lax
from jax.experimental import pallas as pl
from jax.experimental.pallas import tpu as pltpu
from jax.sharding import PartitionSpec as P


GROUPS = 32
EPSILON = 1e-05
TAIL = 16
BF16 = jnp.bfloat16
F32 = jnp.float32


def row_stack(rows, count, width):
    ids = lax.broadcasted_iota(jnp.int32, (count, width), 0)
    total = jnp.zeros((count, width), F32)
    for place, row in enumerate(rows):
        total = jnp.where(ids == place, row, total)
    return total


def bf16_terms(row):
    high = row.astype(BF16).astype(F32)
    rest = row - high
    mid = rest.astype(BF16).astype(F32)
    return [high, mid, (rest - mid).astype(BF16).astype(F32)]


def moments_of(value):
    return [
        jnp.sum(value, axis=0, keepdims=True),
        jnp.sum(value * value, axis=0, keepdims=True),
    ]


def group_terms(sums, count):
    width = sums.shape[1]
    size = width // GROUPS
    terms = row_stack(bf16_terms(sums[0:1]) + bf16_terms(sums[1:2]), 16, width).astype(BF16)
    left = lax.broadcasted_iota(jnp.int32, (width, width), 0) // size
    right = lax.broadcasted_iota(jnp.int32, (width, width), 1) // size
    together = jnp.where(left == right, 1.0, 0.0).astype(BF16)
    summed = jnp.dot(terms, together, preferred_element_type=F32) * (1.0 / (count * size))
    mean = summed[0:1] + summed[1:2] + summed[2:3]
    square = summed[3:4] + summed[4:5] + summed[5:6]
    variance = jnp.maximum(square - mean * mean, 0.0)
    return mean, lax.rsqrt(variance + EPSILON)


def silu(z):
    half = 0.5 * z
    return half + half * jnp.tanh(half)


def parity_matrix(width):
    source = lax.broadcasted_iota(jnp.int32, (width, width), 0)
    target = lax.broadcasted_iota(jnp.int32, (width, width), 1)
    half = width // 2
    wanted = jnp.where(target < half, 2 * target, 2 * (target - half) + 1)
    return jnp.where(source == wanted, 1.0, 0.0).astype(BF16)


def shifted(value, step):
    rows = value.shape[0]
    ids = lax.broadcasted_iota(jnp.int32, value.shape, 0)
    if step == 1:
        return jnp.where(ids == 0, 0.0, pltpu.roll(value, 1, 0))
    return jnp.where(ids == rows - 1, 0.0, pltpu.roll(value, rows - 1, 0))


class Shape:
    def __init__(self, features, n):
        self.rows = features.shape[1]
        self.cols = features.shape[2]
        self.half = self.cols // 2
        self.narrow = features.shape[3]
        self.wide = 2 * self.narrow
        self.m = min(n, 8)
        self.cols_of = self.wide // self.m
        self.blk = 3 * self.narrow // 2
        self.lanes = -(-self.blk // 128) * 128
        self.fine_count = self.rows * n * self.cols
        self.coarse_count = self.fine_count // 4


def emit(flags, out_ref, outer_ref, inner_ref, stats_ref, keep, rows, width, sums):
    channels = out_ref.shape[1]
    core0 = flags[0] == 0
    tail = row_stack([term for row in sums for term in bf16_terms(row)], TAIL, channels).astype(BF16)
    out_ref[rows * width :, :] = tail
    stats_ref[...] = row_stack(sums, 8, channels)
    size = keep * width
    first = out_ref[0:size, :].astype(F32)
    last = out_ref[(rows - keep) * width : rows * width, :].astype(F32)
    outer_ref[0:size, :] = jnp.where(core0, first, last).astype(BF16)
    outer_ref[size:, :] = tail
    inner_ref[...] = jnp.where(core0, last, first).astype(BF16)


def ext_row(index, block_ref, outer_ref, inner_ref, flags, rows, halo, width):
    if index < halo:
        span = slice(index * width, (index + 1) * width)
        pick = jnp.where(flags[0] == 0, outer_ref[span, :].astype(F32), inner_ref[span, :].astype(F32))
        return pick, flags[1] != 0
    index -= halo
    if index < rows:
        return block_ref[index * width : (index + 1) * width, :].astype(F32), None
    index -= rows
    span = slice(index * width, (index + 1) * width)
    pick = jnp.where(flags[0] == 0, inner_ref[span, :].astype(F32), outer_ref[span, :].astype(F32))
    return pick, flags[2] != 0


def masked(value, outside):
    if outside is None:
        return value
    return jnp.where(outside, 0.0, value)


class Weights:
    def __init__(self, shape, bounds, start, c_in, c_out):
        self.shape = shape
        self.c_in = c_in
        self.c_out = c_out
        self.split = c_out != shape.wide
        self.blocks = 3 * c_in * c_out // shape.wide // shape.blk
        self.start = start // shape.blk
        self.bounds = bounds
        self.depth = self.blocks * shape.lanes
        self.width = (2 if self.split else 1) * self.depth

    def stacks(self, refs):
        refs = list(refs)
        return {low: [refs.pop(0) for _ in owners] for low, _, owners in self.bounds}

    def copies(self, flags, stack_refs, buffer, sems):
        made = []
        lanes = self.shape.lanes
        for dy in range(3):
            mine = []
            begin = self.start + dy * self.blocks
            for low, high, owners in self.bounds:
                a, b = max(begin, low), min(begin + self.blocks, high)
                if a >= b:
                    continue
                for ref, owner in zip(stack_refs[low], owners, strict=True):
                    mine.append(
                        pltpu.make_async_copy(
                            ref.at[:, (a - low) * lanes : (b - low) * lanes],
                            self.slot(buffer.at[dy], owner(flags), a - begin, b - begin),
                            sems.at[dy],
                        )
                    )
            made.append(mine)
        return made

    def slot(self, target, owner, first, last):
        lanes = self.shape.lanes
        if not self.split:
            return target.at[owner, :, first * lanes : last * lanes]
        half = self.shape.m // 2
        shift = pl.multiple_of(owner // half * self.depth, lanes)
        return target.at[owner % half, :, pl.ds(first * lanes + shift, (last - first) * lanes)]

    def product(self, left, buffer, dy):
        right = buffer[dy].reshape(self.c_out, self.width)
        return lax.dot_general(left, right, (((1,), (1,)), ((), ())), preferred_element_type=F32)

    def put(self, image, row, place, tap, value, first=0, channels=None):
        shape = self.shape
        size = value.shape[0]
        half = self.c_in // 2
        runs = []
        if self.split:
            c = value.shape[1] // 2
            runs = [(odd, tap * half + first // 2, odd * c, c) for odd in range(2)]
        else:
            runs = [(0, tap * self.c_in + first, 0, value.shape[1])]
        for odd, index, at, left in runs:
            while left > 0:
                step = min(left, shape.blk - index % shape.blk)
                lane = odd * self.depth + index // shape.blk * shape.lanes + index % shape.blk
                image[row, place : place + size, lane : lane + step] = value[:, at : at + step]
                index, at, left = index + step, at + step, left - step

    def clear(self, image):
        shape = self.shape
        for block in range(self.width // shape.lanes):
            begin = block * shape.lanes + shape.blk
            end = (block + 1) * shape.lanes
            image[:, :, begin:end] = jnp.zeros((image.shape[0], image.shape[1], end - begin), BF16)


def fine_columns(store, row, even, odd):
    half = even.shape[0]
    store(row, 0, half, 0, shifted(odd, 1))
    store(row, 0, half, 1, even)
    store(row, 0, half, 2, odd)
    store(row, half, half, 0, even)
    store(row, half, half, 1, odd)
    store(row, half, half, 2, shifted(even, -1))


def run_conv(weights, buffer, image, acc, sems, rows, width, begin=lambda dy: dy):
    acc[...] = jnp.zeros(acc.shape, F32)

    def step(dy, carry):
        pltpu.make_async_copy(buffer.at[dy], buffer.at[dy], sems.at[dy]).wait()
        left = image[pl.ds(begin(dy), rows)].reshape(rows * width, weights.width)
        acc[...] += weights.product(left, buffer, dy)
        return carry

    lax.fori_loop(0, 3, step, 0)


def scratch_of(weights, image_rows, out_rows, width, extra=()):
    return [
        pltpu.VMEM((3, weights.c_out // weights.shape.cols_of, weights.shape.cols_of, weights.width), BF16),
        pltpu.VMEM((image_rows, width, weights.width), BF16),
        pltpu.VMEM((out_rows * width, weights.c_out), F32),
        pltpu.SemaphoreType.DMA((3,)),
    ] + list(extra)


def call(body, n_smem, n_vmem, n_any, outs, scratch, flops, limit=60 * 1024 * 1024):
    specs = (
        [pl.BlockSpec(memory_space=pltpu.SMEM)] * n_smem
        + [pl.BlockSpec(memory_space=pltpu.VMEM)] * n_vmem
        + [pl.BlockSpec(memory_space=pltpu.HBM)] * n_any
    )
    return pl.pallas_call(
        body,
        out_shape=[jax.ShapeDtypeStruct(s, d) for s, d in outs],
        in_specs=specs,
        out_specs=[pl.BlockSpec(memory_space=pltpu.VMEM)] * len(outs),
        scratch_shapes=scratch,
        compiler_params=pltpu.CompilerParams(vmem_limit_bytes=limit),
        cost_estimate=pl.CostEstimate(flops=flops, bytes_accessed=4_000_000, transcendentals=0),
    )


def message_outs(rows, width, channels, keep):
    return [
        ((rows * width + TAIL, channels), BF16),
        ((keep * width + TAIL, channels), BF16),
        ((keep * width, channels), BF16),
        ((8, channels), F32),
    ]


def prepare(shape, flags, x, keep):
    rows, width, c = shape.rows, shape.cols, shape.narrow

    def body(flags, x_ref, out_ref, outer_ref, inner_ref, stats_ref):
        out_ref[0 : rows * width, :] = x_ref[...]
        sums = moments_of(x_ref[...].astype(F32))
        emit(flags, out_ref, outer_ref, inner_ref, stats_ref, keep, rows, width, sums)

    return call(body, 1, 1, 0, message_outs(rows, width, c, keep), [], 1000)(flags, x)


def fine_conv(shape, flags, weights, pieces, got, halo, out_halo, keep, residual=None):
    rows, width, half, c = shape.rows, shape.cols, shape.half, shape.narrow
    out_rows = rows + 2 * out_halo
    image_rows = out_rows + 2
    n_pieces = len(pieces)
    extra = 0 if residual is None else 3

    def body(flags, block, outer, inner, sa, sb, *rest):
        res = rest[:extra]
        piece_refs = rest[extra : extra + n_pieces]
        rest = rest[extra + n_pieces :]
        outs = rest[:-4]
        buffer, image, acc, sems = rest[-4:]
        copies = weights.copies(flags, weights.stacks(piece_refs), buffer, sems)
        for mine in copies:
            for copy in mine:
                copy.start()
        weights.clear(image)
        mean, inv = group_terms(sa[...] + sb[...], shape.fine_count)
        mix = parity_matrix(c)

        def store(row, place, size, tap, value):
            weights.put(image, row, place, tap, value.astype(BF16))

        for row in range(image_rows):
            value, outside = ext_row(row + halo - out_halo - 1, block, outer, inner, flags, rows, halo, width)
            value = masked(silu((value - mean) * inv), outside).astype(BF16)
            value = jnp.dot(value, mix, preferred_element_type=F32)
            fine_columns(store, row, value[:half], value[half:])
        run_conv(weights, buffer, image, acc, sems, out_rows, width)
        scale = 1.0 / math.sqrt(9 * c)
        if residual is None:
            out_ref, outer_ref, inner_ref, stats_ref = outs
            value = (acc[...] * scale).astype(BF16)
            out_ref[0 : rows * width, :] = value
            emit(flags, out_ref, outer_ref, inner_ref, stats_ref, keep, rows, width, moments_of(value.astype(F32)))
        else:
            (out_ref,) = outs
            for row in range(out_rows):
                own, _ = ext_row(row, res[0], res[1], res[2], flags, rows, out_halo, width)
                span = slice(row * width, (row + 1) * width)
                out_ref[span, :] = (own + acc[span, :] * scale).astype(BF16)

    outs = message_outs(rows, width, c, keep) if residual is None else [((out_rows * width, c), BF16)]
    args = (flags,) + tuple(got) + (() if residual is None else tuple(residual)) + tuple(pieces)
    flops = 2 * out_rows * width * 9 * c * c
    return call(body, 1, 5 + extra, n_pieces, outs, scratch_of(weights, image_rows, out_rows, width), flops)(*args)


def down_conv(shape, flags, weights, pieces, skip, keep):
    rows, width, half, c = shape.rows, shape.cols, shape.half, shape.narrow
    out_rows = rows // 2

    def body(flags, skip_ref, *rest):
        piece_refs = rest[: len(pieces)]
        outs = rest[len(pieces) : -4]
        buffer, image, acc, sems = rest[-4:]
        copies = weights.copies(flags, weights.stacks(piece_refs), buffer, sems)
        for mine in copies:
            for copy in mine:
                copy.start()
        weights.clear(image)
        for row in range(rows + 1):
            value = skip_ref[row * width : (row + 1) * width, :].astype(F32)
            if row == 0:
                value = masked(value, flags[1] != 0)
            even, odd = value[:half], value[half:]
            place = (row % 2) * (out_rows + 1) + row // 2
            weights.put(image, place, 0, 0, shifted(odd, 1).astype(BF16))
            weights.put(image, place, 0, 1, even.astype(BF16))
            weights.put(image, place, 0, 2, odd.astype(BF16))

        def begin(dy):
            return jnp.where(dy == 1, out_rows + 1, dy // 2)

        run_conv(weights, buffer, image, acc, sems, out_rows, half, begin)
        out_ref, outer_ref, inner_ref, stats_ref = outs
        value = (acc[...] * (1.0 / math.sqrt(9 * c))).astype(BF16)
        out_ref[0 : out_rows * half, :] = value
        emit(flags, out_ref, outer_ref, inner_ref, stats_ref, keep, out_rows, half, moments_of(value.astype(F32)))

    scratch = scratch_of(weights, 2 * (out_rows + 1), out_rows, half)
    outs = message_outs(out_rows, half, shape.wide, keep)
    return call(body, 1, 1, len(pieces), outs, scratch, 2 * out_rows * half * 9 * c * shape.wide)(flags, skip, *pieces)


def coarse_conv(shape, flags, weights, pieces, got, keep, residual=None):
    rows, width, c = shape.rows // 2, shape.half, shape.wide
    extra = 0 if residual is None else 1

    def body(flags, block, outer, inner, sa, sb, *rest):
        res = rest[:extra]
        piece_refs = rest[extra : extra + len(pieces)]
        outs = rest[extra + len(pieces) : -4]
        buffer, image, acc, sems = rest[-4:]
        copies = weights.copies(flags, weights.stacks(piece_refs), buffer, sems)
        for mine in copies:
            for copy in mine:
                copy.start()
        weights.clear(image)
        mean, inv = group_terms(sa[...] + sb[...], shape.coarse_count)
        for row in range(rows + 2):
            value, outside = ext_row(row, block, outer, inner, flags, rows, 1, width)
            value = masked(silu((value - mean) * inv), outside)
            weights.put(image, row, 0, 0, shifted(value, 1).astype(BF16))
            weights.put(image, row, 0, 1, value.astype(BF16))
            weights.put(image, row, 0, 2, shifted(value, -1).astype(BF16))
        run_conv(weights, buffer, image, acc, sems, rows, width)
        out_ref, outer_ref, inner_ref, stats_ref = outs
        value = acc[...] * (1.0 / math.sqrt(9 * c))
        if residual is not None:
            value = res[0][0 : rows * width, :].astype(F32) + value
        value = value.astype(BF16)
        out_ref[0 : rows * width, :] = value
        emit(flags, out_ref, outer_ref, inner_ref, stats_ref, keep, rows, width, moments_of(value.astype(F32)))

    args = (flags,) + tuple(got) + (() if residual is None else (residual,)) + tuple(pieces)
    outs = message_outs(rows, width, c, keep)
    flops = 2 * rows * width * 9 * c * c
    return call(body, 1, 5 + extra, len(pieces), outs, scratch_of(weights, rows + 2, rows, width), flops)(*args)


def up_conv(shape, flags, weights, pieces, got, skip, keep):
    rows, width, half = shape.rows, shape.cols, shape.half
    c, c_out = shape.wide, shape.narrow

    def body(flags, block, outer, inner, skip_ref, *rest):
        piece_refs = rest[: len(pieces)]
        outs = rest[len(pieces) : -4]
        buffer, image, acc, sems = rest[-4:]
        copies = weights.copies(flags, weights.stacks(piece_refs), buffer, sems)
        for mine in copies:
            for copy in mine:
                copy.start()
        weights.clear(image)
        mix = parity_matrix(c)
        for row in range(rows // 2 + 2):
            value, outside = ext_row(row, block, outer, inner, flags, rows // 2, 1, half)
            value = masked(value, outside).astype(BF16)
            value = jnp.dot(value, mix, preferred_element_type=F32)
            before, after = shifted(value, 1).astype(BF16), shifted(value, -1).astype(BF16)
            value = value.astype(BF16)
            for fine in (2 * row - 1, 2 * row):
                if 0 <= fine < rows + 2:
                    for tap, (even, odd) in enumerate(((before, value), (value, value), (value, after))):
                        weights.put(image, fine, 0, tap, even)
                        weights.put(image, fine, half, tap, odd)
        run_conv(weights, buffer, image, acc, sems, rows, width)
        out_ref, outer_ref, inner_ref, stats_ref = outs
        value = (acc[...] * (1.0 / math.sqrt(9 * c))).astype(BF16)
        out_ref[0 : rows * width, :] = value
        own = skip_ref[width : (rows + 1) * width, :].astype(F32)
        sums = moments_of(value.astype(F32)) + moments_of(own)
        emit(flags, out_ref, outer_ref, inner_ref, stats_ref, keep, rows, width, sums)

    outs = message_outs(rows, width, c_out, keep)
    flops = 2 * rows * width * 9 * c * c_out
    scratch = scratch_of(weights, rows + 2, rows, width)
    return call(body, 1, 4, len(pieces), outs, scratch, flops)(flags, *got, skip, *pieces)


def join_conv(shape, flags, weights, pieces, got, skip, keep):
    rows, width, half, c = shape.rows, shape.cols, shape.half, shape.narrow

    def body(flags, block, outer, inner, sa, sb, skip_ref, *rest):
        piece_refs = rest[: len(pieces)]
        outs = rest[len(pieces) : -4]
        buffer, image, acc, sems = rest[-4:]
        copies = weights.copies(flags, weights.stacks(piece_refs), buffer, sems)
        for mine in copies:
            for copy in mine:
                copy.start()
        weights.clear(image)
        mix = parity_matrix(c)
        for part in range(2):
            sums = sa[...] + sb[...]
            mean, inv = pair_terms(sums[2 * part : 2 * part + 2], shape.fine_count)

            def store(row, place, size, tap, value, part=part):
                weights.put(image, row, place, tap, value.astype(BF16), first=part * c)

            for row in range(rows + 2):
                if part == 0:
                    value, outside = ext_row(row, block, outer, inner, flags, rows, 1, width)
                else:
                    value = skip_ref[row * width : (row + 1) * width, :].astype(F32)
                    outside = flags[1] != 0 if row == 0 else flags[2] != 0 if row == rows + 1 else None
                value = masked(silu((value - mean) * inv), outside).astype(BF16)
                value = jnp.dot(value, mix, preferred_element_type=F32)
                fine_columns(store, row, value[:half], value[half:])
        run_conv(weights, buffer, image, acc, sems, rows, width)
        out_ref, outer_ref, inner_ref, stats_ref = outs
        value = (acc[...] * (1.0 / math.sqrt(18 * c))).astype(BF16)
        out_ref[0 : rows * width, :] = value
        emit(flags, out_ref, outer_ref, inner_ref, stats_ref, keep, rows, width, moments_of(value.astype(F32)))

    outs = message_outs(rows, width, c, keep)
    flops = 2 * rows * width * 18 * c * c
    scratch = scratch_of(weights, rows + 2, rows, width)
    return call(body, 1, 6, len(pieces), outs, scratch, flops)(flags, *got, skip, *pieces)


def pair_terms(sums, count):
    width = sums.shape[1]
    size = 2 * width // GROUPS
    terms = row_stack(bf16_terms(sums[0:1]) + bf16_terms(sums[1:2]), 16, width).astype(BF16)
    left = lax.broadcasted_iota(jnp.int32, (width, width), 0) // size
    right = lax.broadcasted_iota(jnp.int32, (width, width), 1) // size
    together = jnp.where(left == right, 1.0, 0.0).astype(BF16)
    summed = jnp.dot(terms, together, preferred_element_type=F32) * (1.0 / (count * size))
    mean = summed[0:1] + summed[1:2] + summed[2:3]
    square = summed[3:4] + summed[4:5] + summed[5:6]
    variance = jnp.maximum(square - mean * mean, 0.0)
    return mean, lax.rsqrt(variance + EPSILON)


def last_conv(shape, flags, weights, pieces, got, u, skip, j_start, n_quarters):
    rows, width, half, c = shape.rows, shape.cols, shape.half, shape.narrow
    quarter = half // n_quarters
    j_block = j_start // shape.blk

    def body(flags, block, outer, inner, sa, sb, u_ref, skip_ref, *rest):
        piece_refs = rest[: len(pieces)]
        outs = rest[len(pieces) : -6]
        buffer, image, acc, sems, jbuf, jsem = rest[-6:]
        copies = weights.copies(flags, weights.stacks(piece_refs), buffer, sems)
        for mine in copies:
            for copy in mine:
                copy.start()
        weights.clear(image)
        for low, high, owners in weights.bounds:
            if low <= j_block < high:
                for ref, owner in zip(weights.stacks(piece_refs)[low], owners, strict=True):
                    pltpu.make_async_copy(
                        ref.at[:, (j_block - low) * shape.lanes : (j_block - low + 1) * shape.lanes],
                        jbuf.at[owner(flags)],
                        jsem,
                    ).start()
        mean, inv = group_terms(sa[...] + sb[...], shape.fine_count)
        mix = parity_matrix(c)

        def store(row, place, size, tap, value):
            weights.put(image, row, place, tap, value.astype(BF16))

        for row in range(rows + 2):
            value, outside = ext_row(row, block, outer, inner, flags, rows, 1, width)
            value = masked(silu((value - mean) * inv), outside).astype(BF16)
            value = jnp.dot(value, mix, preferred_element_type=F32)
            fine_columns(store, row, value[:half], value[half:])
        run_conv(weights, buffer, image, acc, sems, rows, width)
        pltpu.make_async_copy(jbuf, jbuf, jsem).wait()
        right = jbuf[...].reshape(2 * c, shape.lanes)
        left = [u_ref[0 : rows * width, :], skip_ref[width : (rows + 1) * width, :]]
        left = [jnp.dot(part, mix, preferred_element_type=F32).astype(BF16) for part in left]
        made = jnp.zeros((rows * width, c), F32)
        for odd in range(2):
            mine = jnp.concatenate(
                [part[:, odd * (c // 2) : (odd + 1) * (c // 2)] for part in left]
                + [jnp.zeros((rows * width, shape.lanes - c), BF16)],
                axis=1,
            )
            made += lax.dot_general(
                mine, right[odd * c : (odd + 1) * c], (((1,), (1,)), ((), ())), preferred_element_type=F32
            )
        value = made * (1.0 / math.sqrt(2 * c)) + acc[...] * (1.0 / math.sqrt(9 * c))
        value = value.reshape(2 * rows, half, c).astype(BF16)
        for q, out in enumerate(outs):
            out[...] = value[:, q * quarter : (q + 1) * quarter, :]

    outs = [((2 * rows, quarter, c), BF16)] * n_quarters
    flops = 2 * rows * width * 11 * c * c
    extra = [pltpu.VMEM((shape.m, shape.cols_of, shape.lanes), BF16), pltpu.SemaphoreType.DMA(())]
    scratch = scratch_of(weights, rows + 2, rows, width, extra)
    return call(body, 1, 7, len(pieces), outs, scratch, flops)(flags, *got, u, skip, *pieces)


def pack_blocks(shape, pack, bounds):
    columns = pack.shape[0]
    first = bounds[0][0] * shape.blk // 128 * 128
    last = min(-(-bounds[-1][1] * shape.blk // 128) * 128, pack.shape[1])

    def body(pack_ref, *rest):
        outs, (rows, sem) = rest[:-2], rest[-2:]
        copy = pltpu.make_async_copy(pack_ref.at[:, first:last], rows, sem)
        copy.start()
        copy.wait()
        for (low, high), out_ref in zip(bounds, outs, strict=True):
            for block in range(high - low):
                begin, end = block * shape.lanes, (block + 1) * shape.lanes
                at = (low + block) * shape.blk - first
                out_ref[:, begin : begin + shape.blk] = rows[:, at : at + shape.blk]
                out_ref[:, begin + shape.blk : end] = jnp.zeros((columns, shape.lanes - shape.blk), BF16)

    scratch = [pltpu.VMEM((columns, last - first), BF16), pltpu.SemaphoreType.DMA(())]
    outs = [((columns, (high - low) * shape.lanes), BF16) for low, high in bounds]
    return call(body, 0, 0, 1, outs, scratch, 1000)(pack)


def shards(n, n_section, features, section_packs):
    section_id = lax.axis_index("section")
    w = lax.axis_index("space")
    shape = Shape(features, n)
    q_rows = shape.narrow * shape.narrow // shape.wide
    pack = section_packs[0]
    flags = jnp.stack([w % 2, (w == 0).astype(jnp.int32), (w == n - 1).astype(jnp.int32), section_id, w]).astype(jnp.int32)

    total = pack.shape[0] // shape.blk
    cuts = [0, 9 * q_rows // shape.blk, 18 * q_rows // shape.blk, 36 * q_rows // shape.blk, total]
    bounds = list(zip(cuts[:-1], cuts[1:], strict=True))

    def permute(value, source, target, move):
        if source == target:
            return within(value, move)
        other = {source: target, target: source}
        pairs = [
            (s * n + i, other[s] * n + move(i) if s in other else s * n + i) for s in range(n_section) for i in range(n)
        ]
        return lax.ppermute(value, ("section", "space"), pairs)

    def within(value, move):
        pairs = [(s * n + i, s * n + move(i)) for s in range(n_section) for i in range(n)]
        return lax.ppermute(value, ("section", "space"), pairs)

    def to_outer(i):
        return (i + 1) % n if i % 2 else (i - 1) % n

    def ahead(i):
        return (i - 2) % n if i % 2 else (i + 2) % n

    def across(i):
        return (i + 4) % n

    def partner(i):
        return i ^ 1

    def sums_of(tail, count):
        tail = tail.astype(F32)
        rows = [tail[i : i + 1] + tail[i + 1 : i + 2] + tail[i + 2 : i + 3] for i in range(0, 3 * count, 3)]
        return jnp.concatenate(rows + [jnp.zeros((8 - count, tail.shape[1]), F32)], 0)

    def exchange(made, source, target, with_stats=True, count=2):
        block, outer, inner, own = made
        if source != target:
            block = permute(block, source, target, lambda i: i)
            rows, size = block.shape[0] - TAIL, inner.shape[0]
            top, bottom, tail = block[:size], block[rows - size : rows], block[rows:]
            outer = jnp.concatenate([jnp.where(flags[0] == 0, top, bottom), tail], 0)
            inner = jnp.where(flags[0] == 0, bottom, top)
            own = sums_of(tail, count)
        stats = own
        outer = permute(outer, target, target, to_outer)
        inner = permute(inner, target, target, partner)
        if not with_stats:
            return block, outer, inner
        if n == 8:
            b = permute(stats, target, target, ahead)
            c = permute(stats, target, target, across)
            mine = own + sums_of(outer[-TAIL:], count) + b + c
            other = permute(mine, target, target, partner)
        else:
            mine = lax.psum(own, "space")
            other = jnp.zeros_like(mine)
        return block, outer, inner, mine, other

    def after(value, *deps):
        return lax.optimization_barrier((value,) + deps)[0]

    pieces = {}
    packed = []
    if n == 8:
        packed = pack_blocks(shape, pack.T, bounds[:1])

    def send(number, *deps):
        low, high = bounds[number]
        if n == 8:
            got = [after(packed[number], *deps)]
            for k in range(1, 4):
                got.append(within(got[0], lambda i, k=k: i ^ (2 * k)))
            return got
        got = lax.all_gather(pack[low * shape.blk : high * shape.blk], "space")
        got = got.reshape(shape.m, n // shape.m, high - low, shape.blk, -1).transpose(0, 1, 4, 2, 3)
        got = got.reshape(shape.m, shape.cols_of, high - low, shape.blk)
        got = jnp.pad(got, ((0, 0), (0, 0), (0, 0), (0, shape.lanes - shape.blk)))
        return list(got.reshape(shape.m, shape.cols_of, -1))

    def finish(number, got, *deps, last_dep=None):
        if n == 8:
            early, late = list(got[:3]), list(got[3:])
            if last_dep is not None:
                late = after(late, last_dep)
            if deps:
                early = after(early, *deps)
            got = early + late
            shared = [within(part, partner) for part in got]
            near = [lambda flags, j=j: ((flags[4] // 2) ^ j) * 2 + flags[0] for j in range(4)]
            far = [lambda flags, j=j: ((flags[4] // 2) ^ j) * 2 + 1 - flags[0] for j in range(4)]
            pieces[number] = (list(got) + shared, near + far)
        else:
            pieces[number] = (got, [lambda flags, j=j: j for j in range(shape.m)])

    def weights(start, c_in, c_out):
        first = start // shape.blk
        end = (start + 9 * c_in * c_out // shape.wide) // shape.blk
        used = [i for i, (a, b) in enumerate(bounds) if a < end and b > first]
        made = Weights(shape, [bounds[i] + (pieces[i][1],) for i in used], start, c_in, c_out)
        return made, [stack for i in used for stack in pieces[i][0]]

    narrow, wide = shape.narrow, shape.wide
    x = features[0].reshape(shape.rows, shape.half, 2, narrow).transpose(0, 2, 1, 3).reshape(-1, narrow)
    ready = prepare(shape, flags, x, 1)
    sent = send(0, ready[3])
    if n == 8:
        packed += pack_blocks(shape, after(pack.T, sent[0]), bounds[1:])
    first = exchange(ready, 0, 0)
    finish(0, sent, first[3])
    sent = send(1, sent)
    first = (after(first[0], sent[0]),) + first[1:]
    hidden = fine_conv(shape, flags, *weights(0, narrow, narrow), first, 1, 0, 2)
    second = exchange(hidden, 0, 0)
    finish(1, sent, second[3])
    sent = send(2, sent, second[3])
    second = (after(second[0], sent[0]),) + second[1:]
    (skip,) = fine_conv(shape, flags, *weights(9 * q_rows, narrow, narrow), second, 2, 1, 0, residual=first[:3])
    finish(2, sent, skip)
    sent = send(3, sent)
    skip = after(skip, sent[0])
    coarse = down_conv(shape, flags, *weights(18 * q_rows, narrow, wide), skip, 1)
    for section in (1, 2):
        got = exchange(coarse, section - 1, section)
        if section == 1:
            skip, got = lax.optimization_barrier((skip, got))
            skip = permute(skip, 0, n_section - 1, lambda i: i)
        hidden = coarse_conv(shape, flags, *weights(0, wide, wide), got, 1)
        if section == 1:
            hidden, skip = lax.optimization_barrier((hidden, skip))
        then = exchange(hidden, section, section)
        if section == 1:
            finish(3, sent, hidden[3], last_dep=then[3])
        coarse = coarse_conv(shape, flags, *weights(36 * q_rows, wide, wide), then, 1, residual=got[0])
    got = exchange(coarse, 2, 3, with_stats=False)
    up = up_conv(shape, flags, *weights(0, wide, narrow), got, skip, 1)
    got = exchange(up, 3, 3, count=4)
    hidden = join_conv(shape, flags, *weights(18 * q_rows, wide, narrow), got, skip, 1)
    then = exchange(hidden, 3, 3)
    outs = last_conv(shape, flags, *weights(36 * q_rows, narrow, narrow), then, got[0], skip, 45 * q_rows, n_section)
    result = outs[3]
    for target in range(3):
        result = jnp.where(section_id == target, permute(outs[target], 3, target, lambda i: i), result)
    quarter = shape.half // n_section
    result = result.reshape(shape.rows, 2, quarter, narrow).transpose(0, 2, 1, 3)
    return result.reshape(1, shape.rows, 2 * quarter, narrow)


def solution(mesh):
    n, n_section = mesh.shape["space"], mesh.shape["section"]

    def body(features, section_packs):
        return shards(n, n_section, features, section_packs)

    return jax.shard_map(
        body,
        mesh=mesh,
        in_specs=(P(None, "space", None, None), P("section", None, "space")),
        out_specs=P(None, "space", "section", None),
        check_vma=False,
    )
```

```python
import math

import jax
import jax.numpy as jnp
from jax import lax
from jax.experimental import pallas as pl
from jax.experimental.pallas import tpu as pltpu
from jax.sharding import PartitionSpec as P


GROUPS = 32
EPSILON = 1e-05
TAIL = 16
RELAYED = (2, 3)
BF16 = jnp.bfloat16
F32 = jnp.float32


def row_stack(rows, count, width):
    ids = lax.broadcasted_iota(jnp.int32, (count, width), 0)
    total = jnp.zeros((count, width), F32)
    for place, row in enumerate(rows):
        total = jnp.where(ids == place, row, total)
    return total


def bf16_terms(row):
    high = row.astype(BF16).astype(F32)
    rest = row - high
    mid = rest.astype(BF16).astype(F32)
    return [high, mid, (rest - mid).astype(BF16).astype(F32)]


def moments_of(value):
    return [
        jnp.sum(value, axis=0, keepdims=True),
        jnp.sum(value * value, axis=0, keepdims=True),
    ]


def group_terms(sums, count):
    width = sums.shape[1]
    size = width // GROUPS
    terms = row_stack(bf16_terms(sums[0:1]) + bf16_terms(sums[1:2]), 16, width).astype(BF16)
    left = lax.broadcasted_iota(jnp.int32, (width, width), 0) // size
    right = lax.broadcasted_iota(jnp.int32, (width, width), 1) // size
    together = jnp.where(left == right, 1.0, 0.0).astype(BF16)
    summed = jnp.dot(terms, together, preferred_element_type=F32) * (1.0 / (count * size))
    mean = summed[0:1] + summed[1:2] + summed[2:3]
    square = summed[3:4] + summed[4:5] + summed[5:6]
    variance = jnp.maximum(square - mean * mean, 0.0)
    return mean, lax.rsqrt(variance + EPSILON)


def silu(z):
    half = 0.5 * z
    return half + half * jnp.tanh(half)


def parity_matrix(width):
    source = lax.broadcasted_iota(jnp.int32, (width, width), 0)
    target = lax.broadcasted_iota(jnp.int32, (width, width), 1)
    half = width // 2
    wanted = jnp.where(target < half, 2 * target, 2 * (target - half) + 1)
    return jnp.where(source == wanted, 1.0, 0.0).astype(BF16)


def shifted(value, step):
    rows = value.shape[0]
    ids = lax.broadcasted_iota(jnp.int32, value.shape, 0)
    if step == 1:
        return jnp.where(ids == 0, 0.0, pltpu.roll(value, 1, 0))
    return jnp.where(ids == rows - 1, 0.0, pltpu.roll(value, rows - 1, 0))


class Shape:
    def __init__(self, features, n):
        self.rows = features.shape[1]
        self.cols = features.shape[2]
        self.half = self.cols // 2
        self.narrow = features.shape[3]
        self.wide = 2 * self.narrow
        self.m = min(n, 8)
        self.cols_of = self.wide // self.m
        self.blk = 3 * self.narrow // 2
        self.lanes = -(-self.blk // 128) * 128
        self.fine_count = self.rows * n * self.cols
        self.coarse_count = self.fine_count // 4


def emit(flags, out_ref, outer_ref, inner_ref, stats_ref, keep, rows, width, sums):
    channels = out_ref.shape[1]
    core0 = flags[0] == 0
    tail = row_stack([term for row in sums for term in bf16_terms(row)], TAIL, channels).astype(BF16)
    out_ref[rows * width :, :] = tail
    stats_ref[...] = row_stack(sums, 8, channels)
    size = keep * width
    first = out_ref[0:size, :].astype(F32)
    last = out_ref[(rows - keep) * width : rows * width, :].astype(F32)
    outer_ref[0:size, :] = jnp.where(core0, first, last).astype(BF16)
    outer_ref[size:, :] = tail
    inner_ref[...] = jnp.where(core0, last, first).astype(BF16)


def ext_row(index, block_ref, outer_ref, inner_ref, flags, rows, halo, width):
    if index < halo:
        span = slice(index * width, (index + 1) * width)
        pick = jnp.where(flags[0] == 0, outer_ref[span, :].astype(F32), inner_ref[span, :].astype(F32))
        return pick, flags[1] != 0
    index -= halo
    if index < rows:
        return block_ref[index * width : (index + 1) * width, :].astype(F32), None
    index -= rows
    span = slice(index * width, (index + 1) * width)
    pick = jnp.where(flags[0] == 0, inner_ref[span, :].astype(F32), outer_ref[span, :].astype(F32))
    return pick, flags[2] != 0


def masked(value, outside):
    if outside is None:
        return value
    return jnp.where(outside, 0.0, value)


class Weights:
    def __init__(self, shape, entries, start, c_in, c_out):
        self.shape = shape
        self.c_in = c_in
        self.c_out = c_out
        self.split = c_out != shape.wide
        self.blocks = 3 * c_in * c_out // shape.wide // shape.blk
        self.start = start // shape.blk
        self.entries = entries
        self.depth = self.blocks * shape.lanes
        self.width = (2 if self.split else 1) * self.depth

    def copies(self, flags, refs, buffer, sems):
        made = []
        lanes = self.shape.lanes
        for dy in range(3):
            mine = []
            begin = self.start + dy * self.blocks
            for ref, (owner, low, high) in zip(refs, self.entries, strict=True):
                a, b = max(begin, low), min(begin + self.blocks, high)
                if a < b:
                    mine.append(
                        pltpu.make_async_copy(
                            ref.at[:, (a - low) * lanes : (b - low) * lanes],
                            self.slot(buffer.at[dy], owner(flags), a - begin, b - begin),
                            sems.at[dy],
                        )
                    )
            made.append(mine)
        return made

    def slot(self, target, owner, first, last):
        lanes = self.shape.lanes
        if not self.split:
            return target.at[owner, :, first * lanes : last * lanes]
        half = self.shape.m // 2
        shift = pl.multiple_of(owner // half * self.depth, lanes)
        return target.at[owner % half, :, pl.ds(first * lanes + shift, (last - first) * lanes)]

    def product(self, left, buffer, dy):
        right = buffer[dy].reshape(self.c_out, self.width)
        return lax.dot_general(left, right, (((1,), (1,)), ((), ())), preferred_element_type=F32)

    def put(self, image, row, place, tap, value, first=0, channels=None):
        shape = self.shape
        size = value.shape[0]
        half = self.c_in // 2
        runs = []
        if self.split:
            c = value.shape[1] // 2
            runs = [(odd, tap * half + first // 2, odd * c, c) for odd in range(2)]
        else:
            runs = [(0, tap * self.c_in + first, 0, value.shape[1])]
        for odd, index, at, left in runs:
            while left > 0:
                step = min(left, shape.blk - index % shape.blk)
                lane = odd * self.depth + index // shape.blk * shape.lanes + index % shape.blk
                image[row, place : place + size, lane : lane + step] = value[:, at : at + step]
                index, at, left = index + step, at + step, left - step

    def clear(self, image):
        shape = self.shape
        for block in range(self.width // shape.lanes):
            begin = block * shape.lanes + shape.blk
            end = (block + 1) * shape.lanes
            image[:, :, begin:end] = jnp.zeros((image.shape[0], image.shape[1], end - begin), BF16)


def fine_columns(store, row, even, odd):
    half = even.shape[0]
    store(row, 0, half, 0, shifted(odd, 1))
    store(row, 0, half, 1, even)
    store(row, 0, half, 2, odd)
    store(row, half, half, 0, even)
    store(row, half, half, 1, odd)
    store(row, half, half, 2, shifted(even, -1))


def run_conv(weights, buffer, image, acc, sems, rows, width, begin=lambda dy: dy):
    acc[...] = jnp.zeros(acc.shape, F32)

    def step(dy, carry):
        pltpu.make_async_copy(buffer.at[dy], buffer.at[dy], sems.at[dy]).wait()
        left = image[pl.ds(begin(dy), rows)].reshape(rows * width, weights.width)
        acc[...] += weights.product(left, buffer, dy)
        return carry

    lax.fori_loop(0, 3, step, 0)


def scratch_of(weights, image_rows, out_rows, width, extra=()):
    return [
        pltpu.VMEM((3, weights.c_out // weights.shape.cols_of, weights.shape.cols_of, weights.width), BF16),
        pltpu.VMEM((image_rows, width, weights.width), BF16),
        pltpu.VMEM((out_rows * width, weights.c_out), F32),
        pltpu.SemaphoreType.DMA((3,)),
    ] + list(extra)


def call(body, n_smem, n_vmem, n_any, outs, scratch, flops, limit=60 * 1024 * 1024):
    specs = (
        [pl.BlockSpec(memory_space=pltpu.SMEM)] * n_smem
        + [pl.BlockSpec(memory_space=pltpu.VMEM)] * n_vmem
        + [pl.BlockSpec(memory_space=pltpu.HBM)] * n_any
    )
    return pl.pallas_call(
        body,
        out_shape=[jax.ShapeDtypeStruct(s, d) for s, d in outs],
        in_specs=specs,
        out_specs=[pl.BlockSpec(memory_space=pltpu.VMEM)] * len(outs),
        scratch_shapes=scratch,
        compiler_params=pltpu.CompilerParams(vmem_limit_bytes=limit),
        cost_estimate=pl.CostEstimate(flops=flops, bytes_accessed=4_000_000, transcendentals=0),
    )


def message_outs(rows, width, channels, keep):
    return [
        ((rows * width + TAIL, channels), BF16),
        ((keep * width + TAIL, channels), BF16),
        ((keep * width, channels), BF16),
        ((8, channels), F32),
    ]


def prepare(shape, flags, x, keep):
    rows, width, c = shape.rows, shape.cols, shape.narrow

    def body(flags, x_ref, out_ref, outer_ref, inner_ref, stats_ref):
        out_ref[0 : rows * width, :] = x_ref[...]
        sums = moments_of(x_ref[...].astype(F32))
        emit(flags, out_ref, outer_ref, inner_ref, stats_ref, keep, rows, width, sums)

    return call(body, 1, 1, 0, message_outs(rows, width, c, keep), [], 1000)(flags, x)


def fine_conv(shape, flags, weights, pieces, got, halo, out_halo, keep, residual=None):
    rows, width, half, c = shape.rows, shape.cols, shape.half, shape.narrow
    out_rows = rows + 2 * out_halo
    image_rows = out_rows + 2
    n_pieces = len(pieces)
    extra = 0 if residual is None else 3

    def body(flags, block, outer, inner, sa, sb, *rest):
        res = rest[:extra]
        piece_refs = rest[extra : extra + n_pieces]
        rest = rest[extra + n_pieces :]
        outs = rest[:-4]
        buffer, image, acc, sems = rest[-4:]
        copies = weights.copies(flags, piece_refs, buffer, sems)
        for mine in copies:
            for copy in mine:
                copy.start()
        weights.clear(image)
        mean, inv = group_terms(sa[...] + sb[...], shape.fine_count)
        mix = parity_matrix(c)

        def store(row, place, size, tap, value):
            weights.put(image, row, place, tap, value.astype(BF16))

        for row in range(image_rows):
            value, outside = ext_row(row + halo - out_halo - 1, block, outer, inner, flags, rows, halo, width)
            value = masked(silu((value - mean) * inv), outside).astype(BF16)
            value = jnp.dot(value, mix, preferred_element_type=F32)
            fine_columns(store, row, value[:half], value[half:])
        run_conv(weights, buffer, image, acc, sems, out_rows, width)
        scale = 1.0 / math.sqrt(9 * c)
        if residual is None:
            out_ref, outer_ref, inner_ref, stats_ref = outs
            value = (acc[...] * scale).astype(BF16)
            out_ref[0 : rows * width, :] = value
            emit(flags, out_ref, outer_ref, inner_ref, stats_ref, keep, rows, width, moments_of(value.astype(F32)))
        else:
            (out_ref,) = outs
            for row in range(out_rows):
                own, _ = ext_row(row, res[0], res[1], res[2], flags, rows, out_halo, width)
                span = slice(row * width, (row + 1) * width)
                out_ref[span, 0:c] = (own + acc[span, :] * scale).astype(BF16)
                out_ref[span, c:] = jnp.zeros((width, out_ref.shape[1] - c), BF16)

    outs = message_outs(rows, width, c, keep) if residual is None else [((out_rows * width, -(-c // 128) * 128), BF16)]
    args = (flags,) + tuple(got) + (() if residual is None else tuple(residual)) + tuple(pieces)
    flops = 2 * out_rows * width * 9 * c * c
    return call(body, 1, 5 + extra, n_pieces, outs, scratch_of(weights, image_rows, out_rows, width), flops)(*args)


def down_conv(shape, flags, weights, pieces, skip, keep):
    rows, width, half, c = shape.rows, shape.cols, shape.half, shape.narrow
    out_rows = rows // 2

    def body(flags, skip_ref, *rest):
        piece_refs = rest[: len(pieces)]
        outs = rest[len(pieces) : -4]
        buffer, image, acc, sems = rest[-4:]
        copies = weights.copies(flags, piece_refs, buffer, sems)
        for mine in copies:
            for copy in mine:
                copy.start()
        weights.clear(image)
        for row in range(rows + 1):
            value = skip_ref[row * width : (row + 1) * width, 0:c].astype(F32)
            if row == 0:
                value = masked(value, flags[1] != 0)
            even, odd = value[:half], value[half:]
            place = (row % 2) * (out_rows + 1) + row // 2
            weights.put(image, place, 0, 0, shifted(odd, 1).astype(BF16))
            weights.put(image, place, 0, 1, even.astype(BF16))
            weights.put(image, place, 0, 2, odd.astype(BF16))

        def begin(dy):
            return jnp.where(dy == 1, out_rows + 1, dy // 2)

        run_conv(weights, buffer, image, acc, sems, out_rows, half, begin)
        out_ref, outer_ref, inner_ref, stats_ref = outs
        value = (acc[...] * (1.0 / math.sqrt(9 * c))).astype(BF16)
        out_ref[0 : out_rows * half, :] = value
        emit(flags, out_ref, outer_ref, inner_ref, stats_ref, keep, out_rows, half, moments_of(value.astype(F32)))

    scratch = scratch_of(weights, 2 * (out_rows + 1), out_rows, half)
    outs = message_outs(out_rows, half, shape.wide, keep)
    return call(body, 1, 1, len(pieces), outs, scratch, 2 * out_rows * half * 9 * c * shape.wide)(flags, skip, *pieces)


def coarse_conv(shape, flags, weights, pieces, got, keep, residual=None):
    rows, width, c = shape.rows // 2, shape.half, shape.wide
    extra = 0 if residual is None else 1

    def body(flags, block, outer, inner, sa, sb, *rest):
        res = rest[:extra]
        piece_refs = rest[extra : extra + len(pieces)]
        outs = rest[extra + len(pieces) : -4]
        buffer, image, acc, sems = rest[-4:]
        copies = weights.copies(flags, piece_refs, buffer, sems)
        for mine in copies:
            for copy in mine:
                copy.start()
        weights.clear(image)
        mean, inv = group_terms(sa[...] + sb[...], shape.coarse_count)
        for row in range(rows + 2):
            value, outside = ext_row(row, block, outer, inner, flags, rows, 1, width)
            value = masked(silu((value - mean) * inv), outside)
            weights.put(image, row, 0, 0, shifted(value, 1).astype(BF16))
            weights.put(image, row, 0, 1, value.astype(BF16))
            weights.put(image, row, 0, 2, shifted(value, -1).astype(BF16))
        run_conv(weights, buffer, image, acc, sems, rows, width)
        out_ref, outer_ref, inner_ref, stats_ref = outs
        value = acc[...] * (1.0 / math.sqrt(9 * c))
        if residual is not None:
            value = res[0][0 : rows * width, :].astype(F32) + value
        value = value.astype(BF16)
        out_ref[0 : rows * width, :] = value
        emit(flags, out_ref, outer_ref, inner_ref, stats_ref, keep, rows, width, moments_of(value.astype(F32)))

    args = (flags,) + tuple(got) + (() if residual is None else (residual,)) + tuple(pieces)
    outs = message_outs(rows, width, c, keep)
    flops = 2 * rows * width * 9 * c * c
    return call(body, 1, 5 + extra, len(pieces), outs, scratch_of(weights, rows + 2, rows, width), flops)(*args)


def up_conv(shape, flags, weights, pieces, got, skip, keep):
    rows, width, half = shape.rows, shape.cols, shape.half
    c, c_out = shape.wide, shape.narrow

    def body(flags, block, outer, inner, skip_ref, *rest):
        piece_refs = rest[: len(pieces)]
        outs = rest[len(pieces) : -4]
        buffer, image, acc, sems = rest[-4:]
        copies = weights.copies(flags, piece_refs, buffer, sems)
        for mine in copies:
            for copy in mine:
                copy.start()
        weights.clear(image)
        mix = parity_matrix(c)
        for row in range(rows // 2 + 2):
            value, outside = ext_row(row, block, outer, inner, flags, rows // 2, 1, half)
            value = masked(value, outside).astype(BF16)
            value = jnp.dot(value, mix, preferred_element_type=F32)
            before, after = shifted(value, 1).astype(BF16), shifted(value, -1).astype(BF16)
            value = value.astype(BF16)
            for fine in (2 * row - 1, 2 * row):
                if 0 <= fine < rows + 2:
                    for tap, (even, odd) in enumerate(((before, value), (value, value), (value, after))):
                        weights.put(image, fine, 0, tap, even)
                        weights.put(image, fine, half, tap, odd)
        run_conv(weights, buffer, image, acc, sems, rows, width)
        out_ref, outer_ref, inner_ref, stats_ref = outs
        value = (acc[...] * (1.0 / math.sqrt(9 * c))).astype(BF16)
        out_ref[0 : rows * width, :] = value
        own = skip_ref[width : (rows + 1) * width, 0:c_out].astype(F32)
        sums = moments_of(value.astype(F32)) + moments_of(own)
        emit(flags, out_ref, outer_ref, inner_ref, stats_ref, keep, rows, width, sums)

    outs = message_outs(rows, width, c_out, keep)
    flops = 2 * rows * width * 9 * c * c_out
    scratch = scratch_of(weights, rows + 2, rows, width)
    return call(body, 1, 4, len(pieces), outs, scratch, flops)(flags, *got, skip, *pieces)


def join_conv(shape, flags, weights, pieces, got, skip, keep):
    rows, width, half, c = shape.rows, shape.cols, shape.half, shape.narrow

    def body(flags, block, outer, inner, sa, sb, skip_ref, *rest):
        piece_refs = rest[: len(pieces)]
        outs = rest[len(pieces) : -4]
        buffer, image, acc, sems = rest[-4:]
        copies = weights.copies(flags, piece_refs, buffer, sems)
        for mine in copies:
            for copy in mine:
                copy.start()
        weights.clear(image)
        mix = parity_matrix(c)
        for part in range(2):
            sums = sa[...] + sb[...]
            mean, inv = pair_terms(sums[2 * part : 2 * part + 2], shape.fine_count)

            def store(row, place, size, tap, value, part=part):
                weights.put(image, row, place, tap, value.astype(BF16), first=part * c)

            for row in range(rows + 2):
                if part == 0:
                    value, outside = ext_row(row, block, outer, inner, flags, rows, 1, width)
                else:
                    value = skip_ref[row * width : (row + 1) * width, 0:c].astype(F32)
                    outside = flags[1] != 0 if row == 0 else flags[2] != 0 if row == rows + 1 else None
                value = masked(silu((value - mean) * inv), outside).astype(BF16)
                value = jnp.dot(value, mix, preferred_element_type=F32)
                fine_columns(store, row, value[:half], value[half:])
        run_conv(weights, buffer, image, acc, sems, rows, width)
        out_ref, outer_ref, inner_ref, stats_ref = outs
        value = (acc[...] * (1.0 / math.sqrt(18 * c))).astype(BF16)
        out_ref[0 : rows * width, :] = value
        emit(flags, out_ref, outer_ref, inner_ref, stats_ref, keep, rows, width, moments_of(value.astype(F32)))

    outs = message_outs(rows, width, c, keep)
    flops = 2 * rows * width * 18 * c * c
    scratch = scratch_of(weights, rows + 2, rows, width)
    return call(body, 1, 6, len(pieces), outs, scratch, flops)(flags, *got, skip, *pieces)


def pair_terms(sums, count):
    width = sums.shape[1]
    size = 2 * width // GROUPS
    terms = row_stack(bf16_terms(sums[0:1]) + bf16_terms(sums[1:2]), 16, width).astype(BF16)
    left = lax.broadcasted_iota(jnp.int32, (width, width), 0) // size
    right = lax.broadcasted_iota(jnp.int32, (width, width), 1) // size
    together = jnp.where(left == right, 1.0, 0.0).astype(BF16)
    summed = jnp.dot(terms, together, preferred_element_type=F32) * (1.0 / (count * size))
    mean = summed[0:1] + summed[1:2] + summed[2:3]
    square = summed[3:4] + summed[4:5] + summed[5:6]
    variance = jnp.maximum(square - mean * mean, 0.0)
    return mean, lax.rsqrt(variance + EPSILON)


def last_conv(shape, flags, weights, pieces, got, u, skip, j_start, n_quarters):
    rows, width, half, c = shape.rows, shape.cols, shape.half, shape.narrow
    quarter = half // n_quarters
    j_block = j_start // shape.blk

    def body(flags, block, outer, inner, sa, sb, u_ref, skip_ref, *rest):
        piece_refs = rest[: len(pieces)]
        outs = rest[len(pieces) : -6]
        buffer, image, acc, sems, jbuf, jsem = rest[-6:]
        copies = weights.copies(flags, piece_refs, buffer, sems)
        for mine in copies:
            for copy in mine:
                copy.start()
        weights.clear(image)
        for ref, (owner, low, high) in zip(piece_refs, weights.entries, strict=True):
            if low <= j_block < high:
                pltpu.make_async_copy(
                    ref.at[:, (j_block - low) * shape.lanes : (j_block - low + 1) * shape.lanes],
                    jbuf.at[owner(flags)],
                    jsem,
                ).start()
        mean, inv = group_terms(sa[...] + sb[...], shape.fine_count)
        mix = parity_matrix(c)

        def store(row, place, size, tap, value):
            weights.put(image, row, place, tap, value.astype(BF16))

        for row in range(rows + 2):
            value, outside = ext_row(row, block, outer, inner, flags, rows, 1, width)
            value = masked(silu((value - mean) * inv), outside).astype(BF16)
            value = jnp.dot(value, mix, preferred_element_type=F32)
            fine_columns(store, row, value[:half], value[half:])
        run_conv(weights, buffer, image, acc, sems, rows, width)
        pltpu.make_async_copy(jbuf, jbuf, jsem).wait()
        right = jbuf[...].reshape(2 * c, shape.lanes)
        left = [u_ref[0 : rows * width, :], skip_ref[width : (rows + 1) * width, 0:c]]
        left = [jnp.dot(part, mix, preferred_element_type=F32).astype(BF16) for part in left]
        made = jnp.zeros((rows * width, c), F32)
        for odd in range(2):
            mine = jnp.concatenate(
                [part[:, odd * (c // 2) : (odd + 1) * (c // 2)] for part in left]
                + [jnp.zeros((rows * width, shape.lanes - c), BF16)],
                axis=1,
            )
            made += lax.dot_general(
                mine, right[odd * c : (odd + 1) * c], (((1,), (1,)), ((), ())), preferred_element_type=F32
            )
        value = made * (1.0 / math.sqrt(2 * c)) + acc[...] * (1.0 / math.sqrt(9 * c))
        value = value.reshape(2 * rows, half, c).astype(BF16)
        for q, out in enumerate(outs):
            out[...] = value[:, q * quarter : (q + 1) * quarter, :]

    outs = [((2 * rows, quarter, c), BF16)] * n_quarters
    flops = 2 * rows * width * 11 * c * c
    extra = [pltpu.VMEM((shape.m, shape.cols_of, shape.lanes), BF16), pltpu.SemaphoreType.DMA(())]
    scratch = scratch_of(weights, rows + 2, rows, width, extra)
    return call(body, 1, 7, len(pieces), outs, scratch, flops)(flags, *got, u, skip, *pieces)


def pack_blocks(shape, pack, bounds):
    columns = pack.shape[0]
    first = bounds[0][0] * shape.blk // 128 * 128
    last = min(-(-bounds[-1][1] * shape.blk // 128) * 128, pack.shape[1])

    def body(pack_ref, *rest):
        outs, (rows, sem) = rest[:-2], rest[-2:]
        copy = pltpu.make_async_copy(pack_ref.at[:, first:last], rows, sem)
        copy.start()
        copy.wait()
        for (low, high), out_ref in zip(bounds, outs, strict=True):
            for block in range(high - low):
                begin, end = block * shape.lanes, (block + 1) * shape.lanes
                at = (low + block) * shape.blk - first
                out_ref[:, begin : begin + shape.blk] = rows[:, at : at + shape.blk]
                out_ref[:, begin + shape.blk : end] = jnp.zeros((columns, shape.lanes - shape.blk), BF16)

    scratch = [pltpu.VMEM((columns, last - first), BF16), pltpu.SemaphoreType.DMA(())]
    outs = [((columns, (high - low) * shape.lanes), BF16) for low, high in bounds]
    return call(body, 0, 0, 1, outs, scratch, 1000)(pack)


def shards(n, n_section, features, section_packs):
    section_id = lax.axis_index("section")
    w = lax.axis_index("space")
    shape = Shape(features, n)
    q_rows = shape.narrow * shape.narrow // shape.wide
    pack = section_packs[0]
    flags = jnp.stack([w % 2, (w == 0).astype(jnp.int32), (w == n - 1).astype(jnp.int32), section_id, w]).astype(jnp.int32)

    total = pack.shape[0] // shape.blk
    cuts = [0, 9 * q_rows // shape.blk, 18 * q_rows // shape.blk, 36 * q_rows // shape.blk, total]
    bounds = list(zip(cuts[:-1], cuts[1:], strict=True))

    def permute(value, source, target, move):
        if source == target:
            return within(value, move)
        pairs = [
            (s * n + i, (s + target - source) % n_section * n + move(i)) for s in range(n_section) for i in range(n)
        ]
        return lax.ppermute(value, ("section", "space"), pairs)

    def within(value, move):
        pairs = [(s * n + i, s * n + move(i)) for s in range(n_section) for i in range(n)]
        return lax.ppermute(value, ("section", "space"), pairs)

    def to_outer(i):
        return (i + 1) % n if i % 2 else (i - 1) % n

    def ahead(i):
        return (i - 2) % n if i % 2 else (i + 2) % n

    def across(i):
        return (i + 4) % n

    def partner(i):
        return i ^ 1

    def sums_of(tail, count):
        tail = tail.astype(F32)
        rows = [tail[i : i + 1] + tail[i + 1 : i + 2] + tail[i + 2 : i + 3] for i in range(0, 3 * count, 3)]
        return jnp.concatenate(rows + [jnp.zeros((8 - count, tail.shape[1]), F32)], 0)

    def exchange(made, source, target, with_stats=True, count=2):
        block, outer, inner, own = made
        if source != target:
            block = permute(block, source, target, lambda i: i)
            rows, size = block.shape[0] - TAIL, inner.shape[0]
            top, bottom, tail = block[:size], block[rows - size : rows], block[rows:]
            outer = jnp.concatenate([jnp.where(flags[0] == 0, top, bottom), tail], 0)
            inner = jnp.where(flags[0] == 0, bottom, top)
            own = sums_of(tail, count)
        stats = own
        outer = permute(outer, target, target, to_outer)
        inner = permute(inner, target, target, partner)
        if not with_stats:
            return block, outer, inner
        if n == 8:
            b = permute(stats, target, target, ahead)
            c = permute(stats, target, target, across)
            mine = own + sums_of(outer[-TAIL:], count) + b + c
            other = permute(mine, target, target, partner)
        else:
            mine = lax.psum(own, "space")
            other = jnp.zeros_like(mine)
        return block, outer, inner, mine, other

    def after(value, *deps):
        return lax.optimization_barrier((value,) + deps)[0]

    pieces = {}
    packed = []
    if n == 8:
        packed = pack_blocks(shape, pack.T, bounds[:1])

    def send(number, *deps):
        low, high = bounds[number]
        if n == 8:
            got = [after(packed[number], *deps)]
            for k in range(1, 3 if number in RELAYED else 4):
                got.append(within(got[0], lambda i, k=k: i ^ (2 * k)))
            return got
        got = lax.all_gather(pack[low * shape.blk : high * shape.blk], "space")
        got = got.reshape(shape.m, n // shape.m, high - low, shape.blk, -1).transpose(0, 1, 4, 2, 3)
        got = got.reshape(shape.m, shape.cols_of, high - low, shape.blk)
        got = jnp.pad(got, ((0, 0), (0, 0), (0, 0), (0, shape.lanes - shape.blk)))
        return list(got.reshape(shape.m, shape.cols_of, -1))

    def relay(got, *deps):
        if n != 8:
            return []
        half = got[1].shape[1] // 2
        first, second = after((got[1][:, :half], got[2][:, half:]), *deps)
        made = []
        for k, part in ((2, first), (1, second)):
            made.append(within(part, lambda i, k=k: i ^ (2 * k)))
        return made

    def share(number, got, first=0):
        low, high = bounds[number]
        middle = (low + high) // 2
        spans = [(low, high)] * len(got) if n != 8 or first == 0 else [(low, middle), (middle, high)]
        mine = pieces.setdefault(number, [])
        for place, (part, span) in enumerate(zip(got, spans, strict=True)):
            if n == 8:
                j = min(first + place, 3)
                mine.append((part, lambda flags, j=j: ((flags[4] // 2) ^ j) * 2 + flags[0]) + span)
                mine.append((within(part, partner), lambda flags, j=j: ((flags[4] // 2) ^ j) * 2 + 1 - flags[0]) + span)
            else:
                mine.append((part, lambda flags, j=place: j) + span)

    def weights(start, c_in, c_out, extra=0):
        first = start // shape.blk
        end = (start + 9 * c_in * c_out // shape.wide) // shape.blk
        used = [e for number in sorted(pieces) for e in pieces[number] if e[2] < end + extra and e[3] > first]
        return Weights(shape, [e[1:] for e in used], start, c_in, c_out), [e[0] for e in used]

    narrow, wide = shape.narrow, shape.wide
    x = features[0].reshape(shape.rows, shape.half, 2, narrow).transpose(0, 2, 1, 3).reshape(-1, narrow)
    ready = prepare(shape, flags, x, 1)
    sent = send(0, ready[3])
    if n == 8:
        packed += pack_blocks(shape, after(pack.T, sent[0]), bounds[1:])
    first = exchange(ready, 0, 0)
    sent = after(sent, first[3])
    share(0, sent)
    sent = send(1, sent)
    first = (after(first[0], sent[0]),) + first[1:]
    hidden = fine_conv(shape, flags, *weights(0, narrow, narrow), first, 1, 0, 2)
    second = exchange(hidden, 0, 0)
    sent = after(sent, second[3])
    share(1, sent)
    sent = send(2, sent)
    second = (after(second[0], sent[0]),) + second[1:]
    (skip,) = fine_conv(shape, flags, *weights(9 * q_rows, narrow, narrow), second, 2, 1, 0, residual=first[:3])
    sent = after(sent, skip)
    opposite = relay(sent)
    share(2, sent)
    share(2, opposite, 3)
    sent = send(3, sent)
    skip = after(skip, sent[0])
    coarse = down_conv(shape, flags, *weights(18 * q_rows, narrow, wide), skip, 1)
    for section in (1, 2):
        got = exchange(coarse, section - 1, section)
        if section == 1:
            opposite = relay(sent, got[3])
            skip, got = lax.optimization_barrier((skip, got))
            skip = permute(skip, 0, n_section - 1, lambda i: i)
        hidden = coarse_conv(shape, flags, *weights(0, wide, wide), got, 1)
        if section == 1:
            share(3, after(sent, hidden[3]))
            hidden, skip = lax.optimization_barrier((hidden, skip))
        then = exchange(hidden, section, section)
        if section == 1:
            share(3, after(opposite, then[3]), 3)
        coarse = coarse_conv(shape, flags, *weights(36 * q_rows, wide, wide), then, 1, residual=got[0])
    got = exchange(coarse, 2, 3, with_stats=False)
    up = up_conv(shape, flags, *weights(0, wide, narrow), got, skip, 1)
    got = exchange(up, 3, 3, count=4)
    hidden = join_conv(shape, flags, *weights(18 * q_rows, wide, narrow), got, skip, 1)
    then = exchange(hidden, 3, 3)
    outs = last_conv(
        shape, flags, *weights(36 * q_rows, narrow, narrow, 1), then, got[0], skip, 45 * q_rows, n_section
    )
    result = outs[3]
    for target in range(3):
        result = jnp.where(section_id == target, permute(outs[target], 3, target, lambda i: i), result)
    quarter = shape.half // n_section
    result = result.reshape(shape.rows, 2, quarter, narrow).transpose(0, 2, 1, 3)
    return result.reshape(1, shape.rows, 2 * quarter, narrow)


def solution(mesh):
    n, n_section = mesh.shape["space"], mesh.shape["section"]

    def body(features, section_packs):
        return shards(n, n_section, features, section_packs)

    return jax.shard_map(
        body,
        mesh=mesh,
        in_specs=(P(None, "space", None, None), P("section", None, "space")),
        out_specs=P(None, "space", "section", None),
        check_vma=False,
    )
```

```python
import math

import jax
import jax.numpy as jnp
from jax import lax
from jax.experimental import pallas as pl
from jax.experimental.pallas import tpu as pltpu
from jax.sharding import PartitionSpec as P


GROUPS = 32
EPSILON = 1e-05
TAIL = 16
RELAYED = (2, 3)
BF16 = jnp.bfloat16
F32 = jnp.float32


def row_stack(rows, count, width):
    ids = lax.broadcasted_iota(jnp.int32, (count, width), 0)
    total = jnp.zeros((count, width), F32)
    for place, row in enumerate(rows):
        total = jnp.where(ids == place, row, total)
    return total


def bf16_terms(row):
    high = row.astype(BF16).astype(F32)
    rest = row - high
    mid = rest.astype(BF16).astype(F32)
    return [high, mid, (rest - mid).astype(BF16).astype(F32)]


def moments_of(value):
    return [
        jnp.sum(value, axis=0, keepdims=True),
        jnp.sum(value * value, axis=0, keepdims=True),
    ]


def group_terms(sums, count):
    width = sums.shape[1]
    size = width // GROUPS
    terms = row_stack(bf16_terms(sums[0:1]) + bf16_terms(sums[1:2]), 16, width).astype(BF16)
    left = lax.broadcasted_iota(jnp.int32, (width, width), 0) // size
    right = lax.broadcasted_iota(jnp.int32, (width, width), 1) // size
    together = jnp.where(left == right, 1.0, 0.0).astype(BF16)
    summed = jnp.dot(terms, together, preferred_element_type=F32) * (1.0 / (count * size))
    mean = summed[0:1] + summed[1:2] + summed[2:3]
    square = summed[3:4] + summed[4:5] + summed[5:6]
    variance = jnp.maximum(square - mean * mean, 0.0)
    return mean, lax.rsqrt(variance + EPSILON)


def silu(z):
    half = 0.5 * z
    return half + half * jnp.tanh(half)


def parity_matrix(width):
    source = lax.broadcasted_iota(jnp.int32, (width, width), 0)
    target = lax.broadcasted_iota(jnp.int32, (width, width), 1)
    half = width // 2
    wanted = jnp.where(target < half, 2 * target, 2 * (target - half) + 1)
    return jnp.where(source == wanted, 1.0, 0.0).astype(BF16)


def shifted(value, step):
    rows = value.shape[0]
    ids = lax.broadcasted_iota(jnp.int32, value.shape, 0)
    if step == 1:
        return jnp.where(ids == 0, 0.0, pltpu.roll(value, 1, 0))
    return jnp.where(ids == rows - 1, 0.0, pltpu.roll(value, rows - 1, 0))


class Shape:
    def __init__(self, features, n):
        self.rows = features.shape[1]
        self.cols = features.shape[2]
        self.half = self.cols // 2
        self.narrow = features.shape[3]
        self.wide = 2 * self.narrow
        self.m = min(n, 8)
        self.cols_of = self.wide // self.m
        self.blk = 3 * self.narrow // 2
        self.lanes = -(-self.blk // 128) * 128
        self.fine_count = self.rows * n * self.cols
        self.coarse_count = self.fine_count // 4


def emit(flags, out_ref, outer_ref, inner_ref, stats_ref, keep, rows, width, sums):
    channels = out_ref.shape[1]
    core0 = flags[0] == 0
    tail = row_stack([term for row in sums for term in bf16_terms(row)], TAIL, channels).astype(BF16)
    out_ref[rows * width :, :] = tail
    stats_ref[...] = row_stack(sums, 8, channels)
    size = keep * width
    first = out_ref[0:size, :].astype(F32)
    last = out_ref[(rows - keep) * width : rows * width, :].astype(F32)
    outer_ref[0:size, :] = jnp.where(core0, first, last).astype(BF16)
    outer_ref[size:, :] = tail
    inner_ref[...] = jnp.where(core0, last, first).astype(BF16)


def ext_row(index, block_ref, outer_ref, inner_ref, flags, rows, halo, width):
    if index < halo:
        span = slice(index * width, (index + 1) * width)
        pick = jnp.where(flags[0] == 0, outer_ref[span, :].astype(F32), inner_ref[span, :].astype(F32))
        return pick, flags[1] != 0
    index -= halo
    if index < rows:
        return block_ref[index * width : (index + 1) * width, :].astype(F32), None
    index -= rows
    span = slice(index * width, (index + 1) * width)
    pick = jnp.where(flags[0] == 0, inner_ref[span, :].astype(F32), outer_ref[span, :].astype(F32))
    return pick, flags[2] != 0


def masked(value, outside):
    if outside is None:
        return value
    return jnp.where(outside, 0.0, value)


class Weights:
    def __init__(self, shape, entries, start, c_in, c_out):
        self.shape = shape
        self.c_in = c_in
        self.c_out = c_out
        self.split = c_out != shape.wide
        self.blocks = 3 * c_in * c_out // shape.wide // shape.blk
        self.start = start // shape.blk
        self.entries = entries
        self.depth = self.blocks * shape.lanes
        self.width = (2 if self.split else 1) * self.depth

    def copies(self, flags, refs, buffer, sems):
        made = []
        lanes = self.shape.lanes
        for dy in range(3):
            mine = []
            begin = self.start + dy * self.blocks
            for ref, (owner, low, high) in zip(refs, self.entries, strict=True):
                a, b = max(begin, low), min(begin + self.blocks, high)
                if a < b:
                    mine.append(
                        pltpu.make_async_copy(
                            ref.at[:, (a - low) * lanes : (b - low) * lanes],
                            self.slot(buffer.at[dy], owner(flags), a - begin, b - begin),
                            sems.at[dy],
                        )
                    )
            made.append(mine)
        return made

    def slot(self, target, owner, first, last):
        lanes = self.shape.lanes
        if not self.split:
            return target.at[owner, :, first * lanes : last * lanes]
        half = self.shape.m // 2
        shift = pl.multiple_of(owner // half * self.depth, lanes)
        return target.at[owner % half, :, pl.ds(first * lanes + shift, (last - first) * lanes)]

    def product(self, left, buffer, dy):
        right = buffer[dy].reshape(self.c_out, self.width)
        return lax.dot_general(left, right, (((1,), (1,)), ((), ())), preferred_element_type=F32)

    def put(self, image, row, place, tap, value, first=0, channels=None):
        shape = self.shape
        size = value.shape[0]
        half = self.c_in // 2
        runs = []
        if self.split:
            c = value.shape[1] // 2
            runs = [(odd, tap * half + first // 2, odd * c, c) for odd in range(2)]
        else:
            runs = [(0, tap * self.c_in + first, 0, value.shape[1])]
        for odd, index, at, left in runs:
            while left > 0:
                step = min(left, shape.blk - index % shape.blk)
                lane = odd * self.depth + index // shape.blk * shape.lanes + index % shape.blk
                image[row, place : place + size, lane : lane + step] = value[:, at : at + step]
                index, at, left = index + step, at + step, left - step

    def clear(self, image):
        shape = self.shape
        for block in range(self.width // shape.lanes):
            begin = block * shape.lanes + shape.blk
            end = (block + 1) * shape.lanes
            image[:, :, begin:end] = jnp.zeros((image.shape[0], image.shape[1], end - begin), BF16)


def fine_columns(store, row, even, odd):
    half = even.shape[0]
    store(row, 0, half, 0, shifted(odd, 1))
    store(row, 0, half, 1, even)
    store(row, 0, half, 2, odd)
    store(row, half, half, 0, even)
    store(row, half, half, 1, odd)
    store(row, half, half, 2, shifted(even, -1))


def run_conv(weights, buffer, image, acc, sems, rows, width, begin=lambda dy: dy):
    acc[...] = jnp.zeros(acc.shape, F32)

    def step(dy, carry):
        pltpu.make_async_copy(buffer.at[dy], buffer.at[dy], sems.at[dy]).wait()
        left = image[pl.ds(begin(dy), rows)].reshape(rows * width, weights.width)
        acc[...] += weights.product(left, buffer, dy)
        return carry

    lax.fori_loop(0, 3, step, 0)


def scratch_of(weights, image_rows, out_rows, width, extra=()):
    return [
        pltpu.VMEM((3, weights.c_out // weights.shape.cols_of, weights.shape.cols_of, weights.width), BF16),
        pltpu.VMEM((image_rows, width, weights.width), BF16),
        pltpu.VMEM((out_rows * width, weights.c_out), F32),
        pltpu.SemaphoreType.DMA((3,)),
    ] + list(extra)


def call(body, n_smem, n_vmem, n_any, outs, scratch, flops, limit=60 * 1024 * 1024):
    specs = (
        [pl.BlockSpec(memory_space=pltpu.SMEM)] * n_smem
        + [pl.BlockSpec(memory_space=pltpu.VMEM)] * n_vmem
        + [pl.BlockSpec(memory_space=pltpu.HBM)] * n_any
    )
    return pl.pallas_call(
        body,
        out_shape=[jax.ShapeDtypeStruct(s, d) for s, d in outs],
        in_specs=specs,
        out_specs=[pl.BlockSpec(memory_space=pltpu.VMEM)] * len(outs),
        scratch_shapes=scratch,
        compiler_params=pltpu.CompilerParams(vmem_limit_bytes=limit),
        cost_estimate=pl.CostEstimate(flops=flops, bytes_accessed=4_000_000, transcendentals=0),
    )


def message_outs(rows, width, channels, keep):
    return [
        ((rows * width + TAIL, channels), BF16),
        ((keep * width + TAIL, channels), BF16),
        ((keep * width, channels), BF16),
        ((8, channels), F32),
    ]


def prepare(shape, flags, x, keep):
    rows, width, c = shape.rows, shape.cols, shape.narrow

    def body(flags, x_ref, out_ref, outer_ref, inner_ref, stats_ref):
        out_ref[0 : rows * width, :] = x_ref[...]
        sums = moments_of(x_ref[...].astype(F32))
        emit(flags, out_ref, outer_ref, inner_ref, stats_ref, keep, rows, width, sums)

    return call(body, 1, 1, 0, message_outs(rows, width, c, keep), [], 1000)(flags, x)


def fine_conv(shape, flags, weights, pieces, got, halo, out_halo, keep, residual=None):
    rows, width, half, c = shape.rows, shape.cols, shape.half, shape.narrow
    out_rows = rows + 2 * out_halo
    image_rows = out_rows + 2
    n_pieces = len(pieces)
    extra = 0 if residual is None else 3

    def body(flags, block, outer, inner, sa, sb, *rest):
        res = rest[:extra]
        piece_refs = rest[extra : extra + n_pieces]
        rest = rest[extra + n_pieces :]
        outs = rest[:-4]
        buffer, image, acc, sems = rest[-4:]
        copies = weights.copies(flags, piece_refs, buffer, sems)
        for mine in copies:
            for copy in mine:
                copy.start()
        weights.clear(image)
        mean, inv = group_terms(sa[...] + sb[...], shape.fine_count)
        mix = parity_matrix(c)

        def store(row, place, size, tap, value):
            weights.put(image, row, place, tap, value.astype(BF16))

        for row in range(image_rows):
            value, outside = ext_row(row + halo - out_halo - 1, block, outer, inner, flags, rows, halo, width)
            value = masked(silu((value - mean) * inv), outside).astype(BF16)
            value = jnp.dot(value, mix, preferred_element_type=F32)
            fine_columns(store, row, value[:half], value[half:])
        run_conv(weights, buffer, image, acc, sems, out_rows, width)
        scale = 1.0 / math.sqrt(9 * c)
        if residual is None:
            out_ref, outer_ref, inner_ref, stats_ref = outs
            value = (acc[...] * scale).astype(BF16)
            out_ref[0 : rows * width, :] = value
            emit(flags, out_ref, outer_ref, inner_ref, stats_ref, keep, rows, width, moments_of(value.astype(F32)))
        else:
            (out_ref,) = outs
            for row in range(out_rows):
                own, _ = ext_row(row, res[0], res[1], res[2], flags, rows, out_halo, width)
                span = slice(row * width, (row + 1) * width)
                out_ref[span, 0:c] = (own + acc[span, :] * scale).astype(BF16)
                out_ref[span, c:] = jnp.zeros((width, out_ref.shape[1] - c), BF16)

    outs = message_outs(rows, width, c, keep) if residual is None else [((out_rows * width, -(-c // 128) * 128), BF16)]
    args = (flags,) + tuple(got) + (() if residual is None else tuple(residual)) + tuple(pieces)
    flops = 2 * out_rows * width * 9 * c * c
    return call(body, 1, 5 + extra, n_pieces, outs, scratch_of(weights, image_rows, out_rows, width), flops)(*args)


def down_conv(shape, flags, weights, pieces, skip, keep):
    rows, width, half, c = shape.rows, shape.cols, shape.half, shape.narrow
    out_rows = rows // 2

    def body(flags, skip_ref, *rest):
        piece_refs = rest[: len(pieces)]
        outs = rest[len(pieces) : -4]
        buffer, image, acc, sems = rest[-4:]
        copies = weights.copies(flags, piece_refs, buffer, sems)
        for mine in copies:
            for copy in mine:
                copy.start()
        weights.clear(image)
        for row in range(rows + 1):
            value = skip_ref[row * width : (row + 1) * width, 0:c].astype(F32)
            if row == 0:
                value = masked(value, flags[1] != 0)
            even, odd = value[:half], value[half:]
            place = (row % 2) * (out_rows + 1) + row // 2
            weights.put(image, place, 0, 0, shifted(odd, 1).astype(BF16))
            weights.put(image, place, 0, 1, even.astype(BF16))
            weights.put(image, place, 0, 2, odd.astype(BF16))

        def begin(dy):
            return jnp.where(dy == 1, out_rows + 1, dy // 2)

        run_conv(weights, buffer, image, acc, sems, out_rows, half, begin)
        out_ref, outer_ref, inner_ref, stats_ref = outs
        value = (acc[...] * (1.0 / math.sqrt(9 * c))).astype(BF16)
        out_ref[0 : out_rows * half, :] = value
        emit(flags, out_ref, outer_ref, inner_ref, stats_ref, keep, out_rows, half, moments_of(value.astype(F32)))

    scratch = scratch_of(weights, 2 * (out_rows + 1), out_rows, half)
    outs = message_outs(out_rows, half, shape.wide, keep)
    return call(body, 1, 1, len(pieces), outs, scratch, 2 * out_rows * half * 9 * c * shape.wide)(flags, skip, *pieces)


def coarse_conv(shape, flags, weights, pieces, got, keep, residual=None):
    rows, width, c = shape.rows // 2, shape.half, shape.wide
    extra = 0 if residual is None else 1

    def body(flags, block, outer, inner, sa, sb, *rest):
        res = rest[:extra]
        piece_refs = rest[extra : extra + len(pieces)]
        outs = rest[extra + len(pieces) : -4]
        buffer, image, acc, sems = rest[-4:]
        copies = weights.copies(flags, piece_refs, buffer, sems)
        for mine in copies:
            for copy in mine:
                copy.start()
        weights.clear(image)
        mean, inv = group_terms(sa[...] + sb[...], shape.coarse_count)
        for row in range(rows + 2):
            value, outside = ext_row(row, block, outer, inner, flags, rows, 1, width)
            value = masked(silu((value - mean) * inv), outside)
            weights.put(image, row, 0, 0, shifted(value, 1).astype(BF16))
            weights.put(image, row, 0, 1, value.astype(BF16))
            weights.put(image, row, 0, 2, shifted(value, -1).astype(BF16))
        run_conv(weights, buffer, image, acc, sems, rows, width)
        out_ref, outer_ref, inner_ref, stats_ref = outs
        value = acc[...] * (1.0 / math.sqrt(9 * c))
        if residual is not None:
            value = res[0][0 : rows * width, :].astype(F32) + value
        value = value.astype(BF16)
        out_ref[0 : rows * width, :] = value
        emit(flags, out_ref, outer_ref, inner_ref, stats_ref, keep, rows, width, moments_of(value.astype(F32)))

    args = (flags,) + tuple(got) + (() if residual is None else (residual,)) + tuple(pieces)
    outs = message_outs(rows, width, c, keep)
    flops = 2 * rows * width * 9 * c * c
    return call(body, 1, 5 + extra, len(pieces), outs, scratch_of(weights, rows + 2, rows, width), flops)(*args)


def up_conv(shape, flags, weights, pieces, got, skip, keep):
    rows, width, half = shape.rows, shape.cols, shape.half
    c, c_out = shape.wide, shape.narrow

    def body(flags, block, outer, inner, skip_ref, *rest):
        piece_refs = rest[: len(pieces)]
        outs = rest[len(pieces) : -4]
        buffer, image, acc, sems = rest[-4:]
        copies = weights.copies(flags, piece_refs, buffer, sems)
        for mine in copies:
            for copy in mine:
                copy.start()
        weights.clear(image)
        mix = parity_matrix(c)
        for row in range(rows // 2 + 2):
            value, outside = ext_row(row, block, outer, inner, flags, rows // 2, 1, half)
            value = masked(value, outside).astype(BF16)
            value = jnp.dot(value, mix, preferred_element_type=F32)
            before, after = shifted(value, 1).astype(BF16), shifted(value, -1).astype(BF16)
            value = value.astype(BF16)
            for fine in (2 * row - 1, 2 * row):
                if 0 <= fine < rows + 2:
                    for tap, (even, odd) in enumerate(((before, value), (value, value), (value, after))):
                        weights.put(image, fine, 0, tap, even)
                        weights.put(image, fine, half, tap, odd)
        run_conv(weights, buffer, image, acc, sems, rows, width)
        out_ref, outer_ref, inner_ref, stats_ref = outs
        value = (acc[...] * (1.0 / math.sqrt(9 * c))).astype(BF16)
        out_ref[0 : rows * width, :] = value
        own = skip_ref[width : (rows + 1) * width, 0:c_out].astype(F32)
        sums = moments_of(value.astype(F32)) + moments_of(own)
        emit(flags, out_ref, outer_ref, inner_ref, stats_ref, keep, rows, width, sums)

    outs = message_outs(rows, width, c_out, keep)
    flops = 2 * rows * width * 9 * c * c_out
    scratch = scratch_of(weights, rows + 2, rows, width)
    return call(body, 1, 4, len(pieces), outs, scratch, flops)(flags, *got, skip, *pieces)


def join_conv(shape, flags, weights, pieces, got, skip, keep):
    rows, width, half, c = shape.rows, shape.cols, shape.half, shape.narrow

    def body(flags, block, outer, inner, sa, sb, skip_ref, *rest):
        piece_refs = rest[: len(pieces)]
        outs = rest[len(pieces) : -4]
        buffer, image, acc, sems = rest[-4:]
        copies = weights.copies(flags, piece_refs, buffer, sems)
        for mine in copies:
            for copy in mine:
                copy.start()
        weights.clear(image)
        mix = parity_matrix(c)
        for part in range(2):
            sums = sa[...] + sb[...]
            mean, inv = pair_terms(sums[2 * part : 2 * part + 2], shape.fine_count)

            def store(row, place, size, tap, value, part=part):
                weights.put(image, row, place, tap, value.astype(BF16), first=part * c)

            for row in range(rows + 2):
                if part == 0:
                    value, outside = ext_row(row, block, outer, inner, flags, rows, 1, width)
                else:
                    value = skip_ref[row * width : (row + 1) * width, 0:c].astype(F32)
                    outside = flags[1] != 0 if row == 0 else flags[2] != 0 if row == rows + 1 else None
                value = masked(silu((value - mean) * inv), outside).astype(BF16)
                value = jnp.dot(value, mix, preferred_element_type=F32)
                fine_columns(store, row, value[:half], value[half:])
        run_conv(weights, buffer, image, acc, sems, rows, width)
        out_ref, outer_ref, inner_ref, stats_ref = outs
        value = (acc[...] * (1.0 / math.sqrt(18 * c))).astype(BF16)
        out_ref[0 : rows * width, :] = value
        emit(flags, out_ref, outer_ref, inner_ref, stats_ref, keep, rows, width, moments_of(value.astype(F32)))

    outs = message_outs(rows, width, c, keep)
    flops = 2 * rows * width * 18 * c * c
    scratch = scratch_of(weights, rows + 2, rows, width)
    return call(body, 1, 6, len(pieces), outs, scratch, flops)(flags, *got, skip, *pieces)


def pair_terms(sums, count):
    width = sums.shape[1]
    size = 2 * width // GROUPS
    terms = row_stack(bf16_terms(sums[0:1]) + bf16_terms(sums[1:2]), 16, width).astype(BF16)
    left = lax.broadcasted_iota(jnp.int32, (width, width), 0) // size
    right = lax.broadcasted_iota(jnp.int32, (width, width), 1) // size
    together = jnp.where(left == right, 1.0, 0.0).astype(BF16)
    summed = jnp.dot(terms, together, preferred_element_type=F32) * (1.0 / (count * size))
    mean = summed[0:1] + summed[1:2] + summed[2:3]
    square = summed[3:4] + summed[4:5] + summed[5:6]
    variance = jnp.maximum(square - mean * mean, 0.0)
    return mean, lax.rsqrt(variance + EPSILON)


def last_conv(shape, flags, weights, pieces, got, u, skip, j_start, n_quarters):
    rows, width, half, c = shape.rows, shape.cols, shape.half, shape.narrow
    quarter = half // n_quarters
    j_block = j_start // shape.blk

    def body(flags, block, outer, inner, sa, sb, u_ref, skip_ref, *rest):
        piece_refs = rest[: len(pieces)]
        outs = rest[len(pieces) : -6]
        buffer, image, acc, sems, jbuf, jsem = rest[-6:]
        copies = weights.copies(flags, piece_refs, buffer, sems)
        for mine in copies:
            for copy in mine:
                copy.start()
        weights.clear(image)
        for ref, (owner, low, high) in zip(piece_refs, weights.entries, strict=True):
            if low <= j_block < high:
                pltpu.make_async_copy(
                    ref.at[:, (j_block - low) * shape.lanes : (j_block - low + 1) * shape.lanes],
                    jbuf.at[owner(flags)],
                    jsem,
                ).start()
        mean, inv = group_terms(sa[...] + sb[...], shape.fine_count)
        mix = parity_matrix(c)

        def store(row, place, size, tap, value):
            weights.put(image, row, place, tap, value.astype(BF16))

        for row in range(rows + 2):
            value, outside = ext_row(row, block, outer, inner, flags, rows, 1, width)
            value = masked(silu((value - mean) * inv), outside).astype(BF16)
            value = jnp.dot(value, mix, preferred_element_type=F32)
            fine_columns(store, row, value[:half], value[half:])
        run_conv(weights, buffer, image, acc, sems, rows, width)
        pltpu.make_async_copy(jbuf, jbuf, jsem).wait()
        right = jbuf[...].reshape(2 * c, shape.lanes)
        left = [u_ref[0 : rows * width, :], skip_ref[width : (rows + 1) * width, 0:c]]
        left = [jnp.dot(part, mix, preferred_element_type=F32).astype(BF16) for part in left]
        made = jnp.zeros((rows * width, c), F32)
        for odd in range(2):
            mine = jnp.concatenate(
                [part[:, odd * (c // 2) : (odd + 1) * (c // 2)] for part in left]
                + [jnp.zeros((rows * width, shape.lanes - c), BF16)],
                axis=1,
            )
            made += lax.dot_general(
                mine, right[odd * c : (odd + 1) * c], (((1,), (1,)), ((), ())), preferred_element_type=F32
            )
        value = made * (1.0 / math.sqrt(2 * c)) + acc[...] * (1.0 / math.sqrt(9 * c))
        value = value.reshape(2 * rows, half, c).astype(BF16)
        for q, out in enumerate(outs):
            out[...] = value[:, q * quarter : (q + 1) * quarter, :]

    outs = [((2 * rows, quarter, c), BF16)] * n_quarters
    flops = 2 * rows * width * 11 * c * c
    extra = [pltpu.VMEM((shape.m, shape.cols_of, shape.lanes), BF16), pltpu.SemaphoreType.DMA(())]
    scratch = scratch_of(weights, rows + 2, rows, width, extra)
    return call(body, 1, 7, len(pieces), outs, scratch, flops)(flags, *got, u, skip, *pieces)


def pack_blocks(shape, pack, bounds):
    columns = pack.shape[0]
    first = bounds[0][0] * shape.blk // 128 * 128
    last = min(-(-bounds[-1][1] * shape.blk // 128) * 128, pack.shape[1])

    def body(pack_ref, *rest):
        outs, (rows, sem) = rest[:-2], rest[-2:]
        copy = pltpu.make_async_copy(pack_ref.at[:, first:last], rows, sem)
        copy.start()
        copy.wait()
        for (low, high), out_ref in zip(bounds, outs, strict=True):
            for block in range(high - low):
                begin, end = block * shape.lanes, (block + 1) * shape.lanes
                at = (low + block) * shape.blk - first
                out_ref[:, begin : begin + shape.blk] = rows[:, at : at + shape.blk]
                out_ref[:, begin + shape.blk : end] = jnp.zeros((columns, shape.lanes - shape.blk), BF16)

    scratch = [pltpu.VMEM((columns, last - first), BF16), pltpu.SemaphoreType.DMA(())]
    outs = [((columns, (high - low) * shape.lanes), BF16) for low, high in bounds]
    return call(body, 0, 0, 1, outs, scratch, 1000)(pack)


def shards(n, n_section, features, section_packs):
    section_id = lax.axis_index("section")
    w = lax.axis_index("space")
    shape = Shape(features, n)
    q_rows = shape.narrow * shape.narrow // shape.wide
    pack = section_packs[0]
    flags = jnp.stack([w % 2, (w == 0).astype(jnp.int32), (w == n - 1).astype(jnp.int32), section_id, w]).astype(jnp.int32)

    total = pack.shape[0] // shape.blk
    cuts = [0, 9 * q_rows // shape.blk, 18 * q_rows // shape.blk, 36 * q_rows // shape.blk, total]
    bounds = list(zip(cuts[:-1], cuts[1:], strict=True))

    def permute(value, source, target, move):
        if source == target:
            return within(value, move)
        pairs = [
            (s * n + i, (s + target - source) % n_section * n + move(i)) for s in range(n_section) for i in range(n)
        ]
        return lax.ppermute(value, ("section", "space"), pairs)

    def within(value, move):
        pairs = [(s * n + i, s * n + move(i)) for s in range(n_section) for i in range(n)]
        return lax.ppermute(value, ("section", "space"), pairs)

    def to_outer(i):
        return (i + 1) % n if i % 2 else (i - 1) % n

    def ahead(i):
        return (i - 2) % n if i % 2 else (i + 2) % n

    def across(i):
        return (i + 4) % n

    def partner(i):
        return i ^ 1

    def sums_of(tail, count):
        tail = tail.astype(F32)
        rows = [tail[i : i + 1] + tail[i + 1 : i + 2] + tail[i + 2 : i + 3] for i in range(0, 3 * count, 3)]
        return jnp.concatenate(rows + [jnp.zeros((8 - count, tail.shape[1]), F32)], 0)

    def exchange(made, source, target, with_stats=True, count=2):
        block, outer, inner, own = made
        if source != target:
            block = permute(block, source, target, lambda i: i)
            rows, size = block.shape[0] - TAIL, inner.shape[0]
            top, bottom, tail = block[:size], block[rows - size : rows], block[rows:]
            outer = jnp.concatenate([jnp.where(flags[0] == 0, top, bottom), tail], 0)
            inner = jnp.where(flags[0] == 0, bottom, top)
            own = sums_of(tail, count)
        stats = own
        outer = permute(outer, target, target, to_outer)
        inner = permute(inner, target, target, partner)
        if not with_stats:
            return block, outer, inner
        if n == 8:
            b = permute(stats, target, target, ahead)
            c = permute(stats, target, target, across)
            mine = own + sums_of(outer[-TAIL:], count) + b + c
            other = permute(mine, target, target, partner)
        else:
            mine = lax.psum(own, "space")
            other = jnp.zeros_like(mine)
        return block, outer, inner, mine, other

    def after(value, *deps):
        return lax.optimization_barrier((value,) + deps)[0]

    pieces = {}
    packed = []
    if n == 8:
        packed = pack_blocks(shape, pack.T, bounds[:1])

    def send(number, *deps):
        low, high = bounds[number]
        if n == 8:
            got = [after(packed[number], *deps)]
            for k in range(1, 3 if number in RELAYED else 4):
                got.append(within(got[0], lambda i, k=k: i ^ (2 * k)))
            return got
        got = lax.all_gather(pack[low * shape.blk : high * shape.blk], "space")
        got = got.reshape(shape.m, n // shape.m, high - low, shape.blk, -1).transpose(0, 1, 4, 2, 3)
        got = got.reshape(shape.m, shape.cols_of, high - low, shape.blk)
        got = jnp.pad(got, ((0, 0), (0, 0), (0, 0), (0, shape.lanes - shape.blk)))
        return list(got.reshape(shape.m, shape.cols_of, -1))

    def relay(got, *deps):
        if n != 8:
            return []
        half = got[1].shape[1] // 2
        first, second = after((got[1][:, :half], got[2][:, half:]), *deps)
        made = []
        for k, part in ((2, first), (1, second)):
            made.append(within(part, lambda i, k=k: i ^ (2 * k)))
        return made

    def share(number, got, first=0):
        low, high = bounds[number]
        middle = (low + high) // 2
        spans = [(low, high)] * len(got) if n != 8 or first == 0 else [(low, middle), (middle, high)]
        mine = pieces.setdefault(number, [])
        for place, (part, span) in enumerate(zip(got, spans, strict=True)):
            if n == 8:
                j = min(first + place, 3)
                mine.append((part, lambda flags, j=j: ((flags[4] // 2) ^ j) * 2 + flags[0]) + span)
                theirs = within(part, partner)
                mine.append((theirs, lambda flags, j=j: ((flags[4] // 2) ^ j) * 2 + 1 - flags[0]) + span)
            else:
                mine.append((part, lambda flags, j=place: j) + span)

    def weights(start, c_in, c_out, extra=0):
        first = start // shape.blk
        end = (start + 9 * c_in * c_out // shape.wide) // shape.blk
        used = [e for number in sorted(pieces) for e in pieces[number] if e[2] < end + extra and e[3] > first]
        return Weights(shape, [e[1:] for e in used], start, c_in, c_out), [e[0] for e in used]

    narrow, wide = shape.narrow, shape.wide
    x = features[0].reshape(shape.rows, shape.half, 2, narrow).transpose(0, 2, 1, 3).reshape(-1, narrow)
    ready = prepare(shape, flags, x, 1)
    sent = send(0, ready[3])
    if n == 8:
        packed += pack_blocks(shape, after(pack.T, sent[0]), bounds[1:])
    third = send(1)
    fourth = send(2)
    first = exchange(ready, 0, 0)
    share(0, after(sent, first[3]))
    first = (after(first[0], third[0], fourth[0]),) + first[1:]
    hidden = fine_conv(shape, flags, *weights(0, narrow, narrow), first, 1, 0, 2)
    second = exchange(hidden, 0, 0)
    fourth = after(fourth, second[3])
    opposite = relay(fourth)
    sent = send(3, second[3])
    share(1, after(third, second[3]))
    share(2, fourth)
    second = (after(second[0], sent[0]),) + second[1:]
    (skip,) = fine_conv(shape, flags, *weights(9 * q_rows, narrow, narrow), second, 2, 1, 0, residual=first[:3])
    share(2, after(opposite, skip), 3)
    coarse = down_conv(shape, flags, *weights(18 * q_rows, narrow, wide), skip, 1)
    for section in (1, 2):
        got = exchange(coarse, section - 1, section)
        if section == 1:
            opposite = relay(sent, got[3])
            skip, got = lax.optimization_barrier((skip, got))
            skip = permute(skip, 0, n_section - 1, lambda i: i)
        hidden = coarse_conv(shape, flags, *weights(0, wide, wide), got, 1)
        if section == 1:
            share(3, after(sent, hidden[3]))
        then = exchange(hidden, section, section)
        if section == 1:
            share(3, after(opposite, then[3]), 3)
            then, skip = lax.optimization_barrier((then, skip))
        coarse = coarse_conv(shape, flags, *weights(36 * q_rows, wide, wide), then, 1, residual=got[0])
    got = exchange(coarse, 2, 3, with_stats=False)
    up = up_conv(shape, flags, *weights(0, wide, narrow), got, skip, 1)
    got = exchange(up, 3, 3, count=4)
    hidden = join_conv(shape, flags, *weights(18 * q_rows, wide, narrow), got, skip, 1)
    then = exchange(hidden, 3, 3)
    outs = last_conv(
        shape, flags, *weights(36 * q_rows, narrow, narrow, 1), then, got[0], skip, 45 * q_rows, n_section
    )
    result = outs[3]
    for target in range(3):
        pairs = [(3 * n + i, target * n + i) for i in range(n)]
        result = jnp.where(section_id == target, lax.ppermute(outs[target], ("section", "space"), pairs), result)
    quarter = shape.half // n_section
    result = result.reshape(shape.rows, 2, quarter, narrow).transpose(0, 2, 1, 3)
    return result.reshape(1, shape.rows, 2 * quarter, narrow)


def solution(mesh):
    n, n_section = mesh.shape["space"], mesh.shape["section"]

    def body(features, section_packs):
        return shards(n, n_section, features, section_packs)

    return jax.shard_map(
        body,
        mesh=mesh,
        in_specs=(P(None, "space", None, None), P("section", None, "space")),
        out_specs=P(None, "space", "section", None),
        check_vma=False,
    )
```

```python
import math

import jax
import jax.numpy as jnp
from jax import lax
from jax.experimental import pallas as pl
from jax.experimental.pallas import tpu as pltpu
from jax.sharding import PartitionSpec as P


GROUPS = 32
EPSILON = 1e-05
TAIL = 16
RELAYED = (2, 3)
BF16 = jnp.bfloat16
F32 = jnp.float32


def row_stack(rows, count, width):
    ids = lax.broadcasted_iota(jnp.int32, (count, width), 0)
    total = jnp.zeros((count, width), F32)
    for place, row in enumerate(rows):
        total = jnp.where(ids == place, row, total)
    return total


def bf16_terms(row):
    high = row.astype(BF16).astype(F32)
    rest = row - high
    mid = rest.astype(BF16).astype(F32)
    return [high, mid, (rest - mid).astype(BF16).astype(F32)]


def moments_of(value):
    return [
        jnp.sum(value, axis=0, keepdims=True),
        jnp.sum(value * value, axis=0, keepdims=True),
    ]


def group_terms(sums, count):
    width = sums.shape[1]
    size = width // GROUPS
    terms = row_stack(bf16_terms(sums[0:1]) + bf16_terms(sums[1:2]), 16, width).astype(BF16)
    left = lax.broadcasted_iota(jnp.int32, (width, width), 0) // size
    right = lax.broadcasted_iota(jnp.int32, (width, width), 1) // size
    together = jnp.where(left == right, 1.0, 0.0).astype(BF16)
    summed = jnp.dot(terms, together, preferred_element_type=F32) * (1.0 / (count * size))
    mean = summed[0:1] + summed[1:2] + summed[2:3]
    square = summed[3:4] + summed[4:5] + summed[5:6]
    variance = jnp.maximum(square - mean * mean, 0.0)
    return mean, lax.rsqrt(variance + EPSILON)


def silu(z):
    half = 0.5 * z
    return half + half * jnp.tanh(half)


def parity_matrix(width):
    source = lax.broadcasted_iota(jnp.int32, (width, width), 0)
    target = lax.broadcasted_iota(jnp.int32, (width, width), 1)
    half = width // 2
    wanted = jnp.where(target < half, 2 * target, 2 * (target - half) + 1)
    return jnp.where(source == wanted, 1.0, 0.0).astype(BF16)


def shifted(value, step):
    rows = value.shape[0]
    ids = lax.broadcasted_iota(jnp.int32, value.shape, 0)
    if step == 1:
        return jnp.where(ids == 0, 0.0, pltpu.roll(value, 1, 0))
    return jnp.where(ids == rows - 1, 0.0, pltpu.roll(value, rows - 1, 0))


class Shape:
    def __init__(self, features, n):
        self.rows = features.shape[1]
        self.cols = features.shape[2]
        self.half = self.cols // 2
        self.narrow = features.shape[3]
        self.wide = 2 * self.narrow
        self.m = min(n, 8)
        self.cols_of = self.wide // self.m
        self.blk = 3 * self.narrow // 2
        self.lanes = -(-self.blk // 128) * 128
        self.fine_count = self.rows * n * self.cols
        self.coarse_count = self.fine_count // 4


def emit(flags, out_ref, outer_ref, inner_ref, stats_ref, keep, rows, width, sums):
    channels = out_ref.shape[1]
    core0 = flags[0] == 0
    tail = row_stack([term for row in sums for term in bf16_terms(row)], TAIL, channels).astype(BF16)
    out_ref[rows * width :, :] = tail
    stats_ref[...] = row_stack(sums, 8, channels)
    size = keep * width
    first = out_ref[0:size, :].astype(F32)
    last = out_ref[(rows - keep) * width : rows * width, :].astype(F32)
    outer_ref[0:size, :] = jnp.where(core0, first, last).astype(BF16)
    outer_ref[size:, :] = tail
    inner_ref[...] = jnp.where(core0, last, first).astype(BF16)


def ext_row(index, block_ref, outer_ref, inner_ref, flags, rows, halo, width):
    if index < halo:
        span = slice(index * width, (index + 1) * width)
        pick = jnp.where(flags[0] == 0, outer_ref[span, :].astype(F32), inner_ref[span, :].astype(F32))
        return pick, flags[1] != 0
    index -= halo
    if index < rows:
        return block_ref[index * width : (index + 1) * width, :].astype(F32), None
    index -= rows
    span = slice(index * width, (index + 1) * width)
    pick = jnp.where(flags[0] == 0, inner_ref[span, :].astype(F32), outer_ref[span, :].astype(F32))
    return pick, flags[2] != 0


def masked(value, outside):
    if outside is None:
        return value
    return jnp.where(outside, 0.0, value)


class Weights:
    def __init__(self, shape, entries, start, c_in, c_out):
        self.shape = shape
        self.c_in = c_in
        self.c_out = c_out
        self.split = c_out != shape.wide
        self.blocks = 3 * c_in * c_out // shape.wide // shape.blk
        self.start = start // shape.blk
        self.entries = entries
        self.depth = self.blocks * shape.lanes
        self.width = (2 if self.split else 1) * self.depth

    def copies(self, flags, refs, buffer, sems):
        made = []
        lanes = self.shape.lanes
        for dy in range(3):
            mine = []
            begin = self.start + dy * self.blocks
            for ref, (owner, low, high) in zip(refs, self.entries, strict=True):
                a, b = max(begin, low), min(begin + self.blocks, high)
                if a < b:
                    mine.append(
                        pltpu.make_async_copy(
                            ref.at[:, (a - low) * lanes : (b - low) * lanes],
                            self.slot(buffer.at[dy], owner(flags), a - begin, b - begin),
                            sems.at[dy],
                        )
                    )
            made.append(mine)
        return made

    def slot(self, target, owner, first, last):
        lanes = self.shape.lanes
        if not self.split:
            return target.at[owner, :, first * lanes : last * lanes]
        half = self.shape.m // 2
        shift = pl.multiple_of(owner // half * self.depth, lanes)
        return target.at[owner % half, :, pl.ds(first * lanes + shift, (last - first) * lanes)]

    def product(self, left, buffer, dy):
        right = buffer[dy].reshape(self.c_out, self.width)
        return lax.dot_general(left, right, (((1,), (1,)), ((), ())), preferred_element_type=F32)

    def put(self, image, row, place, tap, value, first=0, channels=None):
        shape = self.shape
        size = value.shape[0]
        half = self.c_in // 2
        runs = []
        if self.split:
            c = value.shape[1] // 2
            runs = [(odd, tap * half + first // 2, odd * c, c) for odd in range(2)]
        else:
            runs = [(0, tap * self.c_in + first, 0, value.shape[1])]
        for odd, index, at, left in runs:
            while left > 0:
                step = min(left, shape.blk - index % shape.blk)
                lane = odd * self.depth + index // shape.blk * shape.lanes + index % shape.blk
                image[row, place : place + size, lane : lane + step] = value[:, at : at + step]
                index, at, left = index + step, at + step, left - step

    def clear(self, image):
        shape = self.shape
        for block in range(self.width // shape.lanes):
            begin = block * shape.lanes + shape.blk
            end = (block + 1) * shape.lanes
            image[:, :, begin:end] = jnp.zeros((image.shape[0], image.shape[1], end - begin), BF16)


def fine_columns(store, row, even, odd):
    half = even.shape[0]
    store(row, 0, half, 0, shifted(odd, 1))
    store(row, 0, half, 1, even)
    store(row, 0, half, 2, odd)
    store(row, half, half, 0, even)
    store(row, half, half, 1, odd)
    store(row, half, half, 2, shifted(even, -1))


def run_conv(weights, buffer, image, acc, sems, rows, width, begin=lambda dy: dy):
    acc[...] = jnp.zeros(acc.shape, F32)

    def step(dy, carry):
        pltpu.make_async_copy(buffer.at[dy], buffer.at[dy], sems.at[dy]).wait()
        left = image[pl.ds(begin(dy), rows)].reshape(rows * width, weights.width)
        acc[...] += weights.product(left, buffer, dy)
        return carry

    lax.fori_loop(0, 3, step, 0)


def scratch_of(weights, image_rows, out_rows, width, extra=()):
    return [
        pltpu.VMEM((3, weights.c_out // weights.shape.cols_of, weights.shape.cols_of, weights.width), BF16),
        pltpu.VMEM((image_rows, width, weights.width), BF16),
        pltpu.VMEM((out_rows * width, weights.c_out), F32),
        pltpu.SemaphoreType.DMA((3,)),
    ] + list(extra)


def call(body, n_smem, n_vmem, n_any, outs, scratch, flops, limit=53 * 1024 * 1024):
    specs = (
        [pl.BlockSpec(memory_space=pltpu.SMEM)] * n_smem
        + [pl.BlockSpec(memory_space=pltpu.VMEM)] * n_vmem
        + [pl.BlockSpec(memory_space=pltpu.HBM)] * n_any
    )
    return pl.pallas_call(
        body,
        out_shape=[jax.ShapeDtypeStruct(s, d) for s, d in outs],
        in_specs=specs,
        out_specs=[pl.BlockSpec(memory_space=pltpu.VMEM)] * len(outs),
        scratch_shapes=scratch,
        compiler_params=pltpu.CompilerParams(vmem_limit_bytes=limit),
        cost_estimate=pl.CostEstimate(flops=flops, bytes_accessed=4_000_000, transcendentals=0),
    )


def message_outs(rows, width, channels, keep):
    return [
        ((rows * width + TAIL, channels), BF16),
        ((keep * width + TAIL, channels), BF16),
        ((keep * width, channels), BF16),
        ((8, channels), F32),
    ]


def prepare(shape, flags, x, keep):
    rows, width, c = shape.rows, shape.cols, shape.narrow

    def body(flags, x_ref, out_ref, outer_ref, inner_ref, stats_ref):
        out_ref[0 : rows * width, :] = x_ref[...]
        sums = moments_of(x_ref[...].astype(F32))
        emit(flags, out_ref, outer_ref, inner_ref, stats_ref, keep, rows, width, sums)

    return call(body, 1, 1, 0, message_outs(rows, width, c, keep), [], 1000)(flags, x)


def fine_conv(shape, flags, weights, pieces, got, halo, out_halo, keep, residual=None):
    rows, width, half, c = shape.rows, shape.cols, shape.half, shape.narrow
    out_rows = rows + 2 * out_halo
    image_rows = out_rows + 2
    n_pieces = len(pieces)
    extra = 0 if residual is None else 3

    def body(flags, block, outer, inner, sa, sb, *rest):
        res = rest[:extra]
        piece_refs = rest[extra : extra + n_pieces]
        rest = rest[extra + n_pieces :]
        outs = rest[:-4]
        buffer, image, acc, sems = rest[-4:]
        copies = weights.copies(flags, piece_refs, buffer, sems)
        for mine in copies:
            for copy in mine:
                copy.start()
        weights.clear(image)
        mean, inv = group_terms(sa[...] + sb[...], shape.fine_count)
        mix = parity_matrix(c)

        def store(row, place, size, tap, value):
            weights.put(image, row, place, tap, value.astype(BF16))

        for row in range(image_rows):
            value, outside = ext_row(row + halo - out_halo - 1, block, outer, inner, flags, rows, halo, width)
            value = masked(silu((value - mean) * inv), outside).astype(BF16)
            value = jnp.dot(value, mix, preferred_element_type=F32)
            fine_columns(store, row, value[:half], value[half:])
        run_conv(weights, buffer, image, acc, sems, out_rows, width)
        scale = 1.0 / math.sqrt(9 * c)
        if residual is None:
            out_ref, outer_ref, inner_ref, stats_ref = outs
            value = (acc[...] * scale).astype(BF16)
            out_ref[0 : rows * width, :] = value
            emit(flags, out_ref, outer_ref, inner_ref, stats_ref, keep, rows, width, moments_of(value.astype(F32)))
        else:
            (out_ref,) = outs
            for row in range(out_rows):
                own, _ = ext_row(row, res[0], res[1], res[2], flags, rows, out_halo, width)
                span = slice(row * width, (row + 1) * width)
                out_ref[span, 0:c] = (own + acc[span, :] * scale).astype(BF16)
                out_ref[span, c:] = jnp.zeros((width, out_ref.shape[1] - c), BF16)

    outs = message_outs(rows, width, c, keep) if residual is None else [((out_rows * width, -(-c // 128) * 128), BF16)]
    args = (flags,) + tuple(got) + (() if residual is None else tuple(residual)) + tuple(pieces)
    flops = 2 * out_rows * width * 9 * c * c
    return call(body, 1, 5 + extra, n_pieces, outs, scratch_of(weights, image_rows, out_rows, width), flops)(*args)


def down_conv(shape, flags, weights, pieces, skip, keep):
    rows, width, half, c = shape.rows, shape.cols, shape.half, shape.narrow
    out_rows = rows // 2

    def body(flags, skip_ref, *rest):
        piece_refs = rest[: len(pieces)]
        outs = rest[len(pieces) : -4]
        buffer, image, acc, sems = rest[-4:]
        copies = weights.copies(flags, piece_refs, buffer, sems)
        for mine in copies:
            for copy in mine:
                copy.start()
        weights.clear(image)
        for row in range(rows + 1):
            value = skip_ref[row * width : (row + 1) * width, 0:c].astype(F32)
            if row == 0:
                value = masked(value, flags[1] != 0)
            even, odd = value[:half], value[half:]
            place = (row % 2) * (out_rows + 1) + row // 2
            weights.put(image, place, 0, 0, shifted(odd, 1).astype(BF16))
            weights.put(image, place, 0, 1, even.astype(BF16))
            weights.put(image, place, 0, 2, odd.astype(BF16))

        def begin(dy):
            return jnp.where(dy == 1, out_rows + 1, dy // 2)

        run_conv(weights, buffer, image, acc, sems, out_rows, half, begin)
        out_ref, outer_ref, inner_ref, stats_ref = outs
        value = (acc[...] * (1.0 / math.sqrt(9 * c))).astype(BF16)
        out_ref[0 : out_rows * half, :] = value
        emit(flags, out_ref, outer_ref, inner_ref, stats_ref, keep, out_rows, half, moments_of(value.astype(F32)))

    scratch = scratch_of(weights, 2 * (out_rows + 1), out_rows, half)
    outs = message_outs(out_rows, half, shape.wide, keep)
    return call(body, 1, 1, len(pieces), outs, scratch, 2 * out_rows * half * 9 * c * shape.wide)(flags, skip, *pieces)


def coarse_conv(shape, flags, weights, pieces, got, keep, residual=None):
    rows, width, c = shape.rows // 2, shape.half, shape.wide
    extra = 0 if residual is None else 1

    def body(flags, block, outer, inner, sa, sb, *rest):
        res = rest[:extra]
        piece_refs = rest[extra : extra + len(pieces)]
        outs = rest[extra + len(pieces) : -4]
        buffer, image, acc, sems = rest[-4:]
        copies = weights.copies(flags, piece_refs, buffer, sems)
        for mine in copies:
            for copy in mine:
                copy.start()
        weights.clear(image)
        mean, inv = group_terms(sa[...] + sb[...], shape.coarse_count)
        for row in range(rows + 2):
            value, outside = ext_row(row, block, outer, inner, flags, rows, 1, width)
            value = masked(silu((value - mean) * inv), outside)
            weights.put(image, row, 0, 0, shifted(value, 1).astype(BF16))
            weights.put(image, row, 0, 1, value.astype(BF16))
            weights.put(image, row, 0, 2, shifted(value, -1).astype(BF16))
        run_conv(weights, buffer, image, acc, sems, rows, width)
        out_ref, outer_ref, inner_ref, stats_ref = outs
        value = acc[...] * (1.0 / math.sqrt(9 * c))
        if residual is not None:
            value = res[0][0 : rows * width, :].astype(F32) + value
        value = value.astype(BF16)
        out_ref[0 : rows * width, :] = value
        emit(flags, out_ref, outer_ref, inner_ref, stats_ref, keep, rows, width, moments_of(value.astype(F32)))

    args = (flags,) + tuple(got) + (() if residual is None else (residual,)) + tuple(pieces)
    outs = message_outs(rows, width, c, keep)
    flops = 2 * rows * width * 9 * c * c
    return call(body, 1, 5 + extra, len(pieces), outs, scratch_of(weights, rows + 2, rows, width), flops)(*args)


def up_conv(shape, flags, weights, pieces, got, skip, keep):
    rows, width, half = shape.rows, shape.cols, shape.half
    c, c_out = shape.wide, shape.narrow

    def body(flags, block, outer, inner, skip_ref, *rest):
        piece_refs = rest[: len(pieces)]
        outs = rest[len(pieces) : -4]
        buffer, image, acc, sems = rest[-4:]
        copies = weights.copies(flags, piece_refs, buffer, sems)
        for mine in copies:
            for copy in mine:
                copy.start()
        weights.clear(image)
        mix = parity_matrix(c)
        for row in range(rows // 2 + 2):
            value, outside = ext_row(row, block, outer, inner, flags, rows // 2, 1, half)
            value = masked(value, outside).astype(BF16)
            value = jnp.dot(value, mix, preferred_element_type=F32)
            before, after = shifted(value, 1).astype(BF16), shifted(value, -1).astype(BF16)
            value = value.astype(BF16)
            for fine in (2 * row - 1, 2 * row):
                if 0 <= fine < rows + 2:
                    for tap, (even, odd) in enumerate(((before, value), (value, value), (value, after))):
                        weights.put(image, fine, 0, tap, even)
                        weights.put(image, fine, half, tap, odd)
        run_conv(weights, buffer, image, acc, sems, rows, width)
        out_ref, outer_ref, inner_ref, stats_ref = outs
        value = (acc[...] * (1.0 / math.sqrt(9 * c))).astype(BF16)
        out_ref[0 : rows * width, :] = value
        own = skip_ref[width : (rows + 1) * width, 0:c_out].astype(F32)
        sums = moments_of(value.astype(F32)) + moments_of(own)
        emit(flags, out_ref, outer_ref, inner_ref, stats_ref, keep, rows, width, sums)

    outs = message_outs(rows, width, c_out, keep)
    flops = 2 * rows * width * 9 * c * c_out
    scratch = scratch_of(weights, rows + 2, rows, width)
    return call(body, 1, 4, len(pieces), outs, scratch, flops)(flags, *got, skip, *pieces)


def join_conv(shape, flags, weights, pieces, got, skip, keep):
    rows, width, half, c = shape.rows, shape.cols, shape.half, shape.narrow

    def body(flags, block, outer, inner, sa, sb, skip_ref, *rest):
        piece_refs = rest[: len(pieces)]
        outs = rest[len(pieces) : -4]
        buffer, image, acc, sems = rest[-4:]
        copies = weights.copies(flags, piece_refs, buffer, sems)
        for mine in copies:
            for copy in mine:
                copy.start()
        weights.clear(image)
        mix = parity_matrix(c)
        for part in range(2):
            sums = sa[...] + sb[...]
            mean, inv = pair_terms(sums[2 * part : 2 * part + 2], shape.fine_count)

            def store(row, place, size, tap, value, part=part):
                weights.put(image, row, place, tap, value.astype(BF16), first=part * c)

            for row in range(rows + 2):
                if part == 0:
                    value, outside = ext_row(row, block, outer, inner, flags, rows, 1, width)
                else:
                    value = skip_ref[row * width : (row + 1) * width, 0:c].astype(F32)
                    outside = flags[1] != 0 if row == 0 else flags[2] != 0 if row == rows + 1 else None
                value = masked(silu((value - mean) * inv), outside).astype(BF16)
                value = jnp.dot(value, mix, preferred_element_type=F32)
                fine_columns(store, row, value[:half], value[half:])
        run_conv(weights, buffer, image, acc, sems, rows, width)
        out_ref, outer_ref, inner_ref, stats_ref = outs
        value = (acc[...] * (1.0 / math.sqrt(18 * c))).astype(BF16)
        out_ref[0 : rows * width, :] = value
        emit(flags, out_ref, outer_ref, inner_ref, stats_ref, keep, rows, width, moments_of(value.astype(F32)))

    outs = message_outs(rows, width, c, keep)
    flops = 2 * rows * width * 18 * c * c
    scratch = scratch_of(weights, rows + 2, rows, width)
    return call(body, 1, 6, len(pieces), outs, scratch, flops)(flags, *got, skip, *pieces)


def pair_terms(sums, count):
    width = sums.shape[1]
    size = 2 * width // GROUPS
    terms = row_stack(bf16_terms(sums[0:1]) + bf16_terms(sums[1:2]), 16, width).astype(BF16)
    left = lax.broadcasted_iota(jnp.int32, (width, width), 0) // size
    right = lax.broadcasted_iota(jnp.int32, (width, width), 1) // size
    together = jnp.where(left == right, 1.0, 0.0).astype(BF16)
    summed = jnp.dot(terms, together, preferred_element_type=F32) * (1.0 / (count * size))
    mean = summed[0:1] + summed[1:2] + summed[2:3]
    square = summed[3:4] + summed[4:5] + summed[5:6]
    variance = jnp.maximum(square - mean * mean, 0.0)
    return mean, lax.rsqrt(variance + EPSILON)


def last_conv(shape, flags, weights, pieces, got, u, skip, j_start, n_quarters):
    rows, width, half, c = shape.rows, shape.cols, shape.half, shape.narrow
    quarter = half // n_quarters
    j_block = j_start // shape.blk

    def body(flags, block, outer, inner, sa, sb, u_ref, skip_ref, *rest):
        piece_refs = rest[: len(pieces)]
        outs = rest[len(pieces) : -6]
        buffer, image, acc, sems, jbuf, jsem = rest[-6:]
        copies = weights.copies(flags, piece_refs, buffer, sems)
        for mine in copies:
            for copy in mine:
                copy.start()
        weights.clear(image)
        for ref, (owner, low, high) in zip(piece_refs, weights.entries, strict=True):
            if low <= j_block < high:
                pltpu.make_async_copy(
                    ref.at[:, (j_block - low) * shape.lanes : (j_block - low + 1) * shape.lanes],
                    jbuf.at[owner(flags)],
                    jsem,
                ).start()
        mean, inv = group_terms(sa[...] + sb[...], shape.fine_count)
        mix = parity_matrix(c)

        def store(row, place, size, tap, value):
            weights.put(image, row, place, tap, value.astype(BF16))

        for row in range(rows + 2):
            value, outside = ext_row(row, block, outer, inner, flags, rows, 1, width)
            value = masked(silu((value - mean) * inv), outside).astype(BF16)
            value = jnp.dot(value, mix, preferred_element_type=F32)
            fine_columns(store, row, value[:half], value[half:])
        run_conv(weights, buffer, image, acc, sems, rows, width)
        pltpu.make_async_copy(jbuf, jbuf, jsem).wait()
        right = jbuf[...].reshape(2 * c, shape.lanes)
        left = [u_ref[0 : rows * width, :], skip_ref[width : (rows + 1) * width, 0:c]]
        left = [jnp.dot(part, mix, preferred_element_type=F32).astype(BF16) for part in left]
        made = jnp.zeros((rows * width, c), F32)
        for odd in range(2):
            mine = jnp.concatenate(
                [part[:, odd * (c // 2) : (odd + 1) * (c // 2)] for part in left]
                + [jnp.zeros((rows * width, shape.lanes - c), BF16)],
                axis=1,
            )
            made += lax.dot_general(
                mine, right[odd * c : (odd + 1) * c], (((1,), (1,)), ((), ())), preferred_element_type=F32
            )
        value = made * (1.0 / math.sqrt(2 * c)) + acc[...] * (1.0 / math.sqrt(9 * c))
        value = value.reshape(2 * rows, half, c).astype(BF16)
        for q, out in enumerate(outs):
            out[...] = value[:, q * quarter : (q + 1) * quarter, :]

    outs = [((2 * rows, quarter, c), BF16)] * n_quarters
    flops = 2 * rows * width * 11 * c * c
    extra = [pltpu.VMEM((shape.m, shape.cols_of, shape.lanes), BF16), pltpu.SemaphoreType.DMA(())]
    scratch = scratch_of(weights, rows + 2, rows, width, extra)
    return call(body, 1, 7, len(pieces), outs, scratch, flops)(flags, *got, u, skip, *pieces)


def pack_blocks(shape, pack, bounds):
    columns = pack.shape[0]
    first = bounds[0][0] * shape.blk // 128 * 128
    last = min(-(-bounds[-1][1] * shape.blk // 128) * 128, pack.shape[1])

    def body(pack_ref, *rest):
        outs, (rows, sem) = rest[:-2], rest[-2:]
        copy = pltpu.make_async_copy(pack_ref.at[:, first:last], rows, sem)
        copy.start()
        copy.wait()
        for (low, high), out_ref in zip(bounds, outs, strict=True):
            for block in range(high - low):
                begin, end = block * shape.lanes, (block + 1) * shape.lanes
                at = (low + block) * shape.blk - first
                out_ref[:, begin : begin + shape.blk] = rows[:, at : at + shape.blk]
                out_ref[:, begin + shape.blk : end] = jnp.zeros((columns, shape.lanes - shape.blk), BF16)

    scratch = [pltpu.VMEM((columns, last - first), BF16), pltpu.SemaphoreType.DMA(())]
    outs = [((columns, (high - low) * shape.lanes), BF16) for low, high in bounds]
    return call(body, 0, 0, 1, outs, scratch, 1000)(pack)


def shards(n, n_section, features, section_packs):
    section_id = lax.axis_index("section")
    w = lax.axis_index("space")
    shape = Shape(features, n)
    q_rows = shape.narrow * shape.narrow // shape.wide
    pack = section_packs[0]
    flags = jnp.stack([w % 2, (w == 0).astype(jnp.int32), (w == n - 1).astype(jnp.int32), section_id, w]).astype(jnp.int32)

    total = pack.shape[0] // shape.blk
    cuts = [0, 9 * q_rows // shape.blk, 18 * q_rows // shape.blk, 36 * q_rows // shape.blk, total]
    bounds = list(zip(cuts[:-1], cuts[1:], strict=True))

    def permute(value, source, target, move):
        if source == target:
            return within(value, move)
        pairs = [
            (s * n + i, (s + target - source) % n_section * n + move(i)) for s in range(n_section) for i in range(n)
        ]
        return lax.ppermute(value, ("section", "space"), pairs)

    def within(value, move):
        pairs = [(s * n + i, s * n + move(i)) for s in range(n_section) for i in range(n)]
        return lax.ppermute(value, ("section", "space"), pairs)

    def to_outer(i):
        return (i + 1) % n if i % 2 else (i - 1) % n

    def ahead(i):
        return (i - 2) % n if i % 2 else (i + 2) % n

    def across(i):
        return (i + 4) % n

    def partner(i):
        return i ^ 1

    def sums_of(tail, count):
        tail = tail.astype(F32)
        rows = [tail[i : i + 1] + tail[i + 1 : i + 2] + tail[i + 2 : i + 3] for i in range(0, 3 * count, 3)]
        return jnp.concatenate(rows + [jnp.zeros((8 - count, tail.shape[1]), F32)], 0)

    def exchange(made, source, target, with_stats=True, count=2):
        block, outer, inner, own = made
        if source != target:
            block = permute(block, source, target, lambda i: i)
            rows, size = block.shape[0] - TAIL, inner.shape[0]
            top, bottom, tail = block[:size], block[rows - size : rows], block[rows:]
            outer = jnp.concatenate([jnp.where(flags[0] == 0, top, bottom), tail], 0)
            inner = jnp.where(flags[0] == 0, bottom, top)
            own = sums_of(tail, count)
        stats = own
        outer = permute(outer, target, target, to_outer)
        inner = permute(inner, target, target, partner)
        if not with_stats:
            return block, outer, inner
        if n == 8:
            b = permute(stats, target, target, ahead)
            c = permute(stats, target, target, across)
            mine = own + sums_of(outer[-TAIL:], count) + b + c
            other = permute(mine, target, target, partner)
        else:
            mine = lax.psum(own, "space")
            other = jnp.zeros_like(mine)
        return block, outer, inner, mine, other

    def after(value, *deps):
        return lax.optimization_barrier((value,) + deps)[0]

    pieces = {}
    packed = []
    if n == 8:
        packed = pack_blocks(shape, pack.T, bounds[:1])

    def send(number, *deps):
        low, high = bounds[number]
        if n == 8:
            got = [after(packed[number], *deps)]
            for k in range(1, 3 if number in RELAYED else 4):
                got.append(within(got[0], lambda i, k=k: i ^ (2 * k)))
            return got
        got = lax.all_gather(pack[low * shape.blk : high * shape.blk], "space")
        got = got.reshape(shape.m, n // shape.m, high - low, shape.blk, -1).transpose(0, 1, 4, 2, 3)
        got = got.reshape(shape.m, shape.cols_of, high - low, shape.blk)
        got = jnp.pad(got, ((0, 0), (0, 0), (0, 0), (0, shape.lanes - shape.blk)))
        return list(got.reshape(shape.m, shape.cols_of, -1))

    def relay(got, *deps):
        if n != 8:
            return []
        half = got[1].shape[1] // 2
        first, second = after((got[1][:, :half], got[2][:, half:]), *deps)
        made = []
        for k, part in ((2, first), (1, second)):
            made.append(within(part, lambda i, k=k: i ^ (2 * k)))
        return made

    def share(number, got, first=0):
        low, high = bounds[number]
        middle = (low + high) // 2
        spans = [(low, high)] * len(got) if n != 8 or first == 0 else [(low, middle), (middle, high)]
        mine = pieces.setdefault(number, [])
        for place, (part, span) in enumerate(zip(got, spans, strict=True)):
            if n == 8:
                j = min(first + place, 3)
                mine.append((part, lambda flags, j=j: ((flags[4] // 2) ^ j) * 2 + flags[0]) + span)
                theirs = within(part, partner)
                mine.append((theirs, lambda flags, j=j: ((flags[4] // 2) ^ j) * 2 + 1 - flags[0]) + span)
            else:
                mine.append((part, lambda flags, j=place: j) + span)

    def weights(start, c_in, c_out, extra=0):
        first = start // shape.blk
        end = (start + 9 * c_in * c_out // shape.wide) // shape.blk
        used = [e for number in sorted(pieces) for e in pieces[number] if e[2] < end + extra and e[3] > first]
        return Weights(shape, [e[1:] for e in used], start, c_in, c_out), [e[0] for e in used]

    narrow, wide = shape.narrow, shape.wide
    x = features[0].reshape(shape.rows, shape.half, 2, narrow).transpose(0, 2, 1, 3).reshape(-1, narrow)
    sent = send(0)
    ready = prepare(shape, flags, after(x, sent[0]), 1)
    if n == 8:
        packed += pack_blocks(shape, after(pack.T, sent[0]), bounds[1:])
    third = send(1)
    fourth = send(2)
    first = exchange(ready, 0, 0)
    share(0, after(sent, first[3]))
    first = (after(first[0], third[0], fourth[0]),) + first[1:]
    hidden = fine_conv(shape, flags, *weights(0, narrow, narrow), first, 1, 0, 2)
    second = exchange(hidden, 0, 0)
    fourth = after(fourth, second[3])
    opposite = relay(fourth)
    sent = send(3, second[3])
    share(1, after(third, second[3]))
    share(2, fourth)
    second = (after(second[0], sent[0]),) + second[1:]
    (skip,) = fine_conv(shape, flags, *weights(9 * q_rows, narrow, narrow), second, 2, 1, 0, residual=first[:3])
    share(2, after(opposite, skip), 3)
    coarse = down_conv(shape, flags, *weights(18 * q_rows, narrow, wide), skip, 1)
    for section in (1, 2):
        got = exchange(coarse, section - 1, section)
        if section == 1:
            opposite = relay(sent, got[3])
            skip, got = lax.optimization_barrier((skip, got))
            skip = permute(skip, 0, n_section - 1, lambda i: i)
        else:
            skip, got = lax.optimization_barrier((skip, got))
        hidden = coarse_conv(shape, flags, *weights(0, wide, wide), got, 1)
        if section == 1:
            share(3, after(sent, hidden[3]))
        then = exchange(hidden, section, section)
        if section == 1:
            share(3, after(opposite, then[3]), 3)
        coarse = coarse_conv(shape, flags, *weights(36 * q_rows, wide, wide), then, 1, residual=got[0])
    got = exchange(coarse, 2, 3, with_stats=False)
    up = up_conv(shape, flags, *weights(0, wide, narrow), got, skip, 1)
    got = exchange(up, 3, 3, count=4)
    hidden = join_conv(shape, flags, *weights(18 * q_rows, wide, narrow), got, skip, 1)
    then = exchange(hidden, 3, 3)
    outs = last_conv(
        shape, flags, *weights(36 * q_rows, narrow, narrow, 1), then, got[0], skip, 45 * q_rows, n_section
    )
    result = outs[3]
    for target in range(3):
        pairs = [(3 * n + i, target * n + i) for i in range(n)]
        result = jnp.where(section_id == target, lax.ppermute(outs[target], ("section", "space"), pairs), result)
    quarter = shape.half // n_section
    result = result.reshape(shape.rows, 2, quarter, narrow).transpose(0, 2, 1, 3)
    return result.reshape(1, shape.rows, 2 * quarter, narrow)


def solution(mesh):
    n, n_section = mesh.shape["space"], mesh.shape["section"]

    def body(features, section_packs):
        return shards(n, n_section, features, section_packs)

    return jax.shard_map(
        body,
        mesh=mesh,
        in_specs=(P(None, "space", None, None), P("section", None, "space")),
        out_specs=P(None, "space", "section", None),
        check_vma=False,
    )
```
